32 devices in a mesh: dp: 8 (over z, x), tensor: 4 (over y, core).
Axes of the slice: x: 2, y: 2, z: 4, core: 2. Of those that a mesh axis runs over, the one named last changes fastest.
Arguments:
- layer_in: bfloat16 [32768, 768], P(('dp', 'tensor')), may hold values from -6 to 6
- query_weight: bfloat16 [768, 768], P('dp', 'tensor'), may hold values from -0.3125 to 0.3125
- key_weight: bfloat16 [768, 768], P('dp', 'tensor'), may hold values from -0.3125 to 0.3125
- value_weight: bfloat16 [768, 768], P('dp', 'tensor'), may hold values from -0.21875 to 0.21875
- output_weight: bfloat16 [768, 768], P('tensor', 'dp'), may hold values from -0.875 to 0.875
- inner_weight: bfloat16 [768, 3072], P('dp', 'tensor'), may hold values from -0.21875 to 0.21875
- outer_weight: bfloat16 [3072, 768], P('tensor', 'dp'), may hold values from -0.15625 to 0.15625
- query_bias: float32 [768], P(('dp', 'tensor')), may hold values from -3 to 3
- value_bias: float32 [768], P(('dp', 'tensor')), may hold values from -3 to 3
- output_bias: float32 [768], P(('dp', 'tensor')), may hold values from -3 to 3
- inner_bias: float32 [3072], P(('dp', 'tensor')), may hold values from -3 to 3
- outer_bias: float32 [768], P(('dp', 'tensor')), may hold values from -3 to 3
- first_gain: float32 [768], P(('dp', 'tensor')), may hold values from 0.5 to 1.5
- first_shift: float32 [768], P(('dp', 'tensor')), may hold values from -2 to 2
- second_gain: float32 [768], P(('dp', 'tensor')), may hold values from 0.5 to 1.5
- second_shift: float32 [768], P(('dp', 'tensor')), may hold values from -2 to 2
- segment_ids: int32 [32768], P('dp'), may hold values from 0 to 7, as said below
- pad_mask: int32 [32768], P('dp'), may hold values from 0 to 1, as said below
- random_blocks: int32 [16, 32, 3], P('dp'), may hold values from 0 to 31
- global_blocks: int32 [16, 8, 2], P('dp'), may hold values from 0 to 31, as said below
- output_grad: bfloat16 [32768, 768], P(('dp', 'tensor')), may hold values from -6 to 6
Outputs:
- layer_out: bfloat16 [32768, 768], P(('dp', 'tensor'))
- input_grad: float32 [32768, 768], P(('dp', 'tensor'))
- query_weight_grad: float32 [768, 768], P('dp', 'tensor')
- key_weight_grad: float32 [768, 768], P('dp', 'tensor')
- value_weight_grad: float32 [768, 768], P('dp', 'tensor')
- output_weight_grad: float32 [768, 768], P('tensor', 'dp')
- inner_weight_grad: float32 [768, 3072], P('dp', 'tensor')
- outer_weight_grad: float32 [3072, 768], P('tensor', 'dp')
- query_bias_grad: float32 [768], P(('dp', 'tensor'))
- value_bias_grad: float32 [768], P(('dp', 'tensor'))
- output_bias_grad: float32 [768], P(('dp', 'tensor'))
- inner_bias_grad: float32 [3072], P(('dp', 'tensor'))
- outer_bias_grad: float32 [768], P(('dp', 'tensor'))
- first_gain_grad: float32 [768], P(('dp', 'tensor'))
- first_shift_grad: float32 [768], P(('dp', 'tensor'))
- second_gain_grad: float32 [768], P(('dp', 'tensor'))
- second_shift_grad: float32 [768], P(('dp', 'tensor'))
The draws below stay inside these ranges and needn't reach their ends.
Inputs may be any that keep to these rules, and one draw needn't show every extreme that they name: `segment_ids`: within each sequence of 2048 tokens the numbers start at 0, never fall and rise by one at each new document; every sequence holds 8 documents; every document but the last of a sequence has 192 tokens or more; padding tokens carry the number of the sequence's last document. `pad_mask`: the padding of a sequence is its last 0 to 127 tokens. `global_blocks`: row s of a sequence holds two block indices for document number s: the first is the block of the document's first token, the second lies one or two blocks after it, or is the last block; the two may be equal.
All inputs are finite; a program needn't handle non-finite values.
Results may differ from the reference program's by a relative error of at most 0.02.
Values may be sent and summed in bfloat16 or wider, within the bound.
A program may use at most 320 MiB of HBM per device.

```python
import jax
import jax.numpy as jnp
from jax import lax

D = 768
H = 12
HD = 64
FF = 3072
BLK = 64
LEN = 2048
SEQS = 2
SEGS = 8
NB = 32
NSEQ = 16
TOKENS = 32768


def packing_layout(key):
    base = jax.random.fold_in(key, 11)
    seq_keys = jax.random.split(base, NSEQ)

    def one_sequence(seq_key):
        cut_key, pad_key, step_key = jax.random.split(seq_key, 3)
        pad_count = jax.random.randint(pad_key, (), 0, 2 * BLK)
        real_count = LEN - pad_count
        spare = real_count - SEGS * 3 * BLK
        cuts = jnp.sort(jax.random.randint(cut_key, (SEGS - 1,), 0, spare + 1)).astype(jnp.int32)
        bounds = jnp.concatenate([jnp.zeros((1,), jnp.int32), cuts, jnp.reshape(spare, (1,)).astype(jnp.int32)])
        doc_lengths = 3 * BLK + (bounds[1:] - bounds[:-1])
        ends = jnp.cumsum(doc_lengths).astype(jnp.int32)
        positions = jnp.arange(LEN, dtype=jnp.int32)
        capped = jnp.minimum(positions, real_count - 1)
        segments = jnp.sum((ends[None, :] <= capped[:, None]).astype(jnp.int32), axis=1)
        segments = jnp.minimum(segments, SEGS - 1)
        padding = (positions < real_count).astype(jnp.int32)
        starts = jnp.concatenate([jnp.zeros((1,), jnp.int32), ends[:-1]])
        first_block = jnp.minimum(starts // BLK, NB - 1)
        steps_ahead = jax.random.randint(step_key, (SEGS,), 1, 3)
        second_block = jnp.minimum(first_block + steps_ahead, NB - 1)
        return (segments, padding, jnp.stack([first_block, second_block], axis=1))
    return jax.vmap(one_sequence)(seq_keys)


def draw_segment_ids(key, part):
    return packing_layout(key)[0].reshape(TOKENS).astype(jnp.int32)


def draw_pad_mask(key, part):
    return packing_layout(key)[1].reshape(TOKENS).astype(jnp.int32)


def draw_global_blocks(key, part):
    return packing_layout(key)[2].astype(jnp.int32)


def set_ends(entries, own_key, least, high):
    longest = entries.shape.index(max(entries.shape))
    spots = []
    for shift in (0, 1):
        where = [jax.random.randint(jax.random.fold_in(own_key, axis), (), 0, length) for axis, length in enumerate(entries.shape)]
        where[longest] = (where[longest] + shift) % entries.shape[longest]
        spots.append(tuple(where))
    return entries.at[spots[0]].set(least).at[spots[1]].set(high)


def shard_levels(own_key, dims, cuts, smallest, high):
    def one(dim, shards_of):
        steps = jax.random.uniform(jax.random.fold_in(jax.random.fold_in(own_key, 6), dim), (shards_of,), jnp.float32, smallest / len(cuts), high / len(cuts))
        return jnp.repeat(jnp.exp(steps), dims[dim] // shards_of).reshape((-1,) + (1,) * (len(dims) - dim - 1))

    level = one(*cuts[0])
    for cut in cuts[1:]:
        level = level * one(*cut)
    return level


def scatter_about(rng, dims, spread, reach, cuts=(), kind=jnp.bfloat16):
    factor_of = shard_levels(rng, dims, cuts, -0.22, 0.18) if cuts else 1.0
    values = jax.random.normal(rng, dims, jnp.float32) * spread * factor_of
    return jnp.minimum(jnp.maximum(values, -reach), reach).astype(kind)


def setup_inputs(seed: int = 0) -> dict:
    splits = jax.random.split(jax.random.key(seed), 22)
    layer_in = scatter_about(splits[0], (TOKENS, D), 1.0, 6.0, ((0, 32),))
    query_weight = scatter_about(splits[1], (D, D), (D // 2) ** -0.5, 0.3125, ((0, 8), (1, 4)))
    key_weight = scatter_about(splits[2], (D, D), (D // 2) ** -0.5, 0.3125, ((0, 8), (1, 4)))
    value_weight = scatter_about(splits[3], (D, D), D ** -0.5, 0.21875, ((0, 8), (1, 4)))
    output_weight = scatter_about(splits[4], (D, D), (D // 16) ** -0.5, 0.875, ((0, 4), (1, 8)))
    inner_weight = scatter_about(splits[5], (D, FF), D ** -0.5, 0.21875, ((0, 8), (1, 4)))
    outer_weight = scatter_about(splits[6], (FF, D), (FF // 2) ** -0.5, 0.15625, ((0, 4), (1, 8)))
    query_bias = scatter_about(splits[7], (D,), 0.5, 3.0, ((0, 32),), jnp.float32)
    value_bias = scatter_about(splits[8], (D,), 0.5, 3.0, ((0, 32),), jnp.float32)
    output_bias = scatter_about(splits[9], (D,), 0.5, 3.0, ((0, 32),), jnp.float32)
    inner_bias = scatter_about(splits[10], (FF,), 0.5, 3.0, ((0, 32),), jnp.float32)
    outer_bias = scatter_about(splits[11], (D,), 0.5, 3.0, ((0, 32),), jnp.float32)
    first_gain = jnp.clip(1.0 + 0.1 * jax.random.normal(splits[12], (D,), jnp.float32), 0.5, 1.5)
    first_shift = scatter_about(splits[13], (D,), 0.3, 2.0, ((0, 32),), jnp.float32)
    second_gain = jnp.clip(1.0 + 0.1 * jax.random.normal(splits[14], (D,), jnp.float32), 0.5, 1.5)
    second_shift = scatter_about(splits[15], (D,), 0.3, 2.0, ((0, 32),), jnp.float32)
    segment_ids = draw_segment_ids(jax.random.fold_in(splits[21], 71), 0)
    pad_mask = draw_pad_mask(jax.random.fold_in(splits[21], 71), 0)
    random_blocks = set_ends(jax.random.randint(splits[18], (NSEQ, NB, 3), 0, NB), jax.random.fold_in(splits[18], 1), 0, NB - 1).astype(jnp.int32)
    global_blocks = draw_global_blocks(jax.random.fold_in(splits[21], 71), 0)
    output_grad = scatter_about(splits[20], (TOKENS, D), 1.0, 6.0, ((0, 32),))
    return {"layer_in": layer_in, "query_weight": query_weight, "key_weight": key_weight, "value_weight": value_weight, "output_weight": output_weight, "inner_weight": inner_weight, "outer_weight": outer_weight, "query_bias": query_bias, "value_bias": value_bias, "output_bias": output_bias, "inner_bias": inner_bias, "outer_bias": outer_bias, "first_gain": first_gain, "first_shift": first_shift, "second_gain": second_gain, "second_shift": second_shift, "segment_ids": segment_ids, "pad_mask": pad_mask, "random_blocks": random_blocks, "global_blocks": global_blocks, "output_grad": output_grad}


@jax.custom_vjp
def low(v):
    return lax.optimization_barrier(v.astype(jnp.bfloat16)).astype(jnp.float32)

@jax.custom_vjp
def low_back(v):
    return v

def low_keep(v):
    return (low(v), None)

def low_pass(kept, grad):
    return (grad,)

def back_keep(v):
    return (v, None)

def back_low(kept, grad):
    return (low(grad),)
low.defvjp(low_keep, low_pass)
low_back.defvjp(back_keep, back_low)
EPSILON = 1e-06
HIGHEST = lax.Precision.HIGHEST

def allowed_mask(segments, padding, randoms, global_row):
    positions = jnp.arange(LEN, dtype=jnp.int32)
    blocks = positions // BLK
    in_window = jnp.abs(blocks[None, :] - blocks[:, None]) <= 1
    in_random = jnp.any(randoms[blocks][:, :, None] == blocks[None, None, :], axis=1)
    in_global = jnp.any(global_row[segments][:, :, None] == blocks[None, None, :], axis=1)
    same_doc = segments[:, None] == segments[None, :]
    key_live = (padding[None, :] == 1) | (positions[:, None] == positions[None, :])
    return same_doc & key_live & (in_window | in_random | in_global)

def layer_norm(resid, gain, shift):
    center = resid - lax.optimization_barrier(jnp.mean(resid, axis=-1, keepdims=True))
    return center * lax.rsqrt(lax.optimization_barrier(jnp.mean(center * center, axis=-1, keepdims=True)) + EPSILON) * gain + shift

def attend(item):
    queries, keys, values, allowed = item
    query_heads = queries.reshape(LEN, H, HD)
    key_heads = keys.reshape(LEN, H, HD)
    value_heads = values.reshape(LEN, H, HD)
    scores = low_back(jnp.einsum('qhd,khd->hqk', query_heads, key_heads, precision=HIGHEST) * HD ** (-0.5))
    probs = low(jax.nn.softmax(jnp.where(allowed[None], scores, -1e+30), axis=-1))
    mixed = jnp.einsum('hqk,khd->qhd', probs, value_heads, precision=HIGHEST)
    return mixed.reshape(LEN, H * HD)

def forward(layer_in, params, masks):
    query_weight, key_weight, value_weight, output_weight, inner_weight, outer_weight, query_bias, value_bias, output_bias, inner_bias, outer_bias, first_gain, first_shift, second_gain, second_shift = params
    rows = layer_in.shape[0]
    queries = low(low_back(jnp.dot(layer_in, query_weight, precision=HIGHEST) + query_bias))
    keys = low(low_back(jnp.dot(layer_in, key_weight, precision=HIGHEST)))
    values = low(low_back(jnp.dot(layer_in, value_weight, precision=HIGHEST) + value_bias))
    shaped = (queries.reshape(SEQS, LEN, D), keys.reshape(SEQS, LEN, D), values.reshape(SEQS, LEN, D), masks)
    attn = low(low_back(lax.map(jax.checkpoint(attend), shaped).reshape(rows, D)))
    first_resid = layer_in + low_back(jnp.dot(attn, output_weight, precision=HIGHEST)) + output_bias
    first_norm = layer_norm(first_resid, first_gain, first_shift)
    inner = low_back(jnp.dot(low(first_norm), inner_weight, precision=HIGHEST) + inner_bias)
    hidden = low(jax.nn.gelu(inner, approximate=False))
    second_resid = first_norm + low_back(jnp.dot(hidden, outer_weight, precision=HIGHEST)) + outer_bias
    return layer_norm(second_resid, second_gain, second_shift)

def reference(layer_in, query_weight, key_weight, value_weight, output_weight, inner_weight, outer_weight, query_bias, value_bias, output_bias, inner_bias, outer_bias, first_gain, first_shift, second_gain, second_shift, segment_ids, pad_mask, random_blocks, global_blocks, output_grad):
    params = tuple((item.astype(jnp.float32) for item in (query_weight, key_weight, value_weight, output_weight, inner_weight, outer_weight, query_bias, value_bias, output_bias, inner_bias, outer_bias, first_gain, first_shift, second_gain, second_shift)))
    groups = NSEQ // SEQS
    group_rows = SEQS * LEN
    inputs = layer_in.astype(jnp.float32).reshape(groups, group_rows, D)
    cotangents = output_grad.astype(jnp.float32).reshape(groups, group_rows, D)
    segments = segment_ids.reshape(groups, SEQS, LEN)
    paddings = pad_mask.reshape(groups, SEQS, LEN)
    randoms = random_blocks.reshape(groups, SEQS, NB, 3)
    globs = global_blocks.reshape(groups, SEQS, SEGS, 2)

    def one_group(totals, item):
        group_in, group_grad, group_seg, group_pad, group_rand, group_glob = item
        masks = jax.vmap(allowed_mask)(group_seg, group_pad, group_rand, group_glob)
        result, pull = jax.vjp(lambda rows_in, weights: forward(rows_in, weights, masks), group_in, params)
        grad_in, grad_params = pull(group_grad)
        totals = tuple((total + part for total, part in zip(totals, grad_params)))
        return (totals, (result, grad_in))
    zeros = tuple((jnp.zeros_like(item) for item in params))
    grads, (results, grad_inputs) = lax.scan(one_group, zeros, (inputs, cotangents, segments, paddings, randoms, globs))
    return (results.reshape(TOKENS, D).astype(jnp.bfloat16), grad_inputs.reshape(TOKENS, D), grads[0], grads[1], grads[2], grads[3], grads[4], grads[5], grads[6], grads[7], grads[8], grads[9], grads[10], grads[11], grads[12], grads[13], grads[14])
```

```python
from functools import partial

import jax
import jax.numpy as jnp
from jax import lax
from jax.experimental import pallas as pl
from jax.experimental.pallas import tpu as pltpu
from jax.sharding import PartitionSpec as P

HD = 64
PAIR = 2 * HD
QT = 256
KT = 128
EPSILON = 1e-06
NEGATIVE = -1e30
MESH = pl.DeviceIdType.MESH
VMEM_LIMIT = 56 * 2**20
BF = jnp.bfloat16
F32 = jnp.float32


def params_of(collective_id=None):
    if collective_id is None:
        return pltpu.CompilerParams(vmem_limit_bytes=VMEM_LIMIT)
    return pltpu.CompilerParams(
        vmem_limit_bytes=VMEM_LIMIT, collective_id=collective_id, has_side_effects=True
    )


def nt(left, right, **more):
    return lax.dot_general(
        left, right, (((1,), (1,)), ((), ())), preferred_element_type=F32, **more
    )


def nn(left, right):
    return lax.dot_general(left, right, (((1,), (0,)), ((), ())), preferred_element_type=F32)


def tn(left, right):
    return lax.dot_general(left, right, (((0,), (0,)), ((), ())), preferred_element_type=F32)


def sibling_of():
    rank = lax.axis_index("tensor")
    half = lax.rem(rank, 2)
    return half, {"tensor": rank + 1 - 2 * half}


def meet(sibling):
    barrier = pltpu.get_barrier_semaphore()
    pl.semaphore_signal(barrier, inc=1, device_id=sibling, device_id_type=MESH)
    pl.semaphore_wait(barrier, 1)


def gather_pair_kernel(first, qkv_ref, both_ref, local_sem, send_sem, recv_sem):
    half, sibling = sibling_of()
    meet(sibling)
    own = qkv_ref.at[:, first:]
    away = pltpu.make_async_remote_copy(
        own, both_ref.at[half], send_sem, recv_sem, device_id=sibling, device_id_type=MESH
    )
    away.start()
    here = pltpu.make_async_copy(own, both_ref.at[half], local_sem)
    here.start()
    here.wait()
    away.wait()


def gather_pair(qkv, first):
    rows, width = qkv.shape[0], qkv.shape[1] - first
    return pl.pallas_call(
        partial(gather_pair_kernel, first),
        name="gather_pair",
        out_shape=jax.ShapeDtypeStruct((2, rows, width), qkv.dtype),
        in_specs=[pl.BlockSpec(memory_space=pl.ANY)],
        out_specs=pl.BlockSpec(memory_space=pl.ANY),
        scratch_shapes=[pltpu.SemaphoreType.DMA(())] * 3,
        compiler_params=params_of(1),
    )(qkv)


def swap_pair_kernel(both_ref, other_ref, send_sem, recv_sem):
    half, sibling = sibling_of()
    meet(sibling)
    away = pltpu.make_async_remote_copy(
        both_ref.at[1 - half], other_ref, send_sem, recv_sem,
        device_id=sibling, device_id_type=MESH,
    )
    away.start()
    away.wait()


def swap_pair(both):
    return pl.pallas_call(
        swap_pair_kernel,
        name="swap_pair",
        out_shape=jax.ShapeDtypeStruct(both.shape[1:], both.dtype),
        in_specs=[pl.BlockSpec(memory_space=pl.ANY)],
        out_specs=pl.BlockSpec(memory_space=pl.ANY),
        scratch_shapes=[pltpu.SemaphoreType.DMA(())] * 2,
        compiler_params=params_of(2),
    )(both)


def masked_pairs(source, target, pairs, scale):
    rows = source.shape[0]
    low_lanes = lax.broadcasted_iota(jnp.int32, (rows, PAIR), 1) < HD
    for p in range(pairs):
        both = source[:, p * PAIR : (p + 1) * PAIR]
        if scale is not None:
            both = both * jnp.asarray(scale, both.dtype)
        zero = jnp.zeros_like(both)
        target[p, :rows, :] = jnp.where(low_lanes, both, zero)
        target[p, rows:, :] = jnp.where(low_lanes, zero, both)


def tile_bias(j, q_first, row_info, key_info, bias):
    seg_q, bits_q = row_info[0:1, :], row_info[1:2, :]
    queries = bias.shape[1]
    for part in range(KT // HD):
        block = j * (KT // HD) + part
        bit = jnp.bitwise_and(
            lax.shift_right_logical(bits_q, jnp.full_like(bits_q, block)), 1
        )
        wanted = jnp.where(bit == 1, seg_q, -1)
        base = pl.multiple_of(j * KT + part * HD, HD)
        seg_k = key_info[pl.ds(base, HD), :]
        key_at = base + lax.broadcasted_iota(jnp.int32, (HD, queries), 0)
        query_at = q_first + lax.broadcasted_iota(jnp.int32, (HD, queries), 1)
        allowed = (seg_k == wanted) | (key_at == query_at)
        bias[part * HD : (part + 1) * HD, :] = jnp.where(allowed, 0.0, NEGATIVE)


def attend_forward_kernel(
    bounds, q_ref, kv_ref, row_info, key_info, out_ref, log_ref, q_pairs, v_turned, bias, top, total, acc
):
    step = pl.program_id(0)
    rows, width = q_ref.shape
    pairs = width // PAIR
    tiles = kv_ref.shape[0] // KT

    @pl.when(step == 0)
    def _():
        for j in range(tiles):
            v_turned[j] = kv_ref[j * KT : (j + 1) * KT, width:].T

    masked_pairs(q_ref, q_pairs, pairs, HD**-0.5)
    top[...] = jnp.full_like(top, NEGATIVE)
    total[...] = jnp.zeros_like(total)
    acc[...] = jnp.zeros_like(acc)
    q_first = bounds[step, 2]

    @pl.loop(bounds[step, 0], bounds[step, 1])
    def _(j):
        tile_bias(j, q_first, row_info, key_info, bias)
        keys_at = pl.multiple_of(j * KT, KT)
        for p in range(pairs):
            keys = kv_ref[pl.ds(keys_at, KT), p * PAIR : (p + 1) * PAIR]
            scores = nt(keys, q_pairs[p])
            for e in range(2):
                h = 2 * p + e
                mine = scores[:, e * rows : (e + 1) * rows] + bias[...]
                before = top[h : h + 1, :]
                now = jnp.maximum(before, jnp.max(mine, axis=0, keepdims=True))
                fade = jnp.exp(before - now)
                expos = jnp.exp(mine - now)
                top[h : h + 1, :] = now
                total[h : h + 1, :] = fade * total[h : h + 1, :] + jnp.sum(
                    expos, axis=0, keepdims=True
                )
                span = slice(h * HD, (h + 1) * HD)
                acc[span, :] = acc[span, :] * fade + nn(v_turned[j, span, :], expos.astype(BF))

    heads = width // HD
    for h in range(heads):
        span = slice(h * HD, (h + 1) * HD)
        acc[span, :] = acc[span, :] / total[h : h + 1, :]
    out_ref[...] = acc[...].T.astype(BF)
    log_ref[...] = top[...] + jnp.log(jnp.maximum(total[...], 1e-37))


def attend_forward(bounds, qkv, kv, row_info, key_info):
    rows, width = qkv.shape[0], qkv.shape[1] // 3
    keys = kv.shape[0]
    stat_rows = 16
    return pl.pallas_call(
        attend_forward_kernel,
        name="attend_forward",
        grid_spec=pltpu.PrefetchScalarGridSpec(
            num_scalar_prefetch=1,
            grid=(rows // QT,),
            in_specs=[
                pl.BlockSpec((QT, width), lambda i, b: (i, 0)),
                pl.BlockSpec((keys, 2 * width), lambda i, b: (0, 0), pipeline_mode=pl.Buffered(1)),
                pl.BlockSpec((8, QT), lambda i, b: (0, i)),
                pl.BlockSpec((keys, 1), lambda i, b: (0, 0), pipeline_mode=pl.Buffered(1)),
            ],
            out_specs=[
                pl.BlockSpec((QT, width), lambda i, b: (i, 0)),
                pl.BlockSpec((stat_rows, QT), lambda i, b: (0, i)),
            ],
            scratch_shapes=[
                pltpu.VMEM((width // PAIR, 2 * QT, PAIR), BF),
                pltpu.VMEM((keys // KT, width, KT), BF),
                pltpu.VMEM((KT, QT), F32),
                pltpu.VMEM((stat_rows, QT), F32),
                pltpu.VMEM((stat_rows, QT), F32),
                pltpu.VMEM((width, QT), F32),
            ],
        ),
        out_shape=[
            jax.ShapeDtypeStruct((rows, width), BF),
            jax.ShapeDtypeStruct((stat_rows, rows), F32),
        ],
        compiler_params=params_of(),
    )(bounds, qkv, kv, row_info, key_info)


def attend_backward_kernel(
    bounds, q_ref, kv_ref, row_info, key_info, out_ref, log_ref, grad_ref,
    dq_ref, dkv_ref, q_pairs, g_pairs, k_turned, bias, inner, dq_acc, dkv_acc,
):
    step = pl.program_id(0)
    rows, width = q_ref.shape
    pairs = width // PAIR
    tiles = kv_ref.shape[0] // KT

    @pl.when(step == 0)
    def _():
        for j in range(tiles):
            k_turned[j] = kv_ref[j * KT : (j + 1) * KT, :width].T
        dkv_acc[...] = jnp.zeros_like(dkv_acc)

    masked_pairs(q_ref, q_pairs, pairs, HD**-0.5)
    masked_pairs(grad_ref, g_pairs, pairs, None)
    head_of = lax.broadcasted_iota(jnp.int32, (inner.shape[0], width), 1) // HD
    row_of = lax.broadcasted_iota(jnp.int32, (inner.shape[0], width), 0)
    chosen = jnp.where(head_of == row_of, 1.0, 0.0)
    product = out_ref[...].astype(F32) * grad_ref[...].astype(F32)
    inner[...] = nt(chosen, product, precision=lax.Precision.HIGHEST)
    dq_acc[...] = jnp.zeros_like(dq_acc)
    q_first = bounds[step, 2]

    @pl.loop(bounds[step, 0], bounds[step, 1])
    def _(j):
        tile_bias(j, q_first, row_info, key_info, bias)
        here = pl.ds(pl.multiple_of(j * KT, KT), KT)
        for p in range(pairs):
            lanes = slice(p * PAIR, (p + 1) * PAIR)
            v_lanes = slice(width + p * PAIR, width + (p + 1) * PAIR)
            scores = nt(kv_ref[here, lanes], q_pairs[p])
            grad_probs = nt(kv_ref[here, v_lanes], g_pairs[p])
            probs, grads = [], []
            for e in range(2):
                h = 2 * p + e
                cols = slice(e * rows, (e + 1) * rows)
                prob = jnp.exp(scores[:, cols] + bias[...] - log_ref[h : h + 1, :])
                grad = (prob * (grad_probs[:, cols] - inner[h : h + 1, :])).astype(BF)
                probs.append(prob.astype(BF))
                grads.append(grad)
                span = slice(h * HD, (h + 1) * HD)
                dq_acc[span, :] += nn(k_turned[j, span, :], grad)
            dkv_acc[here, lanes] += nn(jnp.concatenate(grads, axis=1), q_pairs[p])
            dkv_acc[here, v_lanes] += nn(jnp.concatenate(probs, axis=1), g_pairs[p])

    dq_ref[...] = (dq_acc[...] * HD**-0.5).T.astype(BF)

    @pl.when(step == pl.num_programs(0) - 1)
    def _():
        dkv_ref[...] = dkv_acc[...].astype(BF)


def attend_backward(bounds, qkv, kv, row_info, key_info, attn, logs, grad_attn):
    rows, width = attn.shape
    keys = kv.shape[0]
    stat_rows = logs.shape[0]
    whole = dict(pipeline_mode=pl.Buffered(1))
    return pl.pallas_call(
        attend_backward_kernel,
        name="attend_backward",
        grid_spec=pltpu.PrefetchScalarGridSpec(
            num_scalar_prefetch=1,
            grid=(rows // QT,),
            in_specs=[
                pl.BlockSpec((QT, width), lambda i, b: (i, 0)),
                pl.BlockSpec((keys, 2 * width), lambda i, b: (0, 0), **whole),
                pl.BlockSpec((8, QT), lambda i, b: (0, i)),
                pl.BlockSpec((keys, 1), lambda i, b: (0, 0), **whole),
                pl.BlockSpec((QT, width), lambda i, b: (i, 0)),
                pl.BlockSpec((stat_rows, QT), lambda i, b: (0, i)),
                pl.BlockSpec((QT, width), lambda i, b: (i, 0)),
            ],
            out_specs=[
                pl.BlockSpec((QT, width), lambda i, b: (i, 0)),
                pl.BlockSpec((keys, 2 * width), lambda i, b: (0, 0), **whole),
            ],
            scratch_shapes=[
                pltpu.VMEM((width // PAIR, 2 * QT, PAIR), BF),
                pltpu.VMEM((width // PAIR, 2 * QT, PAIR), BF),
                pltpu.VMEM((keys // KT, width, KT), BF),
                pltpu.VMEM((KT, QT), F32),
                pltpu.VMEM((stat_rows, QT), F32),
                pltpu.VMEM((width, QT), F32),
                pltpu.VMEM((keys, 2 * width), F32),
            ],
        ),
        out_shape=[
            jax.ShapeDtypeStruct((rows, width), BF),
            jax.ShapeDtypeStruct((keys, 2 * width), BF),
        ],
        compiler_params=params_of(),
    )(bounds, qkv, kv, row_info, key_info, attn, logs, grad_attn)


def attention_plan(segment_ids, pad_mask, random_blocks, global_blocks, rows):
    seq_count, nblocks = random_blocks.shape[0], random_blocks.shape[1]
    seq_len = segment_ids.shape[0] // seq_count
    rank = lax.axis_index("tensor")
    seq, half = rank // 2, lax.rem(rank, 2)
    segs = lax.dynamic_index_in_dim(segment_ids.reshape(seq_count, seq_len), seq, 0, False)
    pads = lax.dynamic_index_in_dim(pad_mask.reshape(seq_count, seq_len), seq, 0, False)
    randoms = lax.dynamic_index_in_dim(random_blocks, seq, 0, False)
    globs = lax.dynamic_index_in_dim(global_blocks, seq, 0, False)
    block_size = seq_len // nblocks
    one = jnp.int32(1)
    block = jnp.arange(nblocks, dtype=jnp.int32)

    def either(a, b):
        return jnp.bitwise_or(a, b)

    block_bits = lax.shift_left(one, block)
    window = either(
        block_bits,
        either(
            jnp.where(block > 0, lax.shift_left(one, jnp.maximum(block - 1, 0)), 0),
            jnp.where(
                block < nblocks - 1, lax.shift_left(one, jnp.minimum(block + 1, nblocks - 1)), 0
            ),
        ),
    )
    for r in range(randoms.shape[1]):
        window = either(window, lax.shift_left(one, randoms[:, r]))
    glob_bits = either(lax.shift_left(one, globs[:, 0]), lax.shift_left(one, globs[:, 1]))
    first = half * rows
    seg_q = lax.dynamic_slice_in_dim(segs, first, rows)
    own_bits = lax.dynamic_slice_in_dim(window, half * (rows // block_size), rows // block_size)
    bits = jnp.broadcast_to(own_bits[:, None], (rows // block_size, block_size)).reshape(rows)
    numbers = jnp.arange(globs.shape[0], dtype=jnp.int32)
    is_doc = seg_q[None, :] == numbers[:, None]
    bits = either(bits, jnp.sum(jnp.where(is_doc, glob_bits[:, None], 0), axis=0))
    row_info = jnp.concatenate(
        [seg_q[None], bits[None], jnp.zeros((6, rows), jnp.int32)], axis=0
    )
    key_info = jnp.where(pads == 1, segs, -2)[:, None]
    tiles = seg_q.reshape(rows // QT, QT)
    low = jnp.sum((segs[None, :] < tiles[:, :1]).astype(jnp.int32), axis=1)
    high = jnp.sum((segs[None, :] <= tiles[:, -1:]).astype(jnp.int32), axis=1)
    starts = first + QT * jnp.arange(rows // QT, dtype=jnp.int32)
    bounds = jnp.stack([low // KT, (high + KT - 1) // KT, starts, starts], axis=1)
    return bounds, row_info, key_info


def normalize(resid):
    center = resid - jnp.mean(resid, axis=1, keepdims=True)
    inverse = lax.rsqrt(jnp.mean(center * center, axis=1, keepdims=True) + EPSILON)
    return center * inverse, inverse


def norm_backward(grad_normed, normal_hat, inverse, gain):
    grad_hat = grad_normed * gain
    grad_resid = inverse * (
        grad_hat
        - jnp.mean(grad_hat, axis=1, keepdims=True)
        - normal_hat * jnp.mean(grad_hat * normal_hat, axis=1, keepdims=True)
    )
    return grad_resid, jnp.sum(grad_normed * normal_hat, axis=0), jnp.sum(grad_normed, axis=0)


def on_device(
    layer_in, query_weight, key_weight, value_weight, output_weight, inner_weight, outer_weight,
    query_bias, value_bias, output_bias, inner_bias, outer_bias, first_gain, first_shift,
    second_gain, second_shift, segment_ids, pad_mask, random_blocks, global_blocks, output_grad,
):
    rows, width = layer_in.shape
    dp, tp = lax.axis_size("dp"), lax.axis_size("tensor")
    own_rows, own_cols = query_weight.shape
    own_units = inner_weight.shape[1]
    units = own_units * tp

    packed = jnp.concatenate(
        [query_weight, key_weight, value_weight, output_weight.T, inner_weight, outer_weight.T],
        axis=1,
    )
    every = lax.all_gather(packed, ("dp", "tensor"), axis=0, tiled=False)
    every = every.reshape(dp, tp, own_rows, packed.shape[1])

    def whole(first, wide):
        part = every[:, :, :, first : first + wide]
        return part.transpose(0, 2, 1, 3).reshape(dp * own_rows, tp * wide)

    wqkv = jnp.concatenate([whole(i * own_cols, own_cols) for i in range(3)], axis=1)
    wo_t = whole(3 * own_cols, own_cols)
    w_in = whole(4 * own_cols, own_units)
    w_out_t = whole(4 * own_cols + own_units, own_units)

    small = [query_bias, value_bias, output_bias, outer_bias, first_gain, first_shift,
             second_gain, second_shift, inner_bias]
    sizes = [s.shape[0] for s in small]
    all_small = lax.all_gather(jnp.concatenate(small), ("dp", "tensor"), axis=0, tiled=False)
    offsets = [sum(sizes[:i]) for i in range(len(sizes))]
    (bq, bv, bo, bout, g1, s1, g2, s2, bin_) = (
        all_small[:, o : o + n].reshape(-1) for o, n in zip(offsets, sizes)
    )
    bqkv = jnp.concatenate([bq, jnp.zeros_like(bq), bv])

    bounds, row_info, key_info = attention_plan(
        segment_ids, pad_mask, random_blocks, global_blocks, rows
    )
    qkv = (nn(layer_in, wqkv) + bqkv).astype(BF)
    kv = gather_pair(qkv, width).reshape(2 * rows, 2 * width)
    attn, logs = attend_forward(bounds, qkv, kv, row_info, key_info)

    first_resid = layer_in.astype(F32) + nt(attn, wo_t) + bo
    first_hat, first_inverse = normalize(first_resid)
    first_norm = first_hat * g1 + s1
    norm_low = first_norm.astype(BF)
    inner_pre = nn(norm_low, w_in) + bin_
    inner_act, gelu_pull = jax.vjp(partial(jax.nn.gelu, approximate=False), inner_pre)
    hidden = inner_act.astype(BF)
    second_resid = first_norm + nt(hidden, w_out_t) + bout
    second_hat, second_inverse = normalize(second_resid)
    layer_out = (second_hat * g2 + s2).astype(BF)

    grad_second, d_g2, d_s2 = norm_backward(output_grad.astype(F32), second_hat, second_inverse, g2)
    d_bout = jnp.sum(grad_second, axis=0)
    grad_ffn = grad_second.astype(BF)
    d_w_out_t = tn(grad_ffn, hidden)
    grad_inner = gelu_pull(nn(grad_ffn, w_out_t))[0].astype(BF)
    d_bin = jnp.sum(grad_inner.astype(F32), axis=0)
    d_w_in = tn(norm_low, grad_inner)
    grad_first_norm = grad_second + nt(grad_inner, w_in)
    grad_first, d_g1, d_s1 = norm_backward(grad_first_norm, first_hat, first_inverse, g1)
    d_bo = jnp.sum(grad_first, axis=0)
    grad_proj = grad_first.astype(BF)
    d_wo_t = tn(grad_proj, attn)
    grad_attn = nn(grad_proj, wo_t).astype(BF)

    dq, dkv = attend_backward(bounds, qkv, kv, row_info, key_info, attn, logs, grad_attn)
    both = dkv.reshape(2, rows, 2 * width)
    half = lax.rem(lax.axis_index("tensor"), 2)
    other = swap_pair(both)
    mine = lax.dynamic_index_in_dim(both, half, 0, False)
    dkv_own = (mine.astype(F32) + other.astype(F32)).astype(BF)
    d_qkv = jnp.concatenate([dq, dkv_own], axis=1)
    d_bqkv = jnp.sum(d_qkv.astype(F32), axis=0)
    d_wqkv = tn(layer_in, d_qkv)
    input_grad = grad_first + nt(d_qkv, wqkv)

    def split(full, wide):
        return full.reshape(dp, own_rows, tp, wide).transpose(0, 2, 1, 3).astype(BF)

    grads = jnp.concatenate(
        [split(d_wqkv[:, i * width : (i + 1) * width], own_cols) for i in range(3)]
        + [split(d_wo_t, own_cols), split(d_w_in, own_units), split(d_w_out_t, own_units)],
        axis=3,
    ).reshape(dp * tp * own_rows, packed.shape[1])
    mine_w = lax.psum_scatter(grads, ("dp", "tensor"), scatter_dimension=0, tiled=True).astype(F32)
    small_grads = [d_bqkv[:width], d_bqkv[2 * width :], d_bo, d_bout, d_g1, d_s1, d_g2, d_s2, d_bin]
    small_flat = jnp.concatenate([g.reshape(dp * tp, -1) for g in small_grads], axis=1)
    mine_s = lax.psum_scatter(small_flat, ("dp", "tensor"), scatter_dimension=0, tiled=True)[0]
    (r_bq, r_bv, r_bo, r_bout, r_g1, r_s1, r_g2, r_s2, r_bin) = (
        mine_s[o : o + n] for o, n in zip(offsets, sizes)
    )
    c = own_cols
    return (
        layer_out,
        input_grad,
        mine_w[:, :c],
        mine_w[:, c : 2 * c],
        mine_w[:, 2 * c : 3 * c],
        mine_w[:, 3 * c : 4 * c].T,
        mine_w[:, 4 * c : 4 * c + own_units],
        mine_w[:, 4 * c + own_units :].T,
        r_bq, r_bv, r_bo, r_bin, r_bout, r_g1, r_s1, r_g2, r_s2,
    )


def solution(mesh):
    tokens = P(("dp", "tensor"), None)
    vector = P(("dp", "tensor"))
    cols, turned = P("dp", "tensor"), P("tensor", "dp")
    return jax.shard_map(
        on_device,
        mesh=mesh,
        in_specs=(tokens, cols, cols, cols, turned, cols, turned)
        + (vector,) * 9
        + (P("dp"), P("dp"), P("dp", None, None), P("dp", None, None), tokens),
        out_specs=(tokens, tokens, cols, cols, cols, turned, cols, turned) + (vector,) * 9,
        check_vma=False,
    )
```

```python
from functools import partial

import jax
import jax.numpy as jnp
from jax import lax
from jax.experimental import pallas as pl
from jax.experimental.pallas import tpu as pltpu
from jax.sharding import PartitionSpec as P

HD = 64
PAIR = 2 * HD
QT = 256
KT = 128
EPSILON = 1e-06
NEGATIVE = -1e30
MESH = pl.DeviceIdType.MESH
VMEM_LIMIT = 56 * 2**20
BF = jnp.bfloat16
F32 = jnp.float32


def params_of(collective_id=None):
    if collective_id is None:
        return pltpu.CompilerParams(vmem_limit_bytes=VMEM_LIMIT)
    return pltpu.CompilerParams(
        vmem_limit_bytes=VMEM_LIMIT, collective_id=collective_id, has_side_effects=True
    )


def nt(left, right, **more):
    return lax.dot_general(
        left, right, (((1,), (1,)), ((), ())), preferred_element_type=F32, **more
    )


def nn(left, right):
    return lax.dot_general(left, right, (((1,), (0,)), ((), ())), preferred_element_type=F32)


def tn(left, right):
    return lax.dot_general(left, right, (((0,), (0,)), ((), ())), preferred_element_type=F32)


def sibling_of():
    rank = lax.axis_index("tensor")
    half = lax.rem(rank, 2)
    return half, {"tensor": rank + 1 - 2 * half}


def meet(sibling):
    barrier = pltpu.get_barrier_semaphore()
    pl.semaphore_signal(barrier, inc=1, device_id=sibling, device_id_type=MESH)
    pl.semaphore_wait(barrier, 1)


def swap_keys_kernel(qkv_ref, other_ref, send_sem, recv_sem):
    half, sibling = sibling_of()
    meet(sibling)
    third = qkv_ref.shape[1] // 6
    moves = [
        pltpu.make_async_remote_copy(
            qkv_ref.at[:, (3 * y + 1) * third : (3 * y + 3) * third],
            other_ref.at[:, 2 * y * third : 2 * (y + 1) * third],
            send_sem.at[y], recv_sem.at[y], device_id=sibling, device_id_type=MESH,
        )
        for y in range(2)
    ]
    for move in moves:
        move.start()
    for move in moves:
        move.wait()


def swap_keys(qkv):
    rows, width = qkv.shape
    return pl.pallas_call(
        swap_keys_kernel,
        name="swap_keys",
        out_shape=jax.ShapeDtypeStruct((rows, width * 2 // 3), qkv.dtype),
        in_specs=[pl.BlockSpec(memory_space=pl.ANY)],
        out_specs=pl.BlockSpec(memory_space=pl.ANY),
        scratch_shapes=[pltpu.SemaphoreType.DMA((2,))] * 2,
        compiler_params=params_of(1),
    )(qkv)


def swap_pair_kernel(both_ref, other_ref, send_sem, recv_sem):
    half, sibling = sibling_of()
    meet(sibling)
    away = pltpu.make_async_remote_copy(
        both_ref.at[1 - half], other_ref, send_sem, recv_sem,
        device_id=sibling, device_id_type=MESH,
    )
    away.start()
    away.wait()


def swap_pair(both):
    return pl.pallas_call(
        swap_pair_kernel,
        name="swap_pair",
        out_shape=jax.ShapeDtypeStruct(both.shape[1:], both.dtype),
        in_specs=[pl.BlockSpec(memory_space=pl.ANY)],
        out_specs=pl.BlockSpec(memory_space=pl.ANY),
        scratch_shapes=[pltpu.SemaphoreType.DMA(())] * 2,
        compiler_params=params_of(2),
    )(both)


def places():
    dp, rank = lax.axis_index("dp"), lax.axis_index("tensor")
    core, y = lax.rem(rank, 2), rank // 2
    z, x = dp // 2, lax.rem(dp, 2)
    sibling = {"dp": dp, "tensor": rank + 1 - 2 * core}
    near_x = {"dp": dp + 1 - 2 * x, "tensor": rank}
    near_y = {"dp": dp, "tensor": rank + 2 - 4 * y}
    first = {"dp": dp + (1 - core) * (1 - 2 * x), "tensor": rank + core * (2 - 4 * y)}
    second = {"dp": dp + core * (1 - 2 * x), "tensor": rank + (1 - core) * (2 - 4 * y)}
    xa, ya = x + (1 - core) * (1 - 2 * x), y + core * (1 - 2 * y)
    xb, yb = x + core * (1 - 2 * x), y + (1 - core) * (1 - 2 * y)
    return dict(dp=dp, rank=rank, core=core, y=y, z=z, x=x, sibling=sibling, first=first, second=second,
                xa=xa, ya=ya, xb=xb, yb=yb)


def gather_kernel(n, mine_ref, small_ref, out_ref, all_small, chip, sib, local_sem, pair_sem, zs, zr, as_, ar, bs, br, ss, sr):
    w = places()
    dp, rank, core, y, z, x = (w[k] for k in ("dp", "rank", "core", "y", "z", "x"))
    block, wide = mine_ref.shape[1], mine_ref.shape[2]
    slab = block // 2
    up, down = {"dp": lax.rem(dp + 2, 2 * n), "tensor": rank}, {"dp": lax.rem(dp + 2 * n - 2, 2 * n), "tensor": rank}
    barrier = pltpu.get_barrier_semaphore()
    for other in (w["sibling"], w["first"], w["second"], up, down):
        pl.semaphore_signal(barrier, inc=1, device_id=other, device_id_type=MESH)
    pl.semaphore_wait(barrier, 5)

    pair = pltpu.make_async_remote_copy(mine_ref, sib, pair_sem.at[0], pair_sem.at[1], device_id=w["sibling"], device_id_type=MESH)
    pair.start()
    pair.wait()
    chip[...] = mine_ref[...] + sib[...]
    rows_own = pl.ds(pl.multiple_of(core * slab, slab), slab)
    own_at = pl.ds(pl.multiple_of(dp * block, block), block)
    cols_own = pl.ds(pl.multiple_of(y * wide, wide), wide)
    keep = pltpu.make_async_copy(chip, out_ref.at[:, own_at, cols_own], local_sem.at[0])
    keep.start()
    keep_small = pltpu.make_async_copy(small_ref, all_small.at[dp, rank], local_sem.at[1])
    keep_small.start()

    groups = {0: slice(0, 1), 1: slice(1, 3)}

    def spot(g, zi, xi, yi):
        d = zi * 2 + xi
        if g == 2:
            return all_small.at[d, yi * 2 + core]
        rows = pl.ds(pl.multiple_of(d * block + core * slab, slab), slab)
        cols = pl.ds(pl.multiple_of(yi * wide, wide), wide)
        return out_ref.at[groups[g], rows, cols]

    def own(g):
        return small_ref if g == 2 else chip.at[groups[g], rows_own, :]

    def move(g, zi, xi, yi, dev, ssem, rsem, source=None):
        at = spot(g, zi, xi, yi)
        return pltpu.make_async_remote_copy(at if source is None else source, at, ssem, rsem, device_id=dev, device_id_type=MESH)

    def line_up(g, s):
        return move(g, z - s, x, y, up, zs.at[g, 0, s], zr.at[g, 0, s], own(g) if s == 0 else None)

    def line_down(g, s):
        return move(g, z + s, x, y, down, zs.at[g, 1, s], zr.at[g, 1, s], own(g) if s == 0 else None)

    def to_first(g, zi, source=None):
        return move(g, zi, x, y, w["first"], as_.at[g, zi], ar.at[g, zi], source)

    def to_second(g, zi, far, source=None):
        xi, yi = (w["xa"], w["ya"]) if far else (x, y)
        return move(g, zi, xi, yi, w["second"], bs.at[g, far, zi], br.at[g, far, zi], source)

    def to_sibling(g, zi, quarter, source=None):
        xi = (x, w["xa"], w["xb"], w["xa"] + w["xb"] - x)[quarter]
        yi = (y, w["ya"], w["yb"], w["ya"] + w["yb"] - y)[quarter]
        return move(g, zi, xi, yi, w["sibling"], ss.at[g, quarter, zi], sr.at[g, quarter, zi], source)

    def begin(g):
        @pl.when(z < n - 1)
        def _():
            line_up(g, 0).start()

        @pl.when(z > 0)
        def _():
            line_down(g, 0).start()

        to_first(g, z, own(g)).start()
        to_second(g, z, 0, own(g)).start()
        if g == 2:
            to_sibling(g, z, 0, own(g)).start()

    def first_in(g, zi):
        got = move(g, zi, w["xa"], w["ya"], w["first"], as_.at[g, zi], ar.at[g, zi])
        got.wait_recv()
        to_second(g, zi, 1).start()
        to_sibling(g, zi, 1).start()

    def second_in(g, zi, far):
        q = 2 + far
        xi = (w["xb"], w["xa"] + w["xb"] - x)[far]
        yi = (w["yb"], w["ya"] + w["yb"] - y)[far]
        move(g, zi, xi, yi, w["second"], bs.at[g, far, zi], br.at[g, far, zi]).wait_recv()
        to_sibling(g, zi, q).start()

    def below_in(g, s):
        zi = z - 1 - s
        move(g, zi, x, y, up, zs.at[g, 0, s], zr.at[g, 0, s]).wait_recv()
        if s + 1 < n - 1:
            @pl.when(z < n - 1)
            def _():
                line_up(g, s + 1).start()
        to_first(g, zi).start()
        to_second(g, zi, 0).start()
        to_sibling(g, zi, 0).start()

    def above_in(g, s):
        zi = z + 1 + s
        move(g, zi, x, y, down, zs.at[g, 1, s], zr.at[g, 1, s]).wait_recv()
        if s + 1 < n - 1:
            @pl.when(z > 0)
            def _():
                line_down(g, s + 1).start()
        to_first(g, zi).start()
        to_second(g, zi, 0).start()
        to_sibling(g, zi, 0).start()

    def steps(gs):
        for g in gs:
            first_in(g, z)
        for s in range(n - 1):
            @pl.when(z - 1 - s >= 0)
            def _(s=s):
                for g in gs:
                    below_in(g, s)

            @pl.when(z + 1 + s < n)
            def _(s=s):
                for g in gs:
                    above_in(g, s)
            if s > 0:
                both(s, lambda g, zi: first_in(g, zi), gs)
        both(n - 1, lambda g, zi: first_in(g, zi), gs)
        for g in gs:
            second_in(g, z, 0)
        for g in gs:
            second_in(g, z, 1)
        for s in range(1, n):
            both(s, lambda g, zi: second_in(g, zi, 0), gs)
            both(s, lambda g, zi: second_in(g, zi, 1), gs)

    def both(s, what, gs):
        @pl.when(z - s >= 0)
        def _():
            for g in gs:
                what(g, z - s)

        @pl.when(z + s < n)
        def _():
            for g in gs:
                what(g, z + s)

    begin(2)
    begin(0)
    begin(1)
    steps((0, 2, 1))

    keep.wait()
    keep_small.wait()
    for g in (0, 2, 1):
        @pl.when(z < n - 1)
        def _(g=g):
            line_up(g, 0).wait_send()

        @pl.when(z > 0)
        def _(g=g):
            line_down(g, 0).wait_send()
        for s in range(1, n - 1):
            @pl.when((z < n - 1) & (z - s >= 0))
            def _(g=g, s=s):
                line_up(g, s).wait_send()

            @pl.when((z > 0) & (z + s < n))
            def _(g=g, s=s):
                line_down(g, s).wait_send()
        for zi in range(n):
            to_first(g, zi).wait_send()
            for far in range(2):
                to_second(g, zi, far).wait_send()
            for q in range(1, 4):
                to_sibling(g, zi, q).wait()
        if g == 2:
            for zi in range(n):
                to_sibling(g, zi, 0).wait()
        else:
            for zi in range(n):
                @pl.when(zi != z)
                def _(g=g, zi=zi):
                    to_sibling(g, zi, 0).wait()


def gather_weights(mine, small):
    if not in_tiles(mine.shape[1]):
        return gather_plainly(mine, small)
    dp, tp = lax.axis_size("dp"), lax.axis_size("tensor")
    n = dp // 2
    parts, block, wide = mine.shape
    dma = pltpu.SemaphoreType.DMA
    return pl.pallas_call(
        partial(gather_kernel, n), name="gather_weights",
        out_shape=[jax.ShapeDtypeStruct((parts, dp*block, wide*tp//2), mine.dtype), jax.ShapeDtypeStruct((dp, tp)+small.shape, small.dtype)],
        in_specs=[pl.BlockSpec(memory_space=pltpu.VMEM)]*2,
        out_specs=[pl.BlockSpec(memory_space=pl.ANY)]*2,
        scratch_shapes=[pltpu.VMEM(mine.shape, mine.dtype)]*2 + [dma((2,)), dma((2,)), dma((3,2,n)), dma((3,2,n)), dma((3,n)), dma((3,n)), dma((3,2,n)), dma((3,2,n)), dma((3,4,n)), dma((3,4,n))],
        compiler_params=pltpu.CompilerParams(collective_id=3, has_side_effects=True, vmem_limit_bytes=40*2**20))(mine, small)


def reduce_kernel(n, qkv_ref, o_ref, in_ref, out_ref, small_ref, res_ref, res_small,
                  sib_qkv, sib_o, sib_in, sib_out, to_b, from_b, to_a, from_a, line, from_low, from_high,
                  small_sib, small_to_b, small_from_b, small_to_a, small_from_a, small_line, small_low, small_high,
                  ss, sr, bs, br, as_, ar, zs, zr, es, er):
    w = places()
    dp, rank, core, y, z, x = (w[k] for k in ("dp", "rank", "core", "y", "z", "x"))
    block = qkv_ref.shape[2]
    slab = block // 2
    up, down = {"dp": lax.rem(dp + 2, 2 * n), "tensor": rank}, {"dp": lax.rem(dp + 2 * n - 2, 2 * n), "tensor": rank}
    barrier = pltpu.get_barrier_semaphore()
    for other in (w["sibling"], w["first"], w["second"], up, down):
        pl.semaphore_signal(barrier, inc=1, device_id=other, device_id_type=MESH)
    pl.semaphore_wait(barrier, 5)
    xs = (x, w["xa"], w["xb"], w["xa"] + w["xb"] - x)
    ys = (y, w["ya"], w["yb"], w["ya"] + w["yb"] - y)
    pieces, lane = [], 0
    for k, ref, sib in ((0, qkv_ref, sib_qkv), (0, o_ref, sib_o), (1, in_ref, sib_in), (2, out_ref, sib_out)):
        wd = ref.shape[3] // 2
        pieces.append((k, lane if k == 0 else 0, wd, ref, sib))
        lane += wd

    def rows_of(c):
        return pl.ds(pl.multiple_of(c * slab, slab), slab)

    def cols_of(yd, wd):
        return pl.ds(pl.multiple_of(yd * wd, 128), wd)

    def copy(src, dst, ssem, rsem, dev):
        return pltpu.make_async_remote_copy(src, dst, ssem, rsem, device_id=dev, device_id_type=MESH)

    def to_sibling(zd):
        out = [copy(ref.at[zd, :, rows_of(1 - core), :], sib.at[zd], ss.at[i, zd], sr.at[i, zd], w["sibling"])
               for i, (k, lane, wd, ref, sib) in enumerate(pieces)]
        out.append(copy(small_ref.at[zd], small_sib.at[zd], ss.at[4, zd], sr.at[4, zd], w["sibling"]))
        return out

    def put(target, small_target, q, zd, more, small_more):
        xd, yd = xs[q], ys[q]
        for k, lane, wd, ref, sib in pieces:
            lanes = slice(lane, lane + wd)
            total = ref[zd, xd, rows_of(core), cols_of(yd, wd)].astype(F32) + sib[zd, xd, :, cols_of(yd, wd)].astype(F32)
            for term in more:
                total = total + term[k, :, lanes].astype(F32)
            target[k, :, lanes] = total.astype(target.dtype)
        s = small_ref[zd, xd, yd * 2 + core] + small_sib[zd, xd, yd * 2 + core]
        for term in small_more:
            s = s + term[...]
        small_target[...] = s

    def over_b(far, zd):
        return (copy(to_b.at[far, zd], from_b.at[far, zd], bs.at[0, far, zd], br.at[0, far, zd], w["second"]),
                copy(small_to_b.at[far, zd], small_from_b.at[far, zd], bs.at[1, far, zd], br.at[1, far, zd], w["second"]))

    def over_a(zd):
        return (copy(to_a.at[zd], from_a.at[zd], as_.at[0, zd], ar.at[0, zd], w["first"]),
                copy(small_to_a.at[zd], small_from_a.at[zd], as_.at[1, zd], ar.at[1, zd], w["first"]))

    def over_up(zd):
        return (copy(line.at[zd], from_low.at[zd], zs.at[0, zd], zr.at[0, 0, zd], up),
                copy(small_line.at[zd], small_low.at[zd], zs.at[1, zd], zr.at[0, 1, zd], up))

    def over_down(zd):
        return (copy(line.at[zd], from_high.at[zd], zs.at[0, zd], zr.at[1, 0, zd], down),
                copy(small_line.at[zd], small_high.at[zd], zs.at[1, zd], zr.at[1, 1, zd], down))

    def start(cs):
        for c in cs:
            c.start()

    def arrive(cs):
        for c in cs:
            c.wait_recv()

    def stage_send(zd):
        start(to_sibling(zd))

    def stage_b(zd):
        arrive(to_sibling(zd))
        for q, far in ((3, 1), (2, 0)):
            put(to_b.at[far, zd], small_to_b.at[far, zd], q, zd, (), ())
            start(over_b(far, zd))

    def stage_a(zd):
        arrive(over_b(1, zd))
        put(to_a.at[zd], small_to_a.at[zd], 1, zd, (from_b.at[1, zd],), (small_from_b.at[1, zd],))
        start(over_a(zd))

    def stage_line(zd):
        arrive(over_b(0, zd))
        arrive(over_a(zd))
        put(line.at[zd], small_line.at[zd], 0, zd, (from_b.at[0, zd], from_a.at[zd]), (small_from_b.at[0, zd], small_from_a.at[zd]))

        @pl.when((zd > z) & (z == 0))
        def _():
            start(over_up(zd))

        @pl.when((zd < z) & (z == n - 1))
        def _():
            start(over_down(zd))

    def grow(zd, term, small_term):
        for k in range(3):
            line[zd, k] = (line[zd, k].astype(F32) + term[k].astype(F32)).astype(line.dtype)
        small_line[zd] = small_line[zd] + small_term[...]

    def stage_hop(zd):
        @pl.when((zd > z) & (z > 0))
        def _():
            arrive(over_up(zd))
            grow(zd, from_low.at[zd], small_low.at[zd])
            start(over_up(zd))

        @pl.when((zd < z) & (z < n - 1))
        def _():
            arrive(over_down(zd))
            grow(zd, from_high.at[zd], small_high.at[zd])
            start(over_down(zd))

    def turn(i):
        below, above = z, n - 1 - z
        near = jnp.minimum(below, above)
        only = jnp.maximum(below, above) - near
        side = jnp.where(above >= below, 1, -1)
        distance = jnp.where(i < only, only + near - i, near - (i - only) // 2)
        sign = jnp.where(i < only, side, jnp.where(lax.rem(i - only, 2) == 0, side, -side))
        return jnp.where(i == n - 1, z, z + sign * distance)

    for i in range(n):
        stage_send(turn(i))

    @pl.loop(0, n + 3)
    def _(i):
        @pl.when(i < n)
        def _():
            stage_b(turn(i))

        @pl.when((i >= 1) & (i < n + 1))
        def _():
            stage_a(turn(i - 1))

        @pl.when((i >= 2) & (i < n + 2))
        def _():
            stage_line(turn(i - 2))

        @pl.when(i >= 3)
        def _():
            stage_hop(turn(i - 3))

    mine = res_ref.at[:, rows_of(core)]
    for k in range(3):
        res_ref[k, rows_of(core), :] = line[z, k].astype(F32)
    res_small[...] = small_line[z]

    @pl.when(z > 0)
    def _():
        arrive(over_up(z))
        for k in range(3):
            res_ref[k, rows_of(core), :] += from_low[z, k].astype(F32)
        res_small[...] += small_low[z]

    @pl.when(z < n - 1)
    def _():
        arrive(over_down(z))
        for k in range(3):
            res_ref[k, rows_of(core), :] += from_high[z, k].astype(F32)
        res_small[...] += small_high[z]

    last = copy(mine, mine, es, er, w["sibling"])
    last.start()

    @pl.loop(0, n)
    def _(zd):
        for c in tuple(to_sibling(zd)) + over_b(0, zd) + over_b(1, zd) + over_a(zd):
            c.wait_send()

        @pl.when(zd > z)
        def _():
            for c in over_up(zd):
                c.wait_send()

        @pl.when(zd < z)
        def _():
            for c in over_down(zd):
                c.wait_send()
    last.wait_send()
    copy(res_ref.at[:, rows_of(1 - core)], res_ref.at[:, rows_of(1 - core)], es, er, w["sibling"]).wait_recv()


def reduce_grads(g_qkv, g_o, g_in, g_out, small):
    if not in_tiles(g_in.shape[0] // lax.axis_size("dp")):
        return reduce_plainly(g_qkv, g_o, g_in, g_out, small)
    dp, tp = lax.axis_size("dp"), lax.axis_size("tensor")
    n = dp // 2
    block = g_qkv.shape[0] // dp
    slab = block // 2
    wide = g_in.shape[1] // 2
    dma = pltpu.SemaphoreType.DMA
    split = lambda g: g.reshape(n, 2, block, g.shape[1])
    slabs = lambda *lead: pltpu.VMEM(lead + (3, slab, wide), BF)
    smalls = lambda *lead: pltpu.VMEM(lead + small.shape[2:], F32)
    V = pl.BlockSpec(memory_space=pltpu.VMEM)
    return pl.pallas_call(
        partial(reduce_kernel, n), name="reduce_grads",
        out_shape=[jax.ShapeDtypeStruct((3, block, wide), F32), jax.ShapeDtypeStruct(small.shape[2:], F32)],
        in_specs=[V]*5, out_specs=[V]*2,
        scratch_shapes=[pltpu.VMEM((n, 2, slab, g_qkv.shape[1]), BF), pltpu.VMEM((n, 2, slab, g_o.shape[1]), BF), pltpu.VMEM((n, 2, slab, g_in.shape[1]), BF), pltpu.VMEM((n, 2, slab, g_out.shape[1]), BF), slabs(2, n), slabs(2, n), slabs(n), slabs(n), slabs(n), slabs(n), slabs(n),
                        pltpu.VMEM((n, 2) + small.shape[1:], F32), smalls(2, n), smalls(2, n), smalls(n), smalls(n), smalls(n), smalls(n), smalls(n),
                        dma((5, n)), dma((5, n)), dma((2, 2, n)), dma((2, 2, n)), dma((2, n)), dma((2, n)), dma((2, n)), dma((2, 2, n)), dma(()), dma(())],
        compiler_params=pltpu.CompilerParams(collective_id=4, has_side_effects=True, vmem_limit_bytes=58*2**20))(
            split(g_qkv), split(g_o), split(g_in), split(g_out), small.reshape((n, 2) + small.shape[1:]))


def in_tiles(block):
    return block % 32 == 0


def gather_plainly(mine, small):
    dp, tp = lax.axis_size("dp"), lax.axis_size("tensor")
    parts, block, wide = mine.shape
    every = lax.all_gather(mine, ("dp", "tensor"), axis=0, tiled=False)
    every = every.reshape(dp, tp // 2, 2, parts, block, wide).sum(axis=2)
    every = every.transpose(2, 0, 3, 1, 4).reshape(parts, dp * block, tp // 2 * wide)
    all_small = lax.all_gather(small, ("dp", "tensor"), axis=0, tiled=False)
    return every, all_small.reshape((dp, tp) + small.shape)


def reduce_plainly(g_qkv, g_o, g_in, g_out, small):
    dp, tp = lax.axis_size("dp"), lax.axis_size("tensor")
    width, units = g_in.shape
    pairs, block = tp // 2, width // dp
    joined = jnp.concatenate([g.reshape(width, pairs, -1) for g in (g_qkv, g_o)], axis=2)
    every = jnp.stack([joined.reshape(width, units), g_in, g_out])
    every = every.reshape(3, dp, block, pairs, 1, units // pairs).transpose(1, 3, 4, 0, 2, 5)
    every = jnp.broadcast_to(every, (dp, pairs, 2, 3, block, units // pairs))
    every = every.reshape(dp * tp, 3, block, units // pairs)
    total = lax.psum_scatter(every, ("dp", "tensor"), scatter_dimension=0, tiled=False)
    flat = small.reshape((dp * tp,) + small.shape[2:])
    total_small = lax.psum_scatter(flat, ("dp", "tensor"), scatter_dimension=0, tiled=False)
    return total.astype(F32), total_small


def q_lanes(p, pairs):
    third = pairs // 2 * PAIR
    first = p // (pairs // 2) * 3 * third + p % (pairs // 2) * PAIR
    return slice(first, first + PAIR)


def k_lanes(p, pairs):
    third = pairs // 2 * PAIR
    first = p // (pairs // 2) * 2 * third + p % (pairs // 2) * PAIR
    return slice(first, first + PAIR)


def v_lanes(p, pairs):
    third = pairs // 2 * PAIR
    lanes = k_lanes(p, pairs)
    return slice(lanes.start + third, lanes.stop + third)


def fetch_keys(qkv_ref, other_ref, kv, sems):
    rows, third = other_ref.shape[0], other_ref.shape[1] // 4
    half = lax.rem(lax.axis_index("tensor"), 2)
    here = pl.ds(pl.multiple_of(half * rows, rows), rows)
    there = pl.ds(pl.multiple_of((1 - half) * rows, rows), rows)
    moves = [pltpu.make_async_copy(other_ref, kv.at[there, :], sems.at[2])]
    for y in range(2):
        moves.append(
            pltpu.make_async_copy(
                qkv_ref.at[:, (3 * y + 1) * third : (3 * y + 3) * third],
                kv.at[here, 2 * y * third : 2 * (y + 1) * third],
                sems.at[y],
            )
        )
    for move in moves:
        move.start()
    for move in moves:
        move.wait()


def masked_pairs(source, target, lanes_of, pairs, scale):
    rows = source.shape[0]
    low_lanes = lax.broadcasted_iota(jnp.int32, (rows, PAIR), 1) < HD
    for p in range(pairs):
        both = source[:, lanes_of(p)]
        if scale is not None:
            both = both * jnp.asarray(scale, both.dtype)
        zero = jnp.zeros_like(both)
        target[p, :rows, :] = jnp.where(low_lanes, both, zero)
        target[p, rows:, :] = jnp.where(low_lanes, zero, both)


def tile_bias(j, q_first, row_info, key_info, bias):
    seg_q, bits_q = row_info[0:1, :], row_info[1:2, :]
    queries = bias.shape[1]
    for part in range(KT // HD):
        block = j * (KT // HD) + part
        bit = jnp.bitwise_and(
            lax.shift_right_logical(bits_q, jnp.full_like(bits_q, block)), 1
        )
        wanted = jnp.where(bit == 1, seg_q, -1)
        base = pl.multiple_of(j * KT + part * HD, HD)
        seg_k = key_info[pl.ds(base, HD), :]
        key_at = base + lax.broadcasted_iota(jnp.int32, (HD, queries), 0)
        query_at = q_first + lax.broadcasted_iota(jnp.int32, (HD, queries), 1)
        allowed = (seg_k == wanted) | (key_at == query_at)
        bias[part * HD : (part + 1) * HD, :] = jnp.where(allowed, 0.0, NEGATIVE)


def attend_forward_kernel(
    bounds, q_ref, qkv_ref, other_ref, row_info, key_info, out_ref, log_ref,
    q_pairs, kv_ref, v_turned, bias, top, total, acc, sems,
):
    step = pl.program_id(0)
    rows, width = out_ref.shape
    pairs = width // PAIR
    tiles = kv_ref.shape[0] // KT

    @pl.when(step == 0)
    def _():
        fetch_keys(qkv_ref, other_ref, kv_ref, sems)
        for j in range(tiles):
            for p in range(pairs):
                span = slice(p * PAIR, (p + 1) * PAIR)
                v_turned[j, span, :] = kv_ref[j * KT : (j + 1) * KT, v_lanes(p, pairs)].T

    masked_pairs(q_ref, q_pairs, partial(q_lanes, pairs=pairs), pairs, HD**-0.5)
    top[...] = jnp.full_like(top, NEGATIVE)
    total[...] = jnp.zeros_like(total)
    acc[...] = jnp.zeros_like(acc)
    q_first = bounds[step, 2]

    @pl.loop(bounds[step, 0], bounds[step, 1])
    def _(j):
        tile_bias(j, q_first, row_info, key_info, bias)
        keys_at = pl.multiple_of(j * KT, KT)
        for p in range(pairs):
            keys = kv_ref[pl.ds(keys_at, KT), k_lanes(p, pairs)]
            scores = nt(keys, q_pairs[p])
            for e in range(2):
                h = 2 * p + e
                mine = scores[:, e * rows : (e + 1) * rows] + bias[...]
                before = top[h : h + 1, :]
                now = jnp.maximum(before, jnp.max(mine, axis=0, keepdims=True))
                fade = jnp.exp(before - now)
                expos = jnp.exp(mine - now)
                top[h : h + 1, :] = now
                total[h : h + 1, :] = fade * total[h : h + 1, :] + jnp.sum(
                    expos, axis=0, keepdims=True
                )
                span = slice(h * HD, (h + 1) * HD)
                acc[span, :] = acc[span, :] * fade + nn(v_turned[j, span, :], expos.astype(BF))

    heads = width // HD
    for h in range(heads):
        span = slice(h * HD, (h + 1) * HD)
        acc[span, :] = acc[span, :] / total[h : h + 1, :]
    out_ref[...] = acc[...].T.astype(BF)
    log_ref[...] = top[...] + jnp.log(jnp.maximum(total[...], 1e-37))


def attend_forward(bounds, qkv, other, row_info, key_info):
    rows, width = qkv.shape[0], qkv.shape[1] // 3
    keys = 2 * rows
    stat_rows = 16
    return pl.pallas_call(
        attend_forward_kernel,
        name="attend_forward",
        grid_spec=pltpu.PrefetchScalarGridSpec(
            num_scalar_prefetch=1,
            grid=(rows // QT,),
            in_specs=[
                pl.BlockSpec((QT, 3 * width), lambda i, b: (i, 0)),
                pl.BlockSpec(memory_space=pl.ANY),
                pl.BlockSpec(memory_space=pl.ANY),
                pl.BlockSpec((8, QT), lambda i, b: (0, i)),
                pl.BlockSpec((keys, 1), lambda i, b: (0, 0), pipeline_mode=pl.Buffered(1)),
            ],
            out_specs=[
                pl.BlockSpec((QT, width), lambda i, b: (i, 0)),
                pl.BlockSpec((stat_rows, QT), lambda i, b: (0, i)),
            ],
            scratch_shapes=[
                pltpu.VMEM((width // PAIR, 2 * QT, PAIR), BF),
                pltpu.VMEM((keys, 2 * width), BF),
                pltpu.VMEM((keys // KT, width, KT), BF),
                pltpu.VMEM((KT, QT), F32),
                pltpu.VMEM((stat_rows, QT), F32),
                pltpu.VMEM((stat_rows, QT), F32),
                pltpu.VMEM((width, QT), F32),
                pltpu.SemaphoreType.DMA((3,)),
            ],
        ),
        out_shape=[
            jax.ShapeDtypeStruct((rows, width), BF),
            jax.ShapeDtypeStruct((stat_rows, rows), F32),
        ],
        compiler_params=params_of(),
    )(bounds, qkv, qkv, other, row_info, key_info)


def attend_backward_kernel(
    bounds, q_ref, qkv_ref, other_ref, row_info, key_info, out_ref, log_ref, grad_ref,
    dq_ref, dkv_ref, q_pairs, g_pairs, kv_ref, k_turned, bias, inner, dq_acc, dkv_acc, sems,
):
    step = pl.program_id(0)
    rows, width = out_ref.shape
    pairs = width // PAIR
    tiles = kv_ref.shape[0] // KT

    @pl.when(step == 0)
    def _():
        fetch_keys(qkv_ref, other_ref, kv_ref, sems)
        for j in range(tiles):
            for p in range(pairs):
                span = slice(p * PAIR, (p + 1) * PAIR)
                k_turned[j, span, :] = kv_ref[j * KT : (j + 1) * KT, k_lanes(p, pairs)].T
        dkv_acc[...] = jnp.zeros_like(dkv_acc)

    masked_pairs(q_ref, q_pairs, partial(q_lanes, pairs=pairs), pairs, HD**-0.5)
    masked_pairs(grad_ref, g_pairs, lambda p: slice(p * PAIR, (p + 1) * PAIR), pairs, None)
    head_of = lax.broadcasted_iota(jnp.int32, (inner.shape[0], width), 1) // HD
    row_of = lax.broadcasted_iota(jnp.int32, (inner.shape[0], width), 0)
    chosen = jnp.where(head_of == row_of, 1.0, 0.0)
    product = out_ref[...].astype(F32) * grad_ref[...].astype(F32)
    inner[...] = nt(chosen, product, precision=lax.Precision.HIGHEST)
    dq_acc[...] = jnp.zeros_like(dq_acc)
    q_first = bounds[step, 2]

    @pl.loop(bounds[step, 0], bounds[step, 1])
    def _(j):
        tile_bias(j, q_first, row_info, key_info, bias)
        here = pl.ds(pl.multiple_of(j * KT, KT), KT)
        for p in range(pairs):
            k_here, v_here = k_lanes(p, pairs), v_lanes(p, pairs)
            scores = nt(kv_ref[here, k_here], q_pairs[p])
            grad_probs = nt(kv_ref[here, v_here], g_pairs[p])
            probs, grads = [], []
            for e in range(2):
                h = 2 * p + e
                cols = slice(e * rows, (e + 1) * rows)
                prob = jnp.exp(scores[:, cols] + bias[...] - log_ref[h : h + 1, :])
                grad = (prob * (grad_probs[:, cols] - inner[h : h + 1, :])).astype(BF)
                probs.append(prob.astype(BF))
                grads.append(grad)
                span = slice(h * HD, (h + 1) * HD)
                dq_acc[span, :] += nn(k_turned[j, span, :], grad)
            dkv_acc[here, k_here] += nn(jnp.concatenate(grads, axis=1), q_pairs[p])
            dkv_acc[here, v_here] += nn(jnp.concatenate(probs, axis=1), g_pairs[p])

    dq_ref[...] = (dq_acc[...] * HD**-0.5).T.astype(BF)

    @pl.when(step == pl.num_programs(0) - 1)
    def _():
        dkv_ref[...] = dkv_acc[...].astype(BF)


def attend_backward(bounds, qkv, other, row_info, key_info, attn, logs, grad_attn):
    rows, width = attn.shape
    keys = 2 * rows
    stat_rows = logs.shape[0]
    whole = dict(pipeline_mode=pl.Buffered(1))
    return pl.pallas_call(
        attend_backward_kernel,
        name="attend_backward",
        grid_spec=pltpu.PrefetchScalarGridSpec(
            num_scalar_prefetch=1,
            grid=(rows // QT,),
            in_specs=[
                pl.BlockSpec((QT, 3 * width), lambda i, b: (i, 0)),
                pl.BlockSpec(memory_space=pl.ANY),
                pl.BlockSpec(memory_space=pl.ANY),
                pl.BlockSpec((8, QT), lambda i, b: (0, i)),
                pl.BlockSpec((keys, 1), lambda i, b: (0, 0), **whole),
                pl.BlockSpec((QT, width), lambda i, b: (i, 0)),
                pl.BlockSpec((stat_rows, QT), lambda i, b: (0, i)),
                pl.BlockSpec((QT, width), lambda i, b: (i, 0)),
            ],
            out_specs=[
                pl.BlockSpec((QT, width), lambda i, b: (i, 0)),
                pl.BlockSpec((keys, 2 * width), lambda i, b: (0, 0), **whole),
            ],
            scratch_shapes=[
                pltpu.VMEM((width // PAIR, 2 * QT, PAIR), BF),
                pltpu.VMEM((width // PAIR, 2 * QT, PAIR), BF),
                pltpu.VMEM((keys, 2 * width), BF),
                pltpu.VMEM((keys // KT, width, KT), BF),
                pltpu.VMEM((KT, QT), F32),
                pltpu.VMEM((stat_rows, QT), F32),
                pltpu.VMEM((width, QT), F32),
                pltpu.VMEM((keys, 2 * width), F32),
                pltpu.SemaphoreType.DMA((3,)),
            ],
        ),
        out_shape=[
            jax.ShapeDtypeStruct((rows, width), BF),
            jax.ShapeDtypeStruct((keys, 2 * width), BF),
        ],
        compiler_params=params_of(),
    )(bounds, qkv, qkv, other, row_info, key_info, attn, logs, grad_attn)


def attention_plan(segment_ids, pad_mask, random_blocks, global_blocks, rows):
    seq_count, nblocks = random_blocks.shape[0], random_blocks.shape[1]
    seq_len = segment_ids.shape[0] // seq_count
    rank = lax.axis_index("tensor")
    seq, half = rank // 2, lax.rem(rank, 2)
    segs = lax.dynamic_index_in_dim(segment_ids.reshape(seq_count, seq_len), seq, 0, False)
    pads = lax.dynamic_index_in_dim(pad_mask.reshape(seq_count, seq_len), seq, 0, False)
    randoms = lax.dynamic_index_in_dim(random_blocks, seq, 0, False)
    globs = lax.dynamic_index_in_dim(global_blocks, seq, 0, False)
    block_size = seq_len // nblocks
    one = jnp.int32(1)
    block = jnp.arange(nblocks, dtype=jnp.int32)

    def either(a, b):
        return jnp.bitwise_or(a, b)

    block_bits = lax.shift_left(one, block)
    window = either(
        block_bits,
        either(
            jnp.where(block > 0, lax.shift_left(one, jnp.maximum(block - 1, 0)), 0),
            jnp.where(
                block < nblocks - 1, lax.shift_left(one, jnp.minimum(block + 1, nblocks - 1)), 0
            ),
        ),
    )
    for r in range(randoms.shape[1]):
        window = either(window, lax.shift_left(one, randoms[:, r]))
    glob_bits = either(lax.shift_left(one, globs[:, 0]), lax.shift_left(one, globs[:, 1]))
    first = half * rows
    seg_q = lax.dynamic_slice_in_dim(segs, first, rows)
    own_bits = lax.dynamic_slice_in_dim(window, half * (rows // block_size), rows // block_size)
    bits = jnp.broadcast_to(own_bits[:, None], (rows // block_size, block_size)).reshape(rows)
    numbers = jnp.arange(globs.shape[0], dtype=jnp.int32)
    is_doc = seg_q[None, :] == numbers[:, None]
    bits = either(bits, jnp.sum(jnp.where(is_doc, glob_bits[:, None], 0), axis=0))
    row_info = jnp.concatenate(
        [seg_q[None], bits[None], jnp.zeros((6, rows), jnp.int32)], axis=0
    )
    key_info = jnp.where(pads == 1, segs, -2)[:, None]
    tiles = seg_q.reshape(rows // QT, QT)
    low = jnp.sum((segs[None, :] < tiles[:, :1]).astype(jnp.int32), axis=1)
    high = jnp.sum((segs[None, :] <= tiles[:, -1:]).astype(jnp.int32), axis=1)
    starts = first + QT * jnp.arange(rows // QT, dtype=jnp.int32)
    bounds = jnp.stack([low // KT, (high + KT - 1) // KT, starts, starts], axis=1)
    return bounds, row_info, key_info


ROWS = 256
CHUNK = 768
TAIL_STEP = 0.47
TAIL = (0.266306628, 0.248031891, 0.336199252, -0.126105651, 0.607561554, -0.420410983, 0.0884173167)


def gelu_and_slope(pre):
    bell = jnp.exp(-0.5 * pre * pre)
    t = 1.0 / (1.0 + (TAIL_STEP * 0.5**0.5) * jnp.abs(pre))
    tail = TAIL[-1]
    for c in TAIL[-2::-1]:
        tail = tail * t + c
    tail = 0.5 * (tail * t) * bell
    cdf = jnp.where(pre < 0, tail, 1.0 - tail)
    return pre * cdf, cdf + pre * (bell * (2.0 * 3.141592653589793) ** -0.5)


def normalize(resid):
    center = resid - jnp.mean(resid, axis=1, keepdims=True)
    inverse = lax.rsqrt(jnp.mean(center * center, axis=1, keepdims=True) + EPSILON)
    return center * inverse, inverse


def norm_backward(grad_normed, normal_hat, inverse, gain):
    grad_hat = grad_normed * gain
    return inverse * (
        grad_hat
        - jnp.mean(grad_hat, axis=1, keepdims=True)
        - normal_hat * jnp.mean(grad_hat * normal_hat, axis=1, keepdims=True)
    )


def middle_kernel(
    x_ref, attn_ref, cot_ref, w_ref, vec_ref, unit_bias,
    final_ref, first_grad, attn_grad, norm_low, hidden, ffn_grad, unit_grad, proj_grad,
    sums, unit_sums, slope,
):
    width = x_ref.shape[1]
    third = width // 2
    wide = w_ref.shape[2] // 2
    proj_cols = [slice((y + 1) * wide - third, (y + 1) * wide) for y in range(2)]
    halves = [slice(y * third, (y + 1) * third) for y in range(2)]
    chunks = [slice(u, u + CHUNK) for u in range(0, w_ref.shape[2], CHUNK)]
    out_bias, last_bias, gain_1, shift_1, gain_2, shift_2 = (vec_ref[i : i + 1, :] for i in range(2, 8))

    @pl.when(pl.program_id(0) == 0)
    def _():
        sums[...] = jnp.zeros_like(sums)
        unit_sums[...] = jnp.zeros_like(unit_sums)

    resid = x_ref[...].astype(F32) + out_bias
    for y in range(2):
        resid += nt(attn_ref[:, halves[y]], w_ref[0, :, proj_cols[y]])
    hat_1, inverse_1 = normalize(resid)
    first_norm = hat_1 * gain_1 + shift_1
    low = first_norm.astype(BF)
    norm_low[...] = low
    resid = first_norm + last_bias
    for cols in chunks:
        act, slope[:, cols] = gelu_and_slope(nn(low, w_ref[1, :, cols]) + unit_bias[:, cols])
        act = act.astype(BF)
        hidden[:, cols] = act
        resid += nt(act, w_ref[2, :, cols])
    hat_2, inverse_2 = normalize(resid)
    final_ref[...] = (hat_2 * gain_2 + shift_2).astype(BF)

    cot = cot_ref[...].astype(F32)
    grad = norm_backward(cot, hat_2, inverse_2, gain_2)
    sums[6:7, :] += jnp.sum(cot * hat_2, axis=0, keepdims=True)
    sums[7:8, :] += jnp.sum(cot, axis=0, keepdims=True)
    sums[3:4, :] += jnp.sum(grad, axis=0, keepdims=True)
    low = grad.astype(BF)
    ffn_grad[...] = low
    for cols in chunks:
        act = (nn(low, w_ref[2, :, cols]) * slope[:, cols]).astype(BF)
        unit_grad[:, cols] = act
        unit_sums[0:1, cols] += jnp.sum(act.astype(F32), axis=0, keepdims=True)
        grad += nt(act, w_ref[1, :, cols])
    sums[4:5, :] += jnp.sum(grad * hat_1, axis=0, keepdims=True)
    sums[5:6, :] += jnp.sum(grad, axis=0, keepdims=True)
    grad = norm_backward(grad, hat_1, inverse_1, gain_1)
    sums[2:3, :] += jnp.sum(grad, axis=0, keepdims=True)
    first_grad[...] = grad
    low = grad.astype(BF)
    proj_grad[...] = low
    for y in range(2):
        attn_grad[:, halves[y]] = nn(low, w_ref[0, :, proj_cols[y]]).astype(BF)


def middle(layer_in, attn, output_grad, weights, vectors, unit_bias):
    rows, width = layer_in.shape
    units = weights.shape[2]
    tile = lambda w: pl.BlockSpec((ROWS, w), lambda i: (i, 0))
    whole = lambda a: pl.BlockSpec(a.shape, lambda i: (0,) * len(a.shape), pipeline_mode=pl.Buffered(1))
    fixed = lambda w: pl.BlockSpec((8, w), lambda i: (0, 0))
    shape = lambda w, t: jax.ShapeDtypeStruct((rows, w), t)
    return pl.pallas_call(
        middle_kernel,
        name="middle",
        grid=(rows // ROWS,),
        in_specs=[tile(width)] * 3 + [whole(weights), whole(vectors), whole(unit_bias)],
        out_specs=[tile(width)] * 4 + [tile(units), tile(width), tile(units), tile(width), fixed(width), fixed(units)],
        out_shape=[
            shape(width, BF), shape(width, F32), shape(width, BF), shape(width, BF), shape(units, BF),
            shape(width, BF), shape(units, BF), shape(width, BF),
            jax.ShapeDtypeStruct((8, width), F32), jax.ShapeDtypeStruct((8, units), F32),
        ],
        scratch_shapes=[pltpu.VMEM((ROWS, units), F32)],
        compiler_params=params_of(),
    )(layer_in, attn, output_grad, weights, vectors, unit_bias)


def on_device(
    layer_in, query_weight, key_weight, value_weight, output_weight, inner_weight, outer_weight,
    query_bias, value_bias, output_bias, inner_bias, outer_bias, first_gain, first_shift,
    second_gain, second_shift, segment_ids, pad_mask, random_blocks, global_blocks, output_grad,
):
    rows, width = layer_in.shape
    dp, tp = lax.axis_size("dp"), lax.axis_size("tensor")
    own_rows, own_cols = query_weight.shape
    own_units = inner_weight.shape[1]
    third = width // 2
    half = lax.rem(lax.axis_index("tensor"), 2)

    def beside(own):
        zero = jnp.zeros_like(own)
        return jnp.concatenate(
            [jnp.where(half == 0, own, zero), jnp.where(half == 0, zero, own)], axis=1
        )

    mine = jnp.stack(
        [
            jnp.concatenate(
                [beside(w) for w in (query_weight, key_weight, value_weight, output_weight.T)], axis=1
            ),
            beside(inner_weight),
            beside(outer_weight.T),
        ]
    )
    small = [query_bias, value_bias, output_bias, outer_bias, first_gain, first_shift,
             second_gain, second_shift, inner_bias]
    one, eight = query_bias.shape[0], 8 * query_bias.shape[0]
    used = eight + inner_bias.shape[0]
    room = -(-used // 1024) * 1024
    flat = jnp.concatenate(small + [jnp.zeros((room - used,), F32)]).reshape(room // 128, 128)
    weights, all_small = gather_weights(mine, flat)
    all_small = all_small.reshape(dp * tp, room)
    vectors = all_small[:, :eight].reshape(dp * tp, 8, one).transpose(1, 0, 2).reshape(8, width)
    unit_bias = all_small[:, eight:used].reshape(1, -1)
    zero = jnp.zeros((1, third), F32)
    bqkv = jnp.concatenate(
        [v for y in range(2) for v in (vectors[:1, y * third : (y + 1) * third], zero,
                                       vectors[1:2, y * third : (y + 1) * third])], axis=1,
    )
    wqkv = weights[0].reshape(width, 2, 4 * third)[:, :, : 3 * third].reshape(width, 3 * width)

    bounds, row_info, key_info = attention_plan(
        segment_ids, pad_mask, random_blocks, global_blocks, rows
    )
    qkv = (nn(layer_in, wqkv) + bqkv).astype(BF)
    other = swap_keys(qkv)
    attn, logs = attend_forward(bounds, qkv, other, row_info, key_info)
    (layer_out, grad_first, grad_attn, norm_low, hidden, ffn_grad, unit_grad, proj_grad, sums, unit_sums) = middle(
        layer_in, attn, output_grad, weights, vectors, unit_bias
    )
    d_out_t = tn(ffn_grad, hidden).astype(BF)
    d_in = tn(norm_low, unit_grad).astype(BF)
    d_o_t = tn(proj_grad, attn).astype(BF)
    dq, dkv = attend_backward(bounds, qkv, other, row_info, key_info, attn, logs, grad_attn)
    both = dkv.reshape(2, rows, 2 * width)
    far = swap_pair(both)
    near = lax.dynamic_index_in_dim(both, half, 0, False)
    dkv_own = (near.astype(F32) + far.astype(F32)).astype(BF)
    d_qkv = jnp.concatenate(
        [dq[:, :third], dkv_own[:, :width], dq[:, third:], dkv_own[:, width:]], axis=1
    )
    d_bqkv = jnp.sum(d_qkv.astype(F32), axis=0).reshape(2, 3, third)
    d_wqkv = tn(layer_in, d_qkv).astype(BF)
    input_grad = grad_first + nt(d_qkv, wqkv)

    sums = jnp.concatenate(
        [d_bqkv[:, 0].reshape(1, width), d_bqkv[:, 2].reshape(1, width), sums[2:]], axis=0
    )
    d_small = jnp.concatenate(
        [
            sums.reshape(8, dp * tp, one).transpose(1, 0, 2).reshape(dp * tp, eight),
            unit_sums[0].reshape(dp * tp, used - eight),
            jnp.zeros((dp * tp, room - used), F32),
        ],
        axis=1,
    ).reshape(dp, tp, room // 128, 128)
    total, total_small = reduce_grads(d_wqkv, d_o_t, d_in, d_out_t, d_small)

    def own(k, first, wide):
        return lax.dynamic_slice_in_dim(total[k], first + half * wide, wide, axis=1)

    parts = total_small.reshape(room)
    (r_bq, r_bv, r_bo, r_bout, r_g1, r_s1, r_g2, r_s2) = (
        parts[i * one : (i + 1) * one] for i in range(8)
    )
    return (
        layer_out,
        input_grad,
        own(0, 0, own_cols),
        own(0, third, own_cols),
        own(0, 2 * third, own_cols),
        own(0, 3 * third, own_cols).T,
        own(1, 0, own_units),
        own(2, 0, own_units).T,
        r_bq, r_bv, r_bo, parts[eight:used], r_bout, r_g1, r_s1, r_g2, r_s2,
    )


def solution(mesh):
    tokens = P(("dp", "tensor"), None)
    vector = P(("dp", "tensor"))
    cols, turned = P("dp", "tensor"), P("tensor", "dp")
    return jax.shard_map(
        on_device,
        mesh=mesh,
        in_specs=(tokens, cols, cols, cols, turned, cols, turned)
        + (vector,) * 9
        + (P("dp"), P("dp"), P("dp", None, None), P("dp", None, None), tokens),
        out_specs=(tokens, tokens, cols, cols, cols, turned, cols, turned) + (vector,) * 9,
        check_vma=False,
    )
```

```python
from functools import partial

import jax
import jax.numpy as jnp
from jax import lax
from jax.experimental import pallas as pl
from jax.experimental.pallas import tpu as pltpu
from jax.sharding import PartitionSpec as P

HD = 64
PAIR = 2 * HD
QT = 256
KT = 128
ROWS = 256
EPSILON = 1e-06
NEGATIVE = -1e30
MESH = pl.DeviceIdType.MESH
VMEM_LIMIT = 56 * 2**20
BF = jnp.bfloat16
F32 = jnp.float32


def params_of(collective_id=None):
    if collective_id is None:
        return pltpu.CompilerParams(vmem_limit_bytes=VMEM_LIMIT)
    return pltpu.CompilerParams(
        vmem_limit_bytes=VMEM_LIMIT, collective_id=collective_id, has_side_effects=True
    )


def nt(left, right, **more):
    return lax.dot_general(
        left, right, (((1,), (1,)), ((), ())), preferred_element_type=F32, **more
    )


def nn(left, right):
    return lax.dot_general(left, right, (((1,), (0,)), ((), ())), preferred_element_type=F32)


def tn(left, right):
    return lax.dot_general(left, right, (((0,), (0,)), ((), ())), preferred_element_type=F32)


def sibling_of():
    rank = lax.axis_index("tensor")
    half = lax.rem(rank, 2)
    return half, {"tensor": rank + 1 - 2 * half}


def meet(others):
    barrier = pltpu.get_barrier_semaphore()
    for other in others:
        pl.semaphore_signal(barrier, inc=1, device_id=other, device_id_type=MESH)
    pl.semaphore_wait(barrier, len(others))


def swap_keys_kernel(qkv_ref, other_ref, send_sem, recv_sem):
    half, sibling = sibling_of()
    meet([sibling])
    third = qkv_ref.shape[1] // 6
    moves = [
        pltpu.make_async_remote_copy(
            qkv_ref.at[:, (3 * y + 1) * third : (3 * y + 3) * third],
            other_ref.at[:, 2 * y * third : 2 * (y + 1) * third],
            send_sem.at[y], recv_sem.at[y], device_id=sibling, device_id_type=MESH,
        )
        for y in range(2)
    ]
    for move in moves:
        move.start()
    for move in moves:
        move.wait()


def swap_keys(qkv):
    rows, width = qkv.shape
    return pl.pallas_call(
        swap_keys_kernel,
        name="swap_keys",
        out_shape=jax.ShapeDtypeStruct((rows, width * 2 // 3), qkv.dtype),
        in_specs=[pl.BlockSpec(memory_space=pl.ANY)],
        out_specs=pl.BlockSpec(memory_space=pl.ANY),
        scratch_shapes=[pltpu.SemaphoreType.DMA((2,))] * 2,
        compiler_params=params_of(1),
    )(qkv)


def swap_pair_kernel(both_ref, other_ref, send_sem, recv_sem):
    half, sibling = sibling_of()
    meet([sibling])
    away = pltpu.make_async_remote_copy(
        both_ref.at[1 - half], other_ref, send_sem, recv_sem,
        device_id=sibling, device_id_type=MESH,
    )
    away.start()
    away.wait()


def swap_pair(both):
    return pl.pallas_call(
        swap_pair_kernel,
        name="swap_pair",
        out_shape=jax.ShapeDtypeStruct(both.shape[1:], both.dtype),
        in_specs=[pl.BlockSpec(memory_space=pl.ANY)],
        out_specs=pl.BlockSpec(memory_space=pl.ANY),
        scratch_shapes=[pltpu.SemaphoreType.DMA(())] * 2,
        compiler_params=params_of(2),
    )(both)


def places():
    dp, rank = lax.axis_index("dp"), lax.axis_index("tensor")
    core, y = lax.rem(rank, 2), rank // 2
    z, x = dp // 2, lax.rem(dp, 2)
    sibling = {"dp": dp, "tensor": rank + 1 - 2 * core}
    near_x = {"dp": dp + 1 - 2 * x, "tensor": rank}
    near_y = {"dp": dp, "tensor": rank + 2 - 4 * y}
    first = {"dp": dp + (1 - core) * (1 - 2 * x), "tensor": rank + core * (2 - 4 * y)}
    second = {"dp": dp + core * (1 - 2 * x), "tensor": rank + (1 - core) * (2 - 4 * y)}
    xa, ya = x + (1 - core) * (1 - 2 * x), y + core * (1 - 2 * y)
    xb, yb = x + core * (1 - 2 * x), y + (1 - core) * (1 - 2 * y)
    return dict(dp=dp, rank=rank, core=core, y=y, z=z, x=x, sibling=sibling, first=first, second=second,
                xa=xa, ya=ya, xb=xb, yb=yb)


def line_jumps(dp, rank, z, n):
    jumps, hop = [], 1
    while hop < n:
        bit = lax.rem(z // hop, 2)
        jumps.append({"dp": dp + 2 * hop * (1 - 2 * bit), "tensor": rank})
        hop *= 2
    return jumps


def start_kernel(
    n, mine_ref, vec_ref, x_ref, w_hbm, qkv_hbm, other_hbm, vec_out,
    out_ref, chip, sib, qkv, vec_sent, vec_got,
    local_sem, pair_sem, zs, zr, as_, ar, bs, br, ss, sr, ks, kr, vs, vr,
):
    w = places()
    dp, rank, core, y, z, x = (w[k] for k in ("dp", "rank", "core", "y", "z", "x"))
    block, wide = mine_ref.shape[1], mine_ref.shape[2]
    slab = block // 2
    up, down = {"dp": lax.rem(dp + 2, 2 * n), "tensor": rank}, {"dp": lax.rem(dp + 2 * n - 2, 2 * n), "tensor": rank}
    partners = [w["sibling"], w["second"], w["first"]] + line_jumps(dp, rank, z, n)
    meet([up, down] + partners)

    pair = pltpu.make_async_remote_copy(mine_ref, sib, pair_sem.at[0], pair_sem.at[1], device_id=w["sibling"], device_id_type=MESH)
    pair.start()

    def small_send(step):
        return pltpu.make_async_remote_copy(vec_sent.at[step], vec_got.at[step], vs.at[step], vr.at[step], device_id=partners[step], device_id_type=MESH)

    def small_step(step):
        small_send(step).wait_recv()
        vec_sent[step + 1] = vec_sent[step] + vec_got[step]
        if step + 1 < len(partners):
            small_send(step + 1).start()

    vec_sent[0] = vec_ref[...]
    small_send(0).start()
    pair.wait()
    chip[...] = mine_ref[...] + sib[...]
    rows_own = pl.ds(pl.multiple_of(core * slab, slab), slab)
    own_at = pl.ds(pl.multiple_of(dp * block, block), block)
    cols_own = pl.ds(pl.multiple_of(y * wide, wide), wide)
    keep = pltpu.make_async_copy(chip, out_ref.at[:, own_at, cols_own], local_sem.at[0])
    keep.start()

    def spot(g, zi, xi, yi):
        d = zi * 2 + xi
        rows = pl.ds(pl.multiple_of(d * block + core * slab, slab), slab)
        cols = pl.ds(pl.multiple_of(yi * wide, wide), wide)
        return out_ref.at[:, rows, cols]

    def own(g):
        return chip.at[:, rows_own, :]

    def move(g, zi, xi, yi, dev, ssem, rsem, source=None):
        at = spot(g, zi, xi, yi)
        return pltpu.make_async_remote_copy(at if source is None else source, at, ssem, rsem, device_id=dev, device_id_type=MESH)

    def line_up(g, s):
        return move(g, z - s, x, y, up, zs.at[g, 0, s], zr.at[g, 0, s], own(g) if s == 0 else None)

    def line_down(g, s):
        return move(g, z + s, x, y, down, zs.at[g, 1, s], zr.at[g, 1, s], own(g) if s == 0 else None)

    def to_first(g, zi, source=None):
        return move(g, zi, x, y, w["first"], as_.at[g, zi], ar.at[g, zi], source)

    def to_second(g, zi, far, source=None):
        xi, yi = (w["xa"], w["ya"]) if far else (x, y)
        return move(g, zi, xi, yi, w["second"], bs.at[g, far, zi], br.at[g, far, zi], source)

    def to_sibling(g, zi, quarter, source=None):
        xi = (x, w["xa"], w["xb"], w["xa"] + w["xb"] - x)[quarter]
        yi = (y, w["ya"], w["yb"], w["ya"] + w["yb"] - y)[quarter]
        return move(g, zi, xi, yi, w["sibling"], ss.at[g, quarter, zi], sr.at[g, quarter, zi], source)

    def begin(g):
        @pl.when(z < n - 1)
        def _():
            line_up(g, 0).start()

        @pl.when(z > 0)
        def _():
            line_down(g, 0).start()

        to_first(g, z, own(g)).start()
        to_second(g, z, 0, own(g)).start()

    def first_in(g, zi):
        got = move(g, zi, w["xa"], w["ya"], w["first"], as_.at[g, zi], ar.at[g, zi])
        got.wait_recv()
        to_second(g, zi, 1).start()
        to_sibling(g, zi, 1).start()

    def second_in(g, zi, far):
        q = 2 + far
        xi = (w["xb"], w["xa"] + w["xb"] - x)[far]
        yi = (w["yb"], w["ya"] + w["yb"] - y)[far]
        move(g, zi, xi, yi, w["second"], bs.at[g, far, zi], br.at[g, far, zi]).wait_recv()
        to_sibling(g, zi, q).start()

    def below_in(g, s):
        zi = z - 1 - s
        move(g, zi, x, y, up, zs.at[g, 0, s], zr.at[g, 0, s]).wait_recv()
        if s + 1 < n - 1:
            @pl.when(z < n - 1)
            def _():
                line_up(g, s + 1).start()
        to_first(g, zi).start()
        to_second(g, zi, 0).start()
        to_sibling(g, zi, 0).start()

    def above_in(g, s):
        zi = z + 1 + s
        move(g, zi, x, y, down, zs.at[g, 1, s], zr.at[g, 1, s]).wait_recv()
        if s + 1 < n - 1:
            @pl.when(z > 0)
            def _():
                line_down(g, s + 1).start()
        to_first(g, zi).start()
        to_second(g, zi, 0).start()
        to_sibling(g, zi, 0).start()

    def steps(gs):
        for g in gs:
            first_in(g, z)
        for s in range(n - 1):
            @pl.when(z - 1 - s >= 0)
            def _(s=s):
                for g in gs:
                    below_in(g, s)

            @pl.when(z + 1 + s < n)
            def _(s=s):
                for g in gs:
                    above_in(g, s)
            if s > 0:
                both(s, lambda g, zi: first_in(g, zi), gs)
        both(n - 1, lambda g, zi: first_in(g, zi), gs)
        for g in gs:
            second_in(g, z, 0)
        for g in gs:
            second_in(g, z, 1)
        for s in range(1, n):
            both(s, lambda g, zi: second_in(g, zi, 0), gs)
            both(s, lambda g, zi: second_in(g, zi, 1), gs)

    def both(s, what, gs):
        @pl.when(z - s >= 0)
        def _():
            for g in gs:
                what(g, z - s)

        @pl.when(z + s < n)
        def _():
            for g in gs:
                what(g, z + s)

    begin(0)
    small_step(0)
    steps((0,))
    for step in range(1, len(partners)):
        small_step(step)

    keep.wait()
    for zi in range(n):
        for q in range(1, 4):
            to_sibling(0, zi, q).wait_recv()

        @pl.when(zi != z)
        def _(zi=zi):
            to_sibling(0, zi, 0).wait_recv()
    save_w = pltpu.make_async_copy(out_ref, w_hbm, local_sem.at[1])
    save_w.start()

    rows, width = x_ref.shape
    third = width // 2
    vec_out[...] = vec_sent[len(partners)]
    tiles = rows // ROWS

    def keys_of(t, yi):
        at = (pl.ds(pl.multiple_of(t * ROWS, ROWS), ROWS), slice((3 * yi + 1) * third, (3 * yi + 3) * third))
        far = (at[0], slice(2 * yi * third, 2 * (yi + 1) * third))
        return pltpu.make_async_remote_copy(qkv.at[at], other_hbm.at[far], ks.at[t, yi], kr.at[t, yi], device_id=w["sibling"], device_id_type=MESH)

    @pl.loop(0, tiles)
    def _(t):
        at = pl.ds(pl.multiple_of(t * ROWS, ROWS), ROWS)
        for yi in range(2):
            both = nn(x_ref[at, :], out_ref[0, :, yi * wide + third : yi * wide + 3 * third])
            first = (3 * yi + 1) * third
            qkv[at, first : first + third] = both[:, :third].astype(BF)
            bias = vec_out[1:2, yi * third : (yi + 1) * third]
            qkv[at, first + third : first + 2 * third] = (both[:, third:] + bias).astype(BF)
            keys_of(t, yi).start()

    @pl.loop(0, tiles)
    def _(t):
        at = pl.ds(pl.multiple_of(t * ROWS, ROWS), ROWS)
        for yi in range(2):
            bias = vec_out[0:1, yi * third : (yi + 1) * third]
            mine = nn(x_ref[at, :], out_ref[0, :, yi * wide : yi * wide + third]) + bias
            qkv[at, 3 * yi * third : (3 * yi + 1) * third] = mine.astype(BF)

    save_qkv = pltpu.make_async_copy(qkv, qkv_hbm, local_sem.at[2])
    save_qkv.start()
    for g in (0,):
        @pl.when(z < n - 1)
        def _(g=g):
            line_up(g, 0).wait_send()

        @pl.when(z > 0)
        def _(g=g):
            line_down(g, 0).wait_send()
        for s in range(1, n - 1):
            @pl.when((z < n - 1) & (z - s >= 0))
            def _(g=g, s=s):
                line_up(g, s).wait_send()

            @pl.when((z > 0) & (z + s < n))
            def _(g=g, s=s):
                line_down(g, s).wait_send()
        for zi in range(n):
            to_first(g, zi).wait_send()
            for far in range(2):
                to_second(g, zi, far).wait_send()
            for q in range(1, 4):
                to_sibling(g, zi, q).wait_send()
        for zi in range(n):
            @pl.when(zi != z)
            def _(g=g, zi=zi):
                to_sibling(g, zi, 0).wait_send()


    for step in range(len(partners)):
        small_send(step).wait_send()

    @pl.loop(0, tiles)
    def _(t):
        for yi in range(2):
            keys_of(t, yi).wait()
    save_w.wait()
    save_qkv.wait()


def start(mine, vec, layer_in):
    dp, tp = lax.axis_size("dp"), lax.axis_size("tensor")
    n = dp // 2
    parts, block, wide = mine.shape
    rows, width = layer_in.shape
    steps = 3 + (n - 1).bit_length()
    tiles = rows // ROWS
    dma = pltpu.SemaphoreType.DMA
    anywhere, inside = pl.BlockSpec(memory_space=pl.ANY), pl.BlockSpec(memory_space=pltpu.VMEM)
    whole = (parts, dp * block, wide * tp // 2)
    return pl.pallas_call(
        partial(start_kernel, n),
        name="start",
        in_specs=[inside] * 3,
        out_specs=[anywhere] * 3 + [inside],
        out_shape=[
            jax.ShapeDtypeStruct(whole, BF),
            jax.ShapeDtypeStruct((rows, 3 * width), BF),
            jax.ShapeDtypeStruct((rows, 2 * width), BF),
            jax.ShapeDtypeStruct(vec.shape, F32),
        ],
        scratch_shapes=[
            pltpu.VMEM(whole, BF), pltpu.VMEM(mine.shape, BF), pltpu.VMEM(mine.shape, BF),
            pltpu.VMEM((rows, 3 * width), BF),
            pltpu.VMEM((steps + 1,) + vec.shape, F32), pltpu.VMEM((steps,) + vec.shape, F32),
            dma((3,)), dma((2,)), dma((1, 2, n)), dma((1, 2, n)), dma((1, n)), dma((1, n)),
            dma((1, 2, n)), dma((1, 2, n)), dma((1, 4, n)), dma((1, 4, n)), dma((tiles, 2)), dma((tiles, 2)),
            dma((steps,)), dma((steps,)),
        ],
        compiler_params=params_of(3),
    )(mine, vec, layer_in)


def in_tiles(block):
    return block % 32 == 0


def start_plainly(mine, vec, layer_in):
    dp, tp = lax.axis_size("dp"), lax.axis_size("tensor")
    parts, block, wide = mine.shape
    width = layer_in.shape[1]
    third = width // 2
    every = lax.all_gather(mine, ("dp", "tensor"), axis=0, tiled=False)
    every = every.reshape(dp, tp // 2, 2, parts, block, wide).sum(axis=2)
    weights = every.transpose(2, 0, 3, 1, 4).reshape(parts, dp * block, tp // 2 * wide)
    vec = lax.psum(vec, ("dp", "tensor"))
    zero = jnp.zeros((1, third), F32)
    bias = jnp.concatenate(
        [v for y in range(2) for v in (vec[:1, y * third : (y + 1) * third], zero,
                                       vec[1:2, y * third : (y + 1) * third])], axis=1,
    )
    wqkv = weights[0].reshape(width, 2, 4 * third)[:, :, : 3 * third].reshape(width, 3 * width)
    qkv = (nn(layer_in, wqkv) + bias).astype(BF)
    return weights, qkv, swap_keys(qkv), vec


def q_lanes(p, pairs):
    third = pairs // 2 * PAIR
    first = p // (pairs // 2) * 3 * third + p % (pairs // 2) * PAIR
    return slice(first, first + PAIR)


def k_lanes(p, pairs):
    third = pairs // 2 * PAIR
    first = p // (pairs // 2) * 2 * third + p % (pairs // 2) * PAIR
    return slice(first, first + PAIR)


def v_lanes(p, pairs):
    third = pairs // 2 * PAIR
    lanes = k_lanes(p, pairs)
    return slice(lanes.start + third, lanes.stop + third)


def fetch_keys(qkv_ref, other_ref, kv, sems):
    rows, third = other_ref.shape[0], other_ref.shape[1] // 4
    half = lax.rem(lax.axis_index("tensor"), 2)
    here = pl.ds(pl.multiple_of(half * rows, rows), rows)
    there = pl.ds(pl.multiple_of((1 - half) * rows, rows), rows)
    moves = [pltpu.make_async_copy(other_ref, kv.at[there, :], sems.at[2])]
    for y in range(2):
        moves.append(
            pltpu.make_async_copy(
                qkv_ref.at[:, (3 * y + 1) * third : (3 * y + 3) * third],
                kv.at[here, 2 * y * third : 2 * (y + 1) * third],
                sems.at[y],
            )
        )
    for move in moves:
        move.start()
    for move in moves:
        move.wait()


def masked_pairs(source, target, lanes_of, pairs, scale):
    rows = source.shape[0]
    low_lanes = lax.broadcasted_iota(jnp.int32, (rows, PAIR), 1) < HD
    for p in range(pairs):
        both = source[:, lanes_of(p)]
        if scale is not None:
            both = both * jnp.asarray(scale, both.dtype)
        zero = jnp.zeros_like(both)
        target[p, :rows, :] = jnp.where(low_lanes, both, zero)
        target[p, rows:, :] = jnp.where(low_lanes, zero, both)


def tile_bias(j, q_first, row_info, key_info, bias):
    seg_q, bits_q = row_info[0:1, :], row_info[1:2, :]
    queries = bias.shape[1]
    for part in range(KT // HD):
        block = j * (KT // HD) + part
        bit = jnp.bitwise_and(
            lax.shift_right_logical(bits_q, jnp.full_like(bits_q, block)), 1
        )
        wanted = jnp.where(bit == 1, seg_q, -1)
        base = pl.multiple_of(j * KT + part * HD, HD)
        seg_k = key_info[pl.ds(base, HD), :]
        key_at = base + lax.broadcasted_iota(jnp.int32, (HD, queries), 0)
        query_at = q_first + lax.broadcasted_iota(jnp.int32, (HD, queries), 1)
        allowed = (seg_k == wanted) | (key_at == query_at)
        bias[part * HD : (part + 1) * HD, :] = jnp.where(allowed, 0.0, NEGATIVE)


def attend_forward_kernel(
    bounds, q_ref, qkv_ref, other_ref, row_info, key_info, out_ref, log_ref,
    q_pairs, kv_ref, v_turned, bias, top, total, acc, sems,
):
    step = pl.program_id(0)
    rows, width = out_ref.shape
    pairs = width // PAIR
    tiles = kv_ref.shape[0] // KT

    @pl.when(step == 0)
    def _():
        fetch_keys(qkv_ref, other_ref, kv_ref, sems)
        for j in range(tiles):
            for p in range(pairs):
                span = slice(p * PAIR, (p + 1) * PAIR)
                v_turned[j, span, :] = kv_ref[j * KT : (j + 1) * KT, v_lanes(p, pairs)].T

    masked_pairs(q_ref, q_pairs, partial(q_lanes, pairs=pairs), pairs, HD**-0.5)
    top[...] = jnp.full_like(top, NEGATIVE)
    total[...] = jnp.zeros_like(total)
    acc[...] = jnp.zeros_like(acc)
    q_first = bounds[step, 2]

    @pl.loop(bounds[step, 0], bounds[step, 1])
    def _(j):
        tile_bias(j, q_first, row_info, key_info, bias)
        keys_at = pl.multiple_of(j * KT, KT)
        for p in range(pairs):
            keys = kv_ref[pl.ds(keys_at, KT), k_lanes(p, pairs)]
            scores = nt(keys, q_pairs[p])
            for e in range(2):
                h = 2 * p + e
                mine = scores[:, e * rows : (e + 1) * rows] + bias[...]
                before = top[h : h + 1, :]
                now = jnp.maximum(before, jnp.max(mine, axis=0, keepdims=True))
                fade = jnp.exp(before - now)
                expos = jnp.exp(mine - now)
                top[h : h + 1, :] = now
                total[h : h + 1, :] = fade * total[h : h + 1, :] + jnp.sum(
                    expos, axis=0, keepdims=True
                )
                span = slice(h * HD, (h + 1) * HD)
                acc[span, :] = acc[span, :] * fade + nn(v_turned[j, span, :], expos.astype(BF))

    heads = width // HD
    for h in range(heads):
        span = slice(h * HD, (h + 1) * HD)
        acc[span, :] = acc[span, :] / total[h : h + 1, :]
    out_ref[...] = acc[...].T.astype(BF)
    log_ref[...] = top[...] + jnp.log(jnp.maximum(total[...], 1e-37))


def attend_forward(bounds, qkv, other, row_info, key_info):
    rows, width = qkv.shape[0], qkv.shape[1] // 3
    keys = 2 * rows
    stat_rows = 16
    return pl.pallas_call(
        attend_forward_kernel,
        name="attend_forward",
        grid_spec=pltpu.PrefetchScalarGridSpec(
            num_scalar_prefetch=1,
            grid=(rows // QT,),
            in_specs=[
                pl.BlockSpec((QT, 3 * width), lambda i, b: (i, 0)),
                pl.BlockSpec(memory_space=pl.ANY),
                pl.BlockSpec(memory_space=pl.ANY),
                pl.BlockSpec((8, QT), lambda i, b: (0, i)),
                pl.BlockSpec((keys, 1), lambda i, b: (0, 0), pipeline_mode=pl.Buffered(1)),
            ],
            out_specs=[
                pl.BlockSpec((QT, width), lambda i, b: (i, 0)),
                pl.BlockSpec((stat_rows, QT), lambda i, b: (0, i)),
            ],
            scratch_shapes=[
                pltpu.VMEM((width // PAIR, 2 * QT, PAIR), BF),
                pltpu.VMEM((keys, 2 * width), BF),
                pltpu.VMEM((keys // KT, width, KT), BF),
                pltpu.VMEM((KT, QT), F32),
                pltpu.VMEM((stat_rows, QT), F32),
                pltpu.VMEM((stat_rows, QT), F32),
                pltpu.VMEM((width, QT), F32),
                pltpu.SemaphoreType.DMA((3,)),
            ],
        ),
        out_shape=[
            jax.ShapeDtypeStruct((rows, width), BF),
            jax.ShapeDtypeStruct((stat_rows, rows), F32),
        ],
        compiler_params=params_of(),
    )(bounds, qkv, qkv, other, row_info, key_info)


def attend_backward_kernel(
    bounds, q_ref, qkv_ref, other_ref, row_info, key_info, out_ref, log_ref, grad_ref,
    dq_ref, dkv_ref, q_pairs, g_pairs, kv_ref, k_turned, bias, inner, dq_acc, dkv_acc, sems,
):
    step = pl.program_id(0)
    rows, width = out_ref.shape
    pairs = width // PAIR
    tiles = kv_ref.shape[0] // KT

    @pl.when(step == 0)
    def _():
        fetch_keys(qkv_ref, other_ref, kv_ref, sems)
        for j in range(tiles):
            for p in range(pairs):
                span = slice(p * PAIR, (p + 1) * PAIR)
                k_turned[j, span, :] = kv_ref[j * KT : (j + 1) * KT, k_lanes(p, pairs)].T
        dkv_acc[...] = jnp.zeros_like(dkv_acc)

    masked_pairs(q_ref, q_pairs, partial(q_lanes, pairs=pairs), pairs, HD**-0.5)
    masked_pairs(grad_ref, g_pairs, lambda p: slice(p * PAIR, (p + 1) * PAIR), pairs, None)
    head_of = lax.broadcasted_iota(jnp.int32, (inner.shape[0], width), 1) // HD
    row_of = lax.broadcasted_iota(jnp.int32, (inner.shape[0], width), 0)
    chosen = jnp.where(head_of == row_of, 1.0, 0.0)
    product = out_ref[...].astype(F32) * grad_ref[...].astype(F32)
    inner[...] = nt(chosen, product, precision=lax.Precision.HIGHEST)
    dq_acc[...] = jnp.zeros_like(dq_acc)
    q_first = bounds[step, 2]

    @pl.loop(bounds[step, 0], bounds[step, 1])
    def _(j):
        tile_bias(j, q_first, row_info, key_info, bias)
        here = pl.ds(pl.multiple_of(j * KT, KT), KT)
        for p in range(pairs):
            k_here, v_here = k_lanes(p, pairs), v_lanes(p, pairs)
            scores = nt(kv_ref[here, k_here], q_pairs[p])
            grad_probs = nt(kv_ref[here, v_here], g_pairs[p])
            probs, grads = [], []
            for e in range(2):
                h = 2 * p + e
                cols = slice(e * rows, (e + 1) * rows)
                prob = jnp.exp(scores[:, cols] + bias[...] - log_ref[h : h + 1, :])
                grad = (prob * (grad_probs[:, cols] - inner[h : h + 1, :])).astype(BF)
                probs.append(prob.astype(BF))
                grads.append(grad)
                span = slice(h * HD, (h + 1) * HD)
                dq_acc[span, :] += nn(k_turned[j, span, :], grad)
            dkv_acc[here, k_here] += nn(jnp.concatenate(grads, axis=1), q_pairs[p])
            dkv_acc[here, v_here] += nn(jnp.concatenate(probs, axis=1), g_pairs[p])

    dq_ref[...] = (dq_acc[...] * HD**-0.5).T.astype(BF)

    @pl.when(step == pl.num_programs(0) - 1)
    def _():
        dkv_ref[...] = dkv_acc[...].astype(BF)


def attend_backward(bounds, qkv, other, row_info, key_info, attn, logs, grad_attn):
    rows, width = attn.shape
    keys = 2 * rows
    stat_rows = logs.shape[0]
    whole = dict(pipeline_mode=pl.Buffered(1))
    return pl.pallas_call(
        attend_backward_kernel,
        name="attend_backward",
        grid_spec=pltpu.PrefetchScalarGridSpec(
            num_scalar_prefetch=1,
            grid=(rows // QT,),
            in_specs=[
                pl.BlockSpec((QT, 3 * width), lambda i, b: (i, 0)),
                pl.BlockSpec(memory_space=pl.ANY),
                pl.BlockSpec(memory_space=pl.ANY),
                pl.BlockSpec((8, QT), lambda i, b: (0, i)),
                pl.BlockSpec((keys, 1), lambda i, b: (0, 0), **whole),
                pl.BlockSpec((QT, width), lambda i, b: (i, 0)),
                pl.BlockSpec((stat_rows, QT), lambda i, b: (0, i)),
                pl.BlockSpec((QT, width), lambda i, b: (i, 0)),
            ],
            out_specs=[
                pl.BlockSpec((QT, width), lambda i, b: (i, 0)),
                pl.BlockSpec((keys, 2 * width), lambda i, b: (0, 0), **whole),
            ],
            scratch_shapes=[
                pltpu.VMEM((width // PAIR, 2 * QT, PAIR), BF),
                pltpu.VMEM((width // PAIR, 2 * QT, PAIR), BF),
                pltpu.VMEM((keys, 2 * width), BF),
                pltpu.VMEM((keys // KT, width, KT), BF),
                pltpu.VMEM((KT, QT), F32),
                pltpu.VMEM((stat_rows, QT), F32),
                pltpu.VMEM((width, QT), F32),
                pltpu.VMEM((keys, 2 * width), F32),
                pltpu.SemaphoreType.DMA((3,)),
            ],
        ),
        out_shape=[
            jax.ShapeDtypeStruct((rows, width), BF),
            jax.ShapeDtypeStruct((keys, 2 * width), BF),
        ],
        compiler_params=params_of(),
    )(bounds, qkv, qkv, other, row_info, key_info, attn, logs, grad_attn)


def attention_plan(segment_ids, pad_mask, random_blocks, global_blocks, rows):
    seq_count, nblocks = random_blocks.shape[0], random_blocks.shape[1]
    seq_len = segment_ids.shape[0] // seq_count
    rank = lax.axis_index("tensor")
    seq, half = rank // 2, lax.rem(rank, 2)
    segs = lax.dynamic_index_in_dim(segment_ids.reshape(seq_count, seq_len), seq, 0, False)
    pads = lax.dynamic_index_in_dim(pad_mask.reshape(seq_count, seq_len), seq, 0, False)
    randoms = lax.dynamic_index_in_dim(random_blocks, seq, 0, False)
    globs = lax.dynamic_index_in_dim(global_blocks, seq, 0, False)
    block_size = seq_len // nblocks
    one = jnp.int32(1)
    block = jnp.arange(nblocks, dtype=jnp.int32)

    def either(a, b):
        return jnp.bitwise_or(a, b)

    block_bits = lax.shift_left(one, block)
    window = either(
        block_bits,
        either(
            jnp.where(block > 0, lax.shift_left(one, jnp.maximum(block - 1, 0)), 0),
            jnp.where(
                block < nblocks - 1, lax.shift_left(one, jnp.minimum(block + 1, nblocks - 1)), 0
            ),
        ),
    )
    for r in range(randoms.shape[1]):
        window = either(window, lax.shift_left(one, randoms[:, r]))
    glob_bits = either(lax.shift_left(one, globs[:, 0]), lax.shift_left(one, globs[:, 1]))
    first = half * rows
    seg_q = lax.dynamic_slice_in_dim(segs, first, rows)
    own_bits = lax.dynamic_slice_in_dim(window, half * (rows // block_size), rows // block_size)
    bits = jnp.broadcast_to(own_bits[:, None], (rows // block_size, block_size)).reshape(rows)
    numbers = jnp.arange(globs.shape[0], dtype=jnp.int32)
    is_doc = seg_q[None, :] == numbers[:, None]
    bits = either(bits, jnp.sum(jnp.where(is_doc, glob_bits[:, None], 0), axis=0))
    row_info = jnp.concatenate(
        [seg_q[None], bits[None], jnp.zeros((6, rows), jnp.int32)], axis=0
    )
    key_info = jnp.where(pads == 1, segs, -2)[:, None]
    tiles = seg_q.reshape(rows // QT, QT)
    low = jnp.sum((segs[None, :] < tiles[:, :1]).astype(jnp.int32), axis=1)
    high = jnp.sum((segs[None, :] <= tiles[:, -1:]).astype(jnp.int32), axis=1)
    starts = first + QT * jnp.arange(rows // QT, dtype=jnp.int32)
    bounds = jnp.stack([low // KT, (high + KT - 1) // KT, starts, starts], axis=1)
    return bounds, row_info, key_info


TAIL_STEP = 0.47
TAIL = (0.266306628, 0.248031891, 0.336199252, -0.126105651, 0.607561554, -0.420410983, 0.0884173167)


def gelu_and_slope(pre):
    bell = jnp.exp(-0.5 * pre * pre)
    t = 1.0 / (1.0 + (TAIL_STEP * 0.5**0.5) * jnp.abs(pre))
    tail = TAIL[-1]
    for c in TAIL[-2::-1]:
        tail = tail * t + c
    tail = 0.5 * (tail * t) * bell
    cdf = jnp.where(pre < 0, tail, 1.0 - tail)
    return pre * cdf, cdf + pre * (bell * (2.0 * 3.141592653589793) ** -0.5)


def normalize(resid):
    center = resid - jnp.mean(resid, axis=1, keepdims=True)
    inverse = lax.rsqrt(jnp.mean(center * center, axis=1, keepdims=True) + EPSILON)
    return center * inverse, inverse


def norm_backward(grad_normed, normal_hat, inverse, gain):
    grad_hat = grad_normed * gain
    return inverse * (
        grad_hat
        - jnp.mean(grad_hat, axis=1, keepdims=True)
        - normal_hat * jnp.mean(grad_hat * normal_hat, axis=1, keepdims=True)
    )


def middle_kernel(
    x_ref, attn_ref, cot_ref, w_ref, blocks_ref, vec_ref,
    final_ref, first_grad, attn_grad, norm_low, unit_grad, proj_grad, out_grad,
    sums, unit_sums, slope, hidden, outer,
):
    width = x_ref.shape[1]
    third = width // 2
    wide = w_ref.shape[2] // 2
    proj_cols = [slice((y + 1) * wide - third, (y + 1) * wide) for y in range(2)]
    halves = [slice(y * third, (y + 1) * third) for y in range(2)]
    own_units = blocks_ref.shape[3] // 2
    chunks = [(t, slice(t * own_units, (t + 1) * own_units)) for t in range(blocks_ref.shape[1])]

    def w_in(t):
        return blocks_ref[:, t, :, :own_units].reshape(width, own_units)

    def w_out(t):
        return blocks_ref[:, t, :, own_units:].reshape(width, own_units)

    out_bias, last_bias, gain_1, shift_1, gain_2, shift_2 = (vec_ref[i : i + 1, :] for i in range(2, 8))

    @pl.when(pl.program_id(0) == 0)
    def _():
        sums[...] = jnp.zeros_like(sums)
        unit_sums[...] = jnp.zeros_like(unit_sums)
        outer[...] = jnp.zeros_like(outer)

    resid = x_ref[...].astype(F32) + out_bias
    for y in range(2):
        resid += nt(attn_ref[:, halves[y]], w_ref[0, :, proj_cols[y]])
    hat_1, inverse_1 = normalize(resid)
    first_norm = hat_1 * gain_1 + shift_1
    low = first_norm.astype(BF)
    norm_low[...] = low
    resid = first_norm + last_bias
    for t, cols in chunks:
        act, slope[:, cols] = gelu_and_slope(nn(low, w_in(t)) + vec_ref[8 + t : 9 + t, :own_units])
        act = act.astype(BF)
        hidden[:, cols] = act
        resid += nt(act, w_out(t))
    hat_2, inverse_2 = normalize(resid)
    final_ref[...] = (hat_2 * gain_2 + shift_2).astype(BF)

    cot = cot_ref[...].astype(F32)
    grad = norm_backward(cot, hat_2, inverse_2, gain_2)
    sums[6:7, :] += jnp.sum(cot * hat_2, axis=0, keepdims=True)
    sums[7:8, :] += jnp.sum(cot, axis=0, keepdims=True)
    sums[3:4, :] += jnp.sum(grad, axis=0, keepdims=True)
    low = grad.astype(BF)
    turned = low.T
    for t, cols in chunks:
        outer[t] += nn(turned, hidden[:, cols])
        act = (nn(low, w_out(t)) * slope[:, cols]).astype(BF)
        unit_grad[:, cols] = act
        unit_sums[0:1, cols] += jnp.sum(act.astype(F32), axis=0, keepdims=True)
        grad += nt(act, w_in(t))
    sums[4:5, :] += jnp.sum(grad * hat_1, axis=0, keepdims=True)
    sums[5:6, :] += jnp.sum(grad, axis=0, keepdims=True)
    grad = norm_backward(grad, hat_1, inverse_1, gain_1)
    sums[2:3, :] += jnp.sum(grad, axis=0, keepdims=True)
    first_grad[...] = grad
    low = grad.astype(BF)
    proj_grad[...] = low
    for y in range(2):
        attn_grad[:, halves[y]] = nn(low, w_ref[0, :, proj_cols[y]]).astype(BF)

    @pl.when(pl.program_id(0) == pl.num_programs(0) - 1)
    def _():
        for t, _ in chunks:
            out_grad[:, t] = outer[t].reshape(out_grad.shape[0], out_grad.shape[2], own_units).astype(BF)


def middle(layer_in, attn, output_grad, weights, blocks, vectors):
    rows, width = layer_in.shape
    units = blocks.shape[1] * blocks.shape[3] // 2
    tile = lambda w: pl.BlockSpec((ROWS, w), lambda i: (i, 0))
    whole = lambda a: pl.BlockSpec(a.shape, lambda i: (0,) * len(a.shape), pipeline_mode=pl.Buffered(1))
    fixed = lambda w: pl.BlockSpec((8, w), lambda i: (0, 0))
    shape = lambda w, t: jax.ShapeDtypeStruct((rows, w), t)
    out_grad = jax.ShapeDtypeStruct(blocks.shape[:3] + (blocks.shape[3] // 2,), BF)
    out_spec = pl.BlockSpec(out_grad.shape, lambda i: (0, 0, 0, 0), pipeline_mode=pl.Buffered(1))
    return pl.pallas_call(
        middle_kernel,
        name="middle",
        grid=(rows // ROWS,),
        in_specs=[tile(width)] * 3 + [whole(weights), whole(blocks), whole(vectors)],
        out_specs=[tile(width)] * 4 + [tile(units), tile(width), out_spec, fixed(width), fixed(units)],
        out_shape=[
            shape(width, BF), shape(width, F32), shape(width, BF), shape(width, BF), shape(units, BF), shape(width, BF),
            out_grad,
            jax.ShapeDtypeStruct((8, width), F32), jax.ShapeDtypeStruct((8, units), F32),
        ],
        scratch_shapes=[
            pltpu.VMEM((ROWS, units), F32),
            pltpu.VMEM((ROWS, units), BF),
            pltpu.VMEM((blocks.shape[1], width, units // blocks.shape[1]), F32),
        ],
        compiler_params=params_of(),
    )(layer_in, attn, output_grad, weights, blocks, vectors)


def finish_kernel(
    n, x_hbm, dq_hbm, dkv_hbm, w_hbm, first_hbm, low_hbm, unit_hbm, proj_hbm, attn_hbm, sums_ref, unit_sums,
    input_hbm, q_out, k_out, v_out, o_out, in_out, vec_out,
    rows_in, turned, unit, d_qkv, attn, far, w_all, tile_in, tile_out, grads, sib, from_b, from_a, from_low, from_high,
    result, vec_sent, vec_got,
    load, swap_s, swap_r, ss, sr, bs, br, as_, ar, zs, zr, es, er, vs, vr, tile_sem,
):
    w = places()
    dp, rank, core, y, z, x = (w[k] for k in ("dp", "rank", "core", "y", "z", "x"))
    rows, width = x_hbm.shape
    third = width // 2
    wide = unit.shape[1] // 2
    slab = result.shape[1] // 2
    up, down = {"dp": lax.rem(dp + 2, 2 * n), "tensor": rank}, {"dp": lax.rem(dp + 2 * n - 2, 2 * n), "tensor": rank}
    partners = [w["sibling"], w["second"], w["first"]] + line_jumps(dp, rank, z, n)
    barrier = pltpu.get_barrier_semaphore()
    for other in partners + [up, down]:
        pl.semaphore_signal(barrier, inc=1, device_id=other, device_id_type=MESH)

    def fetch(i, src, dst):
        return pltpu.make_async_copy(src, dst, load.at[i])

    fetch_low = fetch(0, low_hbm, rows_in.at[0])
    fetch_unit = fetch(1, unit_hbm, unit)
    fetch_x = fetch(2, x_hbm, rows_in.at[1])
    fetch_proj = fetch(3, proj_hbm, rows_in.at[2])
    fetch_attn = fetch(4, attn_hbm, attn)
    fetch_w = fetch(5, w_hbm.at[0], w_all)
    fetch_dq = [fetch(6 + h, dq_hbm.at[:, h * third : (h + 1) * third], d_qkv.at[:, 3 * h * third : (3 * h + 1) * third]) for h in range(2)]
    fetch_kv = [fetch(8 + h, dkv_hbm.at[core, :, 2 * h * third : 2 * (h + 1) * third], d_qkv.at[:, (3 * h + 1) * third : (3 * h + 3) * third]) for h in range(2)]
    for move in [fetch_low, fetch_unit, fetch_x, fetch_proj, fetch_attn] + fetch_dq + fetch_kv + [fetch_w]:
        move.start()
    pl.semaphore_wait(barrier, len(partners) + 2)

    def copy(src, dst, ssem, rsem, dev):
        return pltpu.make_async_remote_copy(src, dst, ssem, rsem, device_id=dev, device_id_type=MESH)

    swap = copy(dkv_hbm.at[1 - core], far, swap_s, swap_r, w["sibling"])
    swap.start()

    def turn_rows(i):
        for c in range(0, width, 128):
            turned[i, c : c + 128, :] = rows_in[i, :, c : c + 128].T

    places_of = [xd * 2 + yd for xd, yd in (
        (x, y), (w["xa"], w["ya"]), (w["xb"], w["yb"]), (w["xa"] + w["xb"] - x, w["ya"] + w["yb"] - y))]
    mine = grads.at[core]

    def keep(k, zd, yd, lane, value):
        for xd in range(2):
            for c in range(2):
                first = (xd * 2 + c) * slab
                grads[c, k, zd, xd * 2 + yd, :, lane : lane + value.shape[1]] = value[first : first + slab, :].astype(BF)

    def rows_of_line(i, zd):
        return turned[i, pl.ds(pl.multiple_of(zd * 4 * slab, 4 * slab), 4 * slab), :]

    def compute_inner(zd):
        left = rows_of_line(0, zd)
        for yd in range(2):
            for lane in range(0, wide, 768):
                keep(1, zd, yd, lane, nn(left, unit[:, yd * wide + lane : yd * wide + lane + 768]))

    def compute_others(zd):
        left = rows_of_line(1, zd)
        for yd in range(2):
            for i in range(3):
                at = (3 * yd + i) * third
                keep(0, zd, yd, i * third, nn(left, d_qkv[:, at : at + third]))
        left = rows_of_line(2, zd)
        for yd in range(2):
            keep(0, zd, yd, 3 * third, nn(left, attn[:, yd * third : (yd + 1) * third]))

    def to_sibling(k, zd):
        return copy(grads.at[1 - core, k, zd], sib.at[k, zd], ss.at[k, zd], sr.at[k, zd], w["sibling"])

    def over_b(k, far_side, zd):
        place = places_of[2 + far_side]
        return copy(mine.at[k, zd, place], from_b.at[k, far_side, zd], bs.at[k, far_side, zd], br.at[k, far_side, zd], w["second"])

    def over_a(k, zd):
        return copy(mine.at[k, zd, places_of[1]], from_a.at[k, zd], as_.at[k, zd], ar.at[k, zd], w["first"])

    def over_up(k, zd):
        return copy(mine.at[k, zd, places_of[0]], from_low.at[k, zd], zs.at[k, zd], zr.at[0, k, zd], up)

    def over_down(k, zd):
        return copy(mine.at[k, zd, places_of[0]], from_high.at[k, zd], zs.at[k, zd], zr.at[1, k, zd], down)

    def put(q, k, zd, more):
        place = places_of[q]
        total = grads[core, k, zd, place].astype(F32) + sib[k, zd, place].astype(F32)
        for term in more:
            total = total + term[...].astype(F32)
        grads[core, k, zd, place] = total.astype(BF)

    def stage_b(k, zd):
        to_sibling(k, zd).wait_recv()
        for far_side in (1, 0):
            put(2 + far_side, k, zd, ())
            over_b(k, far_side, zd).start()

    def stage_a(k, zd):
        over_b(k, 1, zd).wait_recv()
        put(1, k, zd, (from_b.at[k, 1, zd],))
        over_a(k, zd).start()

    def stage_line(k, zd):
        over_b(k, 0, zd).wait_recv()
        over_a(k, zd).wait_recv()
        put(0, k, zd, (from_b.at[k, 0, zd], from_a.at[k, zd]))

        @pl.when((zd > z) & (z == 0))
        def _():
            over_up(k, zd).start()

        @pl.when((zd < z) & (z == n - 1))
        def _():
            over_down(k, zd).start()

    def grow(k, zd, term):
        place = places_of[0]
        grads[core, k, zd, place] = (grads[core, k, zd, place].astype(F32) + term[...].astype(F32)).astype(BF)

    def stage_hop(k, zd):
        @pl.when((zd > z) & (z > 0))
        def _():
            over_up(k, zd).wait_recv()
            grow(k, zd, from_low.at[k, zd])
            over_up(k, zd).start()

        @pl.when((zd < z) & (z < n - 1))
        def _():
            over_down(k, zd).wait_recv()
            grow(k, zd, from_high.at[k, zd])
            over_down(k, zd).start()

    def turn(i):
        below, above = z, n - 1 - z
        near = jnp.minimum(below, above)
        only = jnp.maximum(below, above) - near
        side = jnp.where(above >= below, 1, -1)
        distance = jnp.where(i < only, only + near - i, near - (i - only) // 2)
        sign = jnp.where(i < only, side, jnp.where(lax.rem(i - only, 2) == 0, side, -side))
        return jnp.where(i == n - 1, z, z + sign * distance)

    def item(j):
        return 1 - j // n, turn(lax.rem(j, n))

    def small_send(step):
        return copy(vec_sent.at[step], vec_got.at[step], vs.at[step], vr.at[step], partners[step])

    def input_tile(t):
        at = pl.ds(pl.multiple_of(t * ROWS, ROWS), ROWS)
        return (pltpu.make_async_copy(first_hbm.at[at, :], tile_in.at[lax.rem(t, 2)], tile_sem.at[0, lax.rem(t, 2)]),
                pltpu.make_async_copy(tile_out.at[lax.rem(t, 2)], input_hbm.at[at, :], tile_sem.at[1, lax.rem(t, 2)]), at)

    def input_grad(t):
        into, out, at = input_tile(t)
        into.start()
        total = nt(d_qkv[at, : 3 * third], w_all[:, : 3 * third])
        total += nt(d_qkv[at, 3 * third :], w_all[:, wide : wide + 3 * third])
        into.wait()
        tile_out[lax.rem(t, 2)] = tile_in[lax.rem(t, 2)] + total
        out.start()

    tiles = rows // ROWS
    last_item = 2 * n

    fetch_low.wait()
    turn_rows(0)
    fetch_unit.wait()

    @pl.loop(0, last_item + 4)
    def _(j):
        @pl.when(j < n)
        def _():
            k, zd = item(j)
            compute_inner(zd)
            to_sibling(1, zd).start()

        @pl.when(j == n - 1)
        def _():
            fetch_x.wait()
            fetch_proj.wait()
            fetch_attn.wait()
            turn_rows(1)
            turn_rows(2)
            for move in fetch_dq + fetch_kv:
                move.wait()
            swap.wait_recv()
            for h in range(2):
                at = slice((3 * h + 1) * third, (3 * h + 3) * third)
                d_qkv[:, at] = (d_qkv[:, at].astype(F32) + far[:, 2 * h * third : 2 * (h + 1) * third].astype(F32)).astype(BF)
            vec_sent[0] = jnp.zeros_like(vec_sent[0])
            vec_sent[0, 2:8, :] = sums_ref[2:8, :]
            for h in range(2):
                for row, i in ((0, 0), (1, 2)):
                    cols = d_qkv[:, (3 * h + i) * third : (3 * h + i + 1) * third].astype(F32)
                    vec_sent[0, row : row + 1, h * third : (h + 1) * third] = jnp.sum(cols, axis=0, keepdims=True)
            for u in range(unit_sums.shape[1] // width):
                vec_sent[0, 8 + u : 9 + u, :] = unit_sums[0:1, u * width : (u + 1) * width]
            small_send(0).start()
            fetch_w.wait()

        @pl.when((j >= n) & (j < last_item))
        def _():
            k, zd = item(j)
            compute_others(zd)
            to_sibling(0, zd).start()

        @pl.when((j >= 1) & (j < last_item + 1))
        def _():
            stage_b(*item(j - 1))

        @pl.when((j >= 2) & (j < last_item + 2))
        def _():
            stage_a(*item(j - 2))

        @pl.when((j >= 3) & (j < last_item + 3))
        def _():
            stage_line(*item(j - 3))

        @pl.when(j >= 4)
        def _():
            stage_hop(*item(j - 4))

        for step in range(len(partners)):
            @pl.when(j == n + step)
            def _(step=step):
                small_send(step).wait_recv()
                vec_sent[step + 1] = vec_sent[step] + vec_got[step]
                if step + 1 < len(partners):
                    small_send(step + 1).start()

        @pl.when((j >= last_item - tiles) & (j < last_item))
        def _():
            t = j - (last_item - tiles)

            @pl.when(t >= 2)
            def _():
                input_tile(t - 2)[1].wait()
            input_grad(t)

    vec_out[...] = vec_sent[len(partners)]
    own = pl.ds(pl.multiple_of(core * slab, slab), slab)
    theirs = pl.ds(pl.multiple_of((1 - core) * slab, slab), slab)
    for k in (1, 0):
        result[k, own, :] = grads[core, k, z, places_of[0]].astype(F32)

        @pl.when(z > 0)
        def _():
            over_up(k, z).wait_recv()
            result[k, own, :] += from_low[k, z].astype(F32)

        @pl.when(z < n - 1)
        def _():
            over_down(k, z).wait_recv()
            result[k, own, :] += from_high[k, z].astype(F32)

        copy(result.at[k, own, :], result.at[k, own, :], es.at[k], er.at[k], w["sibling"]).start()
    for t in range(max(tiles - 2, 0), tiles):
        input_tile(t)[1].wait()
    swap.wait_send()
    for step in range(len(partners)):
        small_send(step).wait_send()

    @pl.loop(0, n)
    def _(zd):
        for k in range(2):
            to_sibling(k, zd).wait_send()
            over_b(k, 0, zd).wait_send()
            over_b(k, 1, zd).wait_send()
            over_a(k, zd).wait_send()

            @pl.when(zd > z)
            def _():
                over_up(k, zd).wait_send()

            @pl.when(zd < z)
            def _():
                over_down(k, zd).wait_send()
    for k in (1, 0):
        copy(result.at[k, theirs, :], result.at[k, theirs, :], es.at[k], er.at[k], w["sibling"]).wait()

    def chosen(k, lane, w_own):
        both = result[k, :, lane : lane + 2 * w_own]
        return jnp.where(core == 0, both[:, :w_own], both[:, w_own:])

    for i, out in enumerate((q_out, k_out, v_out, o_out)):
        out[...] = chosen(0, i * third, third // 2)
    in_out[...] = chosen(1, 0, wide // 2)


def finish(layer_in, dq, dkv, weights, grad_first, norm_low, unit_grad, proj_grad, attn, sums, unit_sums):
    rows, width = layer_in.shape
    units = unit_grad.shape[1]
    dp, tp = lax.axis_size("dp"), lax.axis_size("tensor")
    n = dp // 2
    block = width // dp
    slab, wide, third = block // 2, units // 2, width // 2
    steps = 3 + (n - 1).bit_length()
    dma = pltpu.SemaphoreType.DMA
    slabs = lambda *lead: pltpu.VMEM(lead + (slab, wide), BF)
    anywhere, inside = pl.BlockSpec(memory_space=pl.ANY), pl.BlockSpec(memory_space=pltpu.VMEM)
    result = lambda *shape: jax.ShapeDtypeStruct(shape, F32)
    return pl.pallas_call(
        partial(finish_kernel, n),
        name="finish",
        in_specs=[anywhere] * 9 + [inside] * 2,
        out_specs=[anywhere] + [inside] * 6,
        out_shape=[result(rows, width)] + [result(block, third // 2)] * 4 + [result(block, wide // 2), result(16, width)],
        scratch_shapes=[
            pltpu.VMEM((3, rows, width), BF),
            pltpu.VMEM((3, width, rows), BF),
            pltpu.VMEM((rows, units), BF),
            pltpu.VMEM((rows, 3 * width), BF),
            pltpu.VMEM((rows, width), BF),
            pltpu.VMEM((rows, 2 * width), BF),
            pltpu.VMEM((width, units), BF),
            pltpu.VMEM((2, ROWS, width), F32),
            pltpu.VMEM((2, ROWS, width), F32),
            slabs(2, 2, n, 4),
            slabs(2, n, 4),
            slabs(2, 2, n),
            slabs(2, n),
            slabs(2, n),
            slabs(2, n),
            pltpu.VMEM((2, block, wide), F32),
            pltpu.VMEM((steps + 1, 16, width), F32),
            pltpu.VMEM((steps, 16, width), F32),
            dma((10,)), dma(()), dma(()),
            dma((2, n)), dma((2, n)), dma((2, 2, n)), dma((2, 2, n)), dma((2, n)), dma((2, n)),
            dma((2, n)), dma((2, 2, n)), dma((2,)), dma((2,)), dma((steps,)), dma((steps,)), dma((2, 2)),
        ],
        compiler_params=pltpu.CompilerParams(
            collective_id=4, has_side_effects=True, vmem_limit_bytes=60 * 2**20
        ),
    )(layer_in, dq, dkv.reshape(2, rows, 2 * width), weights, grad_first, norm_low, unit_grad, proj_grad, attn, sums, unit_sums)


def finish_plainly(layer_in, dq, dkv, weights, grad_first, norm_low, unit_grad, proj_grad, attn, sums, unit_sums):
    rows, width = layer_in.shape
    units = unit_grad.shape[1]
    dp, tp = lax.axis_size("dp"), lax.axis_size("tensor")
    third, block, pairs = width // 2, width // dp, tp // 2
    half = lax.rem(lax.axis_index("tensor"), 2)
    both = dkv.reshape(2, rows, 2 * width)
    far = swap_pair(both)
    near = lax.dynamic_index_in_dim(both, half, 0, False)
    own = (near.astype(F32) + far.astype(F32)).astype(BF)
    d_qkv = jnp.concatenate([dq[:, :third], own[:, :width], dq[:, third:], own[:, width:]], axis=1)
    wqkv = weights[0].reshape(width, 2, 4 * third)[:, :, : 3 * third].reshape(width, 3 * width)
    input_grad = grad_first + nt(d_qkv, wqkv)
    grads = [g.astype(BF) for g in (tn(layer_in, d_qkv), tn(proj_grad, attn), tn(norm_low, unit_grad))]
    joined = jnp.concatenate([g.reshape(width, pairs, -1) for g in grads[:2]], axis=2)
    every = jnp.stack([joined.reshape(width, units), grads[2]])
    every = every.reshape(2, dp, block, pairs, 1, units // pairs).transpose(1, 3, 4, 0, 2, 5)
    every = jnp.broadcast_to(every, (dp, pairs, 2, 2, block, units // pairs))
    total = lax.psum_scatter(
        every.reshape(dp * tp, 2, block, units // pairs), ("dp", "tensor"), scatter_dimension=0, tiled=False
    ).astype(F32)
    d_bias = jnp.sum(d_qkv.astype(F32), axis=0).reshape(2, 3, third)
    vec = jnp.concatenate(
        [d_bias[:, 0].reshape(1, width), d_bias[:, 2].reshape(1, width), sums[2:],
         unit_sums[0].reshape(-1, width), jnp.zeros((8 - units // width, width), F32)], axis=0,
    )
    vec = lax.psum(vec, ("dp", "tensor"))

    def chosen(k, lane, w_own):
        return lax.dynamic_slice_in_dim(total[k], lane + half * w_own, w_own, axis=1)

    return (input_grad,) + tuple(chosen(0, i * third, third // 2) for i in range(4)) + (
        chosen(1, 0, units // tp), vec)


def on_device(
    layer_in, query_weight, key_weight, value_weight, output_weight, inner_weight, outer_weight,
    query_bias, value_bias, output_bias, inner_bias, outer_bias, first_gain, first_shift,
    second_gain, second_shift, segment_ids, pad_mask, random_blocks, global_blocks, output_grad,
):
    rows, width = layer_in.shape
    dp, tp = lax.axis_size("dp"), lax.axis_size("tensor")
    own_rows, own_cols = query_weight.shape
    own_units = inner_weight.shape[1]
    third = width // 2
    half = lax.rem(lax.axis_index("tensor"), 2)

    def beside(own):
        zero = jnp.zeros_like(own)
        return jnp.concatenate(
            [jnp.where(half == 0, own, zero), jnp.where(half == 0, zero, own)], axis=1
        )

    units_own = jnp.concatenate([inner_weight, outer_weight.T], axis=1)
    blocks = lax.all_gather(units_own, ("dp", "tensor"), axis=0, tiled=False)
    blocks = blocks.reshape(dp, tp, own_rows, 2 * own_units)
    mine = jnp.concatenate(
        [beside(w) for w in (query_weight, key_weight, value_weight, output_weight.T)], axis=1
    )[None]
    place = lax.axis_index("dp") * tp + lax.axis_index("tensor")
    one, own_bias = query_bias.shape[0], inner_bias.shape[0]
    small = jnp.stack([query_bias, value_bias, output_bias, outer_bias, first_gain, first_shift,
                       second_gain, second_shift])
    eight = lax.dynamic_update_slice(jnp.zeros((8, width), F32), small, (0, place * one))
    unit = lax.dynamic_update_slice(jnp.zeros((8 * width,), F32), inner_bias, (place * own_bias,))
    vec = jnp.concatenate([eight, unit.reshape(8, width)], axis=0)
    begin = start if in_tiles(own_rows) else start_plainly
    weights, qkv, other, vectors = begin(mine, vec, layer_in)

    bounds, row_info, key_info = attention_plan(
        segment_ids, pad_mask, random_blocks, global_blocks, rows
    )
    attn, logs = attend_forward(bounds, qkv, other, row_info, key_info)
    (layer_out, grad_first, grad_attn, norm_low, unit_grad, proj_grad, out_grad, sums, unit_sums) = middle(
        layer_in, attn, output_grad, weights, blocks, vectors
    )
    d_outer = lax.psum_scatter(
        out_grad.reshape((dp * tp,) + out_grad.shape[2:]), ("dp", "tensor"), scatter_dimension=0, tiled=False
    )
    dq, dkv = attend_backward(bounds, qkv, other, row_info, key_info, attn, logs, grad_attn)
    end = finish if in_tiles(own_rows) else finish_plainly
    input_grad, d_q, d_k, d_v, d_o, d_inner, vec = end(
        layer_in, dq, dkv, weights, grad_first, norm_low, unit_grad, proj_grad, attn, sums, unit_sums
    )
    pieces = lax.dynamic_slice_in_dim(vec[:8], place * one, one, axis=1)
    (r_bq, r_bv, r_bo, r_bout, r_g1, r_s1, r_g2, r_s2) = (pieces[i] for i in range(8))
    d_bin = lax.dynamic_slice_in_dim(vec[8:].reshape(-1), place * own_bias, own_bias)
    return (
        layer_out, input_grad, d_q, d_k, d_v, d_o.T, d_inner, d_outer.astype(F32).T,
        r_bq, r_bv, r_bo, d_bin, r_bout, r_g1, r_s1, r_g2, r_s2,
    )


def solution(mesh):
    tokens = P(("dp", "tensor"), None)
    vector = P(("dp", "tensor"))
    cols, turned = P("dp", "tensor"), P("tensor", "dp")
    return jax.shard_map(
        on_device,
        mesh=mesh,
        in_specs=(tokens, cols, cols, cols, turned, cols, turned)
        + (vector,) * 9
        + (P("dp"), P("dp"), P("dp", None, None), P("dp", None, None), tokens),
        out_specs=(tokens, tokens, cols, cols, cols, turned, cols, turned) + (vector,) * 9,
        check_vma=False,
    )
```

```python
from functools import partial

import jax
import jax.numpy as jnp
from jax import lax
from jax.experimental import pallas as pl
from jax.experimental.pallas import tpu as pltpu
from jax.sharding import PartitionSpec as P

HD = 64
PAIR = 2 * HD
QT = 256
KT = 128
ROWS = 256
EPSILON = 1e-06
NEGATIVE = -1e30
MESH = pl.DeviceIdType.MESH
VMEM_LIMIT = 56 * 2**20
BF = jnp.bfloat16
F32 = jnp.float32


def params_of(collective_id=None):
    if collective_id is None:
        return pltpu.CompilerParams(vmem_limit_bytes=VMEM_LIMIT)
    return pltpu.CompilerParams(
        vmem_limit_bytes=VMEM_LIMIT, collective_id=collective_id, has_side_effects=True
    )


def nt(left, right, **more):
    return lax.dot_general(
        left, right, (((1,), (1,)), ((), ())), preferred_element_type=F32, **more
    )


def nn(left, right):
    return lax.dot_general(left, right, (((1,), (0,)), ((), ())), preferred_element_type=F32)


def tn(left, right):
    return lax.dot_general(left, right, (((0,), (0,)), ((), ())), preferred_element_type=F32)


def sibling_of():
    rank = lax.axis_index("tensor")
    half = lax.rem(rank, 2)
    return half, {"tensor": rank + 1 - 2 * half}


def meet(others):
    barrier = pltpu.get_barrier_semaphore()
    for other in others:
        pl.semaphore_signal(barrier, inc=1, device_id=other, device_id_type=MESH)
    pl.semaphore_wait(barrier, len(others))


def swap_keys_kernel(qkv_ref, other_ref, send_sem, recv_sem):
    half, sibling = sibling_of()
    meet([sibling])
    third = qkv_ref.shape[1] // 6
    moves = [
        pltpu.make_async_remote_copy(
            qkv_ref.at[:, (3 * y + 1) * third : (3 * y + 3) * third],
            other_ref.at[:, 2 * y * third : 2 * (y + 1) * third],
            send_sem.at[y], recv_sem.at[y], device_id=sibling, device_id_type=MESH,
        )
        for y in range(2)
    ]
    for move in moves:
        move.start()
    for move in moves:
        move.wait()


def swap_keys(qkv):
    rows, width = qkv.shape
    return pl.pallas_call(
        swap_keys_kernel,
        name="swap_keys",
        out_shape=jax.ShapeDtypeStruct((rows, width * 2 // 3), qkv.dtype),
        in_specs=[pl.BlockSpec(memory_space=pl.ANY)],
        out_specs=pl.BlockSpec(memory_space=pl.ANY),
        scratch_shapes=[pltpu.SemaphoreType.DMA((2,))] * 2,
        compiler_params=params_of(1),
    )(qkv)


def swap_pair_kernel(both_ref, other_ref, send_sem, recv_sem):
    half, sibling = sibling_of()
    meet([sibling])
    away = pltpu.make_async_remote_copy(
        both_ref.at[1 - half], other_ref, send_sem, recv_sem,
        device_id=sibling, device_id_type=MESH,
    )
    away.start()
    away.wait()


def swap_pair(both):
    return pl.pallas_call(
        swap_pair_kernel,
        name="swap_pair",
        out_shape=jax.ShapeDtypeStruct(both.shape[1:], both.dtype),
        in_specs=[pl.BlockSpec(memory_space=pl.ANY)],
        out_specs=pl.BlockSpec(memory_space=pl.ANY),
        scratch_shapes=[pltpu.SemaphoreType.DMA(())] * 2,
        compiler_params=params_of(2),
    )(both)


def places():
    dp, rank = lax.axis_index("dp"), lax.axis_index("tensor")
    core, y = lax.rem(rank, 2), rank // 2
    z, x = dp // 2, lax.rem(dp, 2)
    sibling = {"dp": dp, "tensor": rank + 1 - 2 * core}
    near_x = {"dp": dp + 1 - 2 * x, "tensor": rank}
    near_y = {"dp": dp, "tensor": rank + 2 - 4 * y}
    first = {"dp": dp + (1 - core) * (1 - 2 * x), "tensor": rank + core * (2 - 4 * y)}
    second = {"dp": dp + core * (1 - 2 * x), "tensor": rank + (1 - core) * (2 - 4 * y)}
    xa, ya = x + (1 - core) * (1 - 2 * x), y + core * (1 - 2 * y)
    xb, yb = x + core * (1 - 2 * x), y + (1 - core) * (1 - 2 * y)
    return dict(dp=dp, rank=rank, core=core, y=y, z=z, x=x, sibling=sibling, first=first, second=second,
                xa=xa, ya=ya, xb=xb, yb=yb)


def line_jumps(dp, rank, z, n):
    jumps, hop = [], 1
    while hop < n:
        bit = lax.rem(z // hop, 2)
        jumps.append({"dp": dp + 2 * hop * (1 - 2 * bit), "tensor": rank})
        hop *= 2
    return jumps


def start_kernel(
    n, mine_ref, vec_ref, x_ref, w_hbm, qkv_hbm, other_hbm, vec_out,
    out_ref, chip, sib, qkv, vec_sent, vec_got,
    local_sem, pair_sem, zs, zr, as_, ar, bs, br, ss, sr, ks, kr, vs, vr,
):
    w = places()
    dp, rank, core, y, z, x = (w[k] for k in ("dp", "rank", "core", "y", "z", "x"))
    block, wide = mine_ref.shape[1], mine_ref.shape[2]
    slab = block // 2
    up, down = {"dp": lax.rem(dp + 2, 2 * n), "tensor": rank}, {"dp": lax.rem(dp + 2 * n - 2, 2 * n), "tensor": rank}
    partners = [w["sibling"], w["second"], w["first"]] + line_jumps(dp, rank, z, n)
    meet([up, down] + partners)

    pair = pltpu.make_async_remote_copy(mine_ref, sib, pair_sem.at[0], pair_sem.at[1], device_id=w["sibling"], device_id_type=MESH)
    pair.start()

    def small_send(step):
        return pltpu.make_async_remote_copy(vec_sent.at[step], vec_got.at[step], vs.at[step], vr.at[step], device_id=partners[step], device_id_type=MESH)

    def small_step(step):
        small_send(step).wait_recv()
        vec_sent[step + 1] = vec_sent[step] + vec_got[step]
        if step + 1 < len(partners):
            small_send(step + 1).start()

    vec_sent[0] = vec_ref[...]
    small_send(0).start()
    pair.wait()
    chip[...] = mine_ref[...] + sib[...]
    rows_own = pl.ds(pl.multiple_of(core * slab, slab), slab)
    own_at = pl.ds(pl.multiple_of(dp * block, block), block)
    cols_own = pl.ds(pl.multiple_of(y * wide, wide), wide)
    keep = pltpu.make_async_copy(chip, out_ref.at[:, own_at, cols_own], local_sem.at[0])
    keep.start()

    def spot(g, zi, xi, yi):
        d = zi * 2 + xi
        rows = pl.ds(pl.multiple_of(d * block + core * slab, slab), slab)
        cols = pl.ds(pl.multiple_of(yi * wide, wide), wide)
        return out_ref.at[:, rows, cols]

    def own(g):
        return chip.at[:, rows_own, :]

    def move(g, zi, xi, yi, dev, ssem, rsem, source=None):
        at = spot(g, zi, xi, yi)
        return pltpu.make_async_remote_copy(at if source is None else source, at, ssem, rsem, device_id=dev, device_id_type=MESH)

    def line_up(g, s):
        return move(g, z - s, x, y, up, zs.at[g, 0, s], zr.at[g, 0, s], own(g) if s == 0 else None)

    def line_down(g, s):
        return move(g, z + s, x, y, down, zs.at[g, 1, s], zr.at[g, 1, s], own(g) if s == 0 else None)

    def to_first(g, zi, source=None):
        return move(g, zi, x, y, w["first"], as_.at[g, zi], ar.at[g, zi], source)

    def to_second(g, zi, far, source=None):
        xi, yi = (w["xa"], w["ya"]) if far else (x, y)
        return move(g, zi, xi, yi, w["second"], bs.at[g, far, zi], br.at[g, far, zi], source)

    def to_sibling(g, zi, quarter, source=None):
        xi = (x, w["xa"], w["xb"], w["xa"] + w["xb"] - x)[quarter]
        yi = (y, w["ya"], w["yb"], w["ya"] + w["yb"] - y)[quarter]
        return move(g, zi, xi, yi, w["sibling"], ss.at[g, quarter, zi], sr.at[g, quarter, zi], source)

    def begin(g):
        @pl.when(z < n - 1)
        def _():
            line_up(g, 0).start()

        @pl.when(z > 0)
        def _():
            line_down(g, 0).start()

        to_first(g, z, own(g)).start()
        to_second(g, z, 0, own(g)).start()

    def first_in(g, zi):
        got = move(g, zi, w["xa"], w["ya"], w["first"], as_.at[g, zi], ar.at[g, zi])
        got.wait_recv()
        to_second(g, zi, 1).start()
        to_sibling(g, zi, 1).start()

    def second_in(g, zi, far):
        q = 2 + far
        xi = (w["xb"], w["xa"] + w["xb"] - x)[far]
        yi = (w["yb"], w["ya"] + w["yb"] - y)[far]
        move(g, zi, xi, yi, w["second"], bs.at[g, far, zi], br.at[g, far, zi]).wait_recv()
        to_sibling(g, zi, q).start()

    def below_in(g, s):
        zi = z - 1 - s
        move(g, zi, x, y, up, zs.at[g, 0, s], zr.at[g, 0, s]).wait_recv()
        if s + 1 < n - 1:
            @pl.when(z < n - 1)
            def _():
                line_up(g, s + 1).start()
        to_first(g, zi).start()
        to_second(g, zi, 0).start()
        to_sibling(g, zi, 0).start()

    def above_in(g, s):
        zi = z + 1 + s
        move(g, zi, x, y, down, zs.at[g, 1, s], zr.at[g, 1, s]).wait_recv()
        if s + 1 < n - 1:
            @pl.when(z > 0)
            def _():
                line_down(g, s + 1).start()
        to_first(g, zi).start()
        to_second(g, zi, 0).start()
        to_sibling(g, zi, 0).start()

    def steps(gs):
        for g in gs:
            first_in(g, z)
        for s in range(n - 1):
            @pl.when(z - 1 - s >= 0)
            def _(s=s):
                for g in gs:
                    below_in(g, s)

            @pl.when(z + 1 + s < n)
            def _(s=s):
                for g in gs:
                    above_in(g, s)
            if s > 0:
                both(s, lambda g, zi: first_in(g, zi), gs)
        both(n - 1, lambda g, zi: first_in(g, zi), gs)
        for g in gs:
            second_in(g, z, 0)
        for g in gs:
            second_in(g, z, 1)
        for s in range(1, n):
            both(s, lambda g, zi: second_in(g, zi, 0), gs)
            both(s, lambda g, zi: second_in(g, zi, 1), gs)

    def both(s, what, gs):
        @pl.when(z - s >= 0)
        def _():
            for g in gs:
                what(g, z - s)

        @pl.when(z + s < n)
        def _():
            for g in gs:
                what(g, z + s)

    begin(0)
    small_step(0)
    steps((0,))
    for step in range(1, len(partners)):
        small_step(step)

    keep.wait()
    for zi in range(n):
        for q in range(1, 4):
            to_sibling(0, zi, q).wait_recv()

        @pl.when(zi != z)
        def _(zi=zi):
            to_sibling(0, zi, 0).wait_recv()
    save_w = pltpu.make_async_copy(out_ref, w_hbm, local_sem.at[1])
    save_w.start()

    rows, width = x_ref.shape
    third = width // 2
    vec_out[...] = vec_sent[len(partners)]
    tiles = rows // ROWS

    def keys_of(t, yi):
        at = (pl.ds(pl.multiple_of(t * ROWS, ROWS), ROWS), slice((3 * yi + 1) * third, (3 * yi + 3) * third))
        far = (at[0], slice(2 * yi * third, 2 * (yi + 1) * third))
        return pltpu.make_async_remote_copy(qkv.at[at], other_hbm.at[far], ks.at[t, yi], kr.at[t, yi], device_id=w["sibling"], device_id_type=MESH)

    @pl.loop(0, tiles)
    def _(t):
        at = pl.ds(pl.multiple_of(t * ROWS, ROWS), ROWS)
        for yi in range(2):
            both = nn(x_ref[at, :], out_ref[0, :, yi * wide + third : yi * wide + 3 * third])
            first = (3 * yi + 1) * third
            qkv[at, first : first + third] = both[:, :third].astype(BF)
            bias = vec_out[1:2, yi * third : (yi + 1) * third]
            qkv[at, first + third : first + 2 * third] = (both[:, third:] + bias).astype(BF)
            keys_of(t, yi).start()

    @pl.loop(0, tiles)
    def _(t):
        at = pl.ds(pl.multiple_of(t * ROWS, ROWS), ROWS)
        for yi in range(2):
            bias = vec_out[0:1, yi * third : (yi + 1) * third]
            mine = nn(x_ref[at, :], out_ref[0, :, yi * wide : yi * wide + third]) + bias
            qkv[at, 3 * yi * third : (3 * yi + 1) * third] = mine.astype(BF)

    save_qkv = pltpu.make_async_copy(qkv, qkv_hbm, local_sem.at[2])
    save_qkv.start()
    for g in (0,):
        @pl.when(z < n - 1)
        def _(g=g):
            line_up(g, 0).wait_send()

        @pl.when(z > 0)
        def _(g=g):
            line_down(g, 0).wait_send()
        for s in range(1, n - 1):
            @pl.when((z < n - 1) & (z - s >= 0))
            def _(g=g, s=s):
                line_up(g, s).wait_send()

            @pl.when((z > 0) & (z + s < n))
            def _(g=g, s=s):
                line_down(g, s).wait_send()
        for zi in range(n):
            to_first(g, zi).wait_send()
            for far in range(2):
                to_second(g, zi, far).wait_send()
            for q in range(1, 4):
                to_sibling(g, zi, q).wait_send()
        for zi in range(n):
            @pl.when(zi != z)
            def _(g=g, zi=zi):
                to_sibling(g, zi, 0).wait_send()


    for step in range(len(partners)):
        small_send(step).wait_send()

    @pl.loop(0, tiles)
    def _(t):
        for yi in range(2):
            keys_of(t, yi).wait()
    save_w.wait()
    save_qkv.wait()


def start(mine, vec, layer_in):
    dp, tp = lax.axis_size("dp"), lax.axis_size("tensor")
    n = dp // 2
    parts, block, wide = mine.shape
    rows, width = layer_in.shape
    steps = 3 + (n - 1).bit_length()
    tiles = rows // ROWS
    dma = pltpu.SemaphoreType.DMA
    anywhere, inside = pl.BlockSpec(memory_space=pl.ANY), pl.BlockSpec(memory_space=pltpu.VMEM)
    whole = (parts, dp * block, wide * tp // 2)
    return pl.pallas_call(
        partial(start_kernel, n),
        name="start",
        in_specs=[inside] * 3,
        out_specs=[anywhere] * 3 + [inside],
        out_shape=[
            jax.ShapeDtypeStruct(whole, BF),
            jax.ShapeDtypeStruct((rows, 3 * width), BF),
            jax.ShapeDtypeStruct((rows, 2 * width), BF),
            jax.ShapeDtypeStruct(vec.shape, F32),
        ],
        scratch_shapes=[
            pltpu.VMEM(whole, BF), pltpu.VMEM(mine.shape, BF), pltpu.VMEM(mine.shape, BF),
            pltpu.VMEM((rows, 3 * width), BF),
            pltpu.VMEM((steps + 1,) + vec.shape, F32), pltpu.VMEM((steps,) + vec.shape, F32),
            dma((3,)), dma((2,)), dma((1, 2, n)), dma((1, 2, n)), dma((1, n)), dma((1, n)),
            dma((1, 2, n)), dma((1, 2, n)), dma((1, 4, n)), dma((1, 4, n)), dma((tiles, 2)), dma((tiles, 2)),
            dma((steps,)), dma((steps,)),
        ],
        compiler_params=params_of(3),
    )(mine, vec, layer_in)


def in_tiles(block):
    return block % 32 == 0


def start_plainly(mine, vec, layer_in):
    dp, tp = lax.axis_size("dp"), lax.axis_size("tensor")
    parts, block, wide = mine.shape
    width = layer_in.shape[1]
    third = width // 2
    every = lax.all_gather(mine, ("dp", "tensor"), axis=0, tiled=False)
    every = every.reshape(dp, tp // 2, 2, parts, block, wide).sum(axis=2)
    weights = every.transpose(2, 0, 3, 1, 4).reshape(parts, dp * block, tp // 2 * wide)
    vec = lax.psum(vec, ("dp", "tensor"))
    zero = jnp.zeros((1, third), F32)
    bias = jnp.concatenate(
        [v for y in range(2) for v in (vec[:1, y * third : (y + 1) * third], zero,
                                       vec[1:2, y * third : (y + 1) * third])], axis=1,
    )
    wqkv = weights[0].reshape(width, 2, 4 * third)[:, :, : 3 * third].reshape(width, 3 * width)
    qkv = (nn(layer_in, wqkv) + bias).astype(BF)
    return weights, qkv, swap_keys(qkv), vec


def q_lanes(p, pairs):
    third = pairs // 2 * PAIR
    first = p // (pairs // 2) * 3 * third + p % (pairs // 2) * PAIR
    return slice(first, first + PAIR)


def k_lanes(p, pairs):
    third = pairs // 2 * PAIR
    first = p // (pairs // 2) * 2 * third + p % (pairs // 2) * PAIR
    return slice(first, first + PAIR)


def v_lanes(p, pairs):
    third = pairs // 2 * PAIR
    lanes = k_lanes(p, pairs)
    return slice(lanes.start + third, lanes.stop + third)


def key_tile(j, qkv_ref, other_ref, kv, sems):
    rows, third = other_ref.shape[0], other_ref.shape[1] // 4
    here = pl.ds(pl.multiple_of(j * KT, KT), KT)
    from_row = pl.ds(pl.multiple_of(lax.rem(j * KT, rows), KT), KT)
    own = [
        pltpu.make_async_copy(
            qkv_ref.at[from_row, (3 * y + 1) * third : (3 * y + 3) * third],
            kv.at[here, 2 * y * third : 2 * (y + 1) * third],
            sems.at[y, j],
        )
        for y in range(2)
    ]
    far = pltpu.make_async_copy(other_ref.at[from_row, :], kv.at[here, :], sems.at[0, j])
    is_own = (j * KT) // rows == lax.rem(lax.axis_index("tensor"), 2)
    return is_own, own, far


def fetch_keys(low, high, qkv_ref, other_ref, kv, sems, use):
    @pl.loop(low, high)
    def _(j):
        is_own, own, far = key_tile(j, qkv_ref, other_ref, kv, sems)

        @pl.when(is_own)
        def _():
            for move in own:
                move.start()

        @pl.when(jnp.logical_not(is_own))
        def _():
            far.start()

    @pl.loop(low, high)
    def _(j):
        is_own, own, far = key_tile(j, qkv_ref, other_ref, kv, sems)

        @pl.when(is_own)
        def _():
            for move in own:
                move.wait()

        @pl.when(jnp.logical_not(is_own))
        def _():
            far.wait()
        use(j)


def masked_pairs(source, target, lanes_of, pairs, scale):
    rows = source.shape[0]
    low_lanes = lax.broadcasted_iota(jnp.int32, (rows, PAIR), 1) < HD
    for p in range(pairs):
        both = source[:, lanes_of(p)]
        if scale is not None:
            both = both * jnp.asarray(scale, both.dtype)
        zero = jnp.zeros_like(both)
        target[p, :rows, :] = jnp.where(low_lanes, both, zero)
        target[p, rows:, :] = jnp.where(low_lanes, zero, both)


def tile_bias(j, q_first, row_info, key_info, bias):
    seg_q, bits_q = row_info[0:1, :], row_info[1:2, :]
    queries = bias.shape[1]
    for part in range(KT // HD):
        block = j * (KT // HD) + part
        bit = jnp.bitwise_and(
            lax.shift_right_logical(bits_q, jnp.full_like(bits_q, block)), 1
        )
        wanted = jnp.where(bit == 1, seg_q, -1)
        base = pl.multiple_of(j * KT + part * HD, HD)
        seg_k = key_info[pl.ds(base, HD), :]
        key_at = base + lax.broadcasted_iota(jnp.int32, (HD, queries), 0)
        query_at = q_first + lax.broadcasted_iota(jnp.int32, (HD, queries), 1)
        allowed = (seg_k == wanted) | (key_at == query_at)
        bias[part * HD : (part + 1) * HD, :] = jnp.where(allowed, 0.0, NEGATIVE)


def attend_forward_kernel(
    bounds, q_ref, qkv_ref, other_ref, row_info, key_info, out_ref, log_ref,
    q_pairs, kv_ref, v_turned, bias, top, total, acc, scores, fades, lows, sems,
):
    step = pl.program_id(0)
    rows, width = out_ref.shape
    pairs = width // PAIR
    tiles = kv_ref.shape[0] // KT

    @pl.when(step == 0)
    def _():
        def turn(j):
            for p in range(pairs):
                span = slice(p * PAIR, (p + 1) * PAIR)
                v_turned[j, span, :] = kv_ref[pl.ds(pl.multiple_of(j * KT, KT), KT), v_lanes(p, pairs)].T

        fetch_keys(bounds[0, 0], bounds[pl.num_programs(0) - 1, 1], qkv_ref, other_ref, kv_ref, sems, turn)

    masked_pairs(q_ref, q_pairs, partial(q_lanes, pairs=pairs), pairs, HD**-0.5)
    top[...] = jnp.full_like(top, NEGATIVE)
    total[...] = jnp.zeros_like(total)
    acc[...] = jnp.zeros_like(acc)
    q_first = bounds[step, 2]

    @pl.loop(bounds[step, 0], bounds[step, 1])
    def _(j):
        tile_bias(j, q_first, row_info, key_info, bias)
        keys_at = pl.multiple_of(j * KT, KT)
        for p in range(pairs):
            keys = kv_ref[pl.ds(keys_at, KT), k_lanes(p, pairs)]
            scores[p] = nt(keys, q_pairs[p])
        for h in range(2 * pairs):
            p, e = divmod(h, 2)
            mine = scores[p, :, e * rows : (e + 1) * rows] + bias[...]
            before = top[h : h + 1, :]
            now = jnp.maximum(before, jnp.max(mine, axis=0, keepdims=True))
            fade = jnp.exp(before - now)
            expos = jnp.exp(mine - now)
            top[h : h + 1, :] = now
            fades[h : h + 1, :] = fade
            total[h : h + 1, :] = fade * total[h : h + 1, :] + jnp.sum(
                expos, axis=0, keepdims=True
            )
            lows[h] = expos.astype(BF)
        for h in range(2 * pairs):
            span = slice(h * HD, (h + 1) * HD)
            acc[span, :] = acc[span, :] * fades[h : h + 1, :] + nn(v_turned[j, span, :], lows[h])

    heads = width // HD
    for h in range(heads):
        span = slice(h * HD, (h + 1) * HD)
        acc[span, :] = acc[span, :] / total[h : h + 1, :]
    out_ref[...] = acc[...].T.astype(BF)
    log_ref[...] = top[...] + jnp.log(jnp.maximum(total[...], 1e-37))


def attend_forward(bounds, qkv, other, row_info, key_info):
    rows, width = qkv.shape[0], qkv.shape[1] // 3
    keys = 2 * rows
    stat_rows = 16
    return pl.pallas_call(
        attend_forward_kernel,
        name="attend_forward",
        grid_spec=pltpu.PrefetchScalarGridSpec(
            num_scalar_prefetch=1,
            grid=(rows // QT,),
            in_specs=[
                pl.BlockSpec((QT, 3 * width), lambda i, b: (i, 0)),
                pl.BlockSpec(memory_space=pl.ANY),
                pl.BlockSpec(memory_space=pl.ANY),
                pl.BlockSpec((8, QT), lambda i, b: (0, i)),
                pl.BlockSpec((keys, 1), lambda i, b: (0, 0), pipeline_mode=pl.Buffered(1)),
            ],
            out_specs=[
                pl.BlockSpec((QT, width), lambda i, b: (i, 0)),
                pl.BlockSpec((stat_rows, QT), lambda i, b: (0, i)),
            ],
            scratch_shapes=[
                pltpu.VMEM((width // PAIR, 2 * QT, PAIR), BF),
                pltpu.VMEM((keys, 2 * width), BF),
                pltpu.VMEM((keys // KT, width, KT), BF),
                pltpu.VMEM((KT, QT), F32),
                pltpu.VMEM((stat_rows, QT), F32),
                pltpu.VMEM((stat_rows, QT), F32),
                pltpu.VMEM((width, QT), F32),
                pltpu.VMEM((width // PAIR, KT, 2 * QT), F32),
                pltpu.VMEM((stat_rows, QT), F32),
                pltpu.VMEM((width // HD, KT, QT), BF),
                pltpu.SemaphoreType.DMA((2, keys // KT)),
            ],
        ),
        out_shape=[
            jax.ShapeDtypeStruct((rows, width), BF),
            jax.ShapeDtypeStruct((stat_rows, rows), F32),
        ],
        compiler_params=params_of(),
    )(bounds, qkv, qkv, other, row_info, key_info)


def attend_backward_kernel(
    bounds, q_ref, qkv_ref, other_ref, row_info, key_info, out_ref, log_ref, grad_ref,
    dq_ref, dkv_ref, q_pairs, g_pairs, kv_ref, k_turned, bias, inner, dq_acc, dkv_acc,
    scores, changes, probs, grads, sems,
):
    step = pl.program_id(0)
    rows, width = out_ref.shape
    pairs = width // PAIR
    tiles = kv_ref.shape[0] // KT

    @pl.when(step == 0)
    def _():
        def turn(j):
            for p in range(pairs):
                span = slice(p * PAIR, (p + 1) * PAIR)
                k_turned[j, span, :] = kv_ref[pl.ds(pl.multiple_of(j * KT, KT), KT), k_lanes(p, pairs)].T

        fetch_keys(bounds[0, 0], bounds[pl.num_programs(0) - 1, 1], qkv_ref, other_ref, kv_ref, sems, turn)
        dkv_acc[...] = jnp.zeros_like(dkv_acc)

    masked_pairs(q_ref, q_pairs, partial(q_lanes, pairs=pairs), pairs, HD**-0.5)
    masked_pairs(grad_ref, g_pairs, lambda p: slice(p * PAIR, (p + 1) * PAIR), pairs, None)
    dq_acc[...] = (out_ref[...].astype(F32) * grad_ref[...].astype(F32)).T
    for h in range(2 * pairs):
        inner[h : h + 1, :] = jnp.sum(dq_acc[h * HD : (h + 1) * HD, :], axis=0, keepdims=True)
    dq_acc[...] = jnp.zeros_like(dq_acc)
    q_first = bounds[step, 2]

    @pl.loop(bounds[step, 0], bounds[step, 1])
    def _(j):
        tile_bias(j, q_first, row_info, key_info, bias)
        here = pl.ds(pl.multiple_of(j * KT, KT), KT)
        for p in range(pairs):
            scores[p] = nt(kv_ref[here, k_lanes(p, pairs)], q_pairs[p])
            changes[p] = nt(kv_ref[here, v_lanes(p, pairs)], g_pairs[p])
        for h in range(2 * pairs):
            p, e = divmod(h, 2)
            cols = slice(e * rows, (e + 1) * rows)
            prob = jnp.exp(scores[p, :, cols] + bias[...] - log_ref[h : h + 1, :])
            probs[p, :, cols] = prob.astype(BF)
            grads[p, :, cols] = (prob * (changes[p, :, cols] - inner[h : h + 1, :])).astype(BF)
        for p in range(pairs):
            dkv_acc[here, k_lanes(p, pairs)] += nn(grads[p], q_pairs[p])
            dkv_acc[here, v_lanes(p, pairs)] += nn(probs[p], g_pairs[p])
        for h in range(2 * pairs):
            p, e = divmod(h, 2)
            span = slice(h * HD, (h + 1) * HD)
            dq_acc[span, :] += nn(k_turned[j, span, :], grads[p, :, e * rows : (e + 1) * rows])

    dq_ref[...] = (dq_acc[...] * HD**-0.5).T.astype(BF)

    @pl.when(step == pl.num_programs(0) - 1)
    def _():
        dkv_ref[...] = dkv_acc[...].astype(BF)


def attend_backward(bounds, qkv, other, row_info, key_info, attn, logs, grad_attn):
    rows, width = attn.shape
    keys = 2 * rows
    stat_rows = logs.shape[0]
    whole = dict(pipeline_mode=pl.Buffered(1))
    return pl.pallas_call(
        attend_backward_kernel,
        name="attend_backward",
        grid_spec=pltpu.PrefetchScalarGridSpec(
            num_scalar_prefetch=1,
            grid=(rows // QT,),
            in_specs=[
                pl.BlockSpec((QT, 3 * width), lambda i, b: (i, 0)),
                pl.BlockSpec(memory_space=pl.ANY),
                pl.BlockSpec(memory_space=pl.ANY),
                pl.BlockSpec((8, QT), lambda i, b: (0, i)),
                pl.BlockSpec((keys, 1), lambda i, b: (0, 0), **whole),
                pl.BlockSpec((QT, width), lambda i, b: (i, 0)),
                pl.BlockSpec((stat_rows, QT), lambda i, b: (0, i)),
                pl.BlockSpec((QT, width), lambda i, b: (i, 0)),
            ],
            out_specs=[
                pl.BlockSpec((QT, width), lambda i, b: (i, 0)),
                pl.BlockSpec((keys, 2 * width), lambda i, b: (0, 0), **whole),
            ],
            scratch_shapes=[
                pltpu.VMEM((width // PAIR, 2 * QT, PAIR), BF),
                pltpu.VMEM((width // PAIR, 2 * QT, PAIR), BF),
                pltpu.VMEM((keys, 2 * width), BF),
                pltpu.VMEM((keys // KT, width, KT), BF),
                pltpu.VMEM((KT, QT), F32),
                pltpu.VMEM((stat_rows, QT), F32),
                pltpu.VMEM((width, QT), F32),
                pltpu.VMEM((keys, 2 * width), F32),
                pltpu.VMEM((width // PAIR, KT, 2 * QT), F32),
                pltpu.VMEM((width // PAIR, KT, 2 * QT), F32),
                pltpu.VMEM((width // PAIR, KT, 2 * QT), BF),
                pltpu.VMEM((width // PAIR, KT, 2 * QT), BF),
                pltpu.SemaphoreType.DMA((2, keys // KT)),
            ],
        ),
        out_shape=[
            jax.ShapeDtypeStruct((rows, width), BF),
            jax.ShapeDtypeStruct((keys, 2 * width), BF),
        ],
        compiler_params=params_of(),
    )(bounds, qkv, qkv, other, row_info, key_info, attn, logs, grad_attn)


def attention_plan(segment_ids, pad_mask, random_blocks, global_blocks, rows):
    seq_count, nblocks = random_blocks.shape[0], random_blocks.shape[1]
    seq_len = segment_ids.shape[0] // seq_count
    rank = lax.axis_index("tensor")
    seq, half = rank // 2, lax.rem(rank, 2)
    segs = lax.dynamic_index_in_dim(segment_ids.reshape(seq_count, seq_len), seq, 0, False)
    pads = lax.dynamic_index_in_dim(pad_mask.reshape(seq_count, seq_len), seq, 0, False)
    randoms = lax.dynamic_index_in_dim(random_blocks, seq, 0, False)
    globs = lax.dynamic_index_in_dim(global_blocks, seq, 0, False)
    block_size = seq_len // nblocks
    one = jnp.int32(1)
    block = jnp.arange(nblocks, dtype=jnp.int32)

    def either(a, b):
        return jnp.bitwise_or(a, b)

    block_bits = lax.shift_left(one, block)
    window = either(
        block_bits,
        either(
            jnp.where(block > 0, lax.shift_left(one, jnp.maximum(block - 1, 0)), 0),
            jnp.where(
                block < nblocks - 1, lax.shift_left(one, jnp.minimum(block + 1, nblocks - 1)), 0
            ),
        ),
    )
    for r in range(randoms.shape[1]):
        window = either(window, lax.shift_left(one, randoms[:, r]))
    glob_bits = either(lax.shift_left(one, globs[:, 0]), lax.shift_left(one, globs[:, 1]))
    first = half * rows
    seg_q = lax.dynamic_slice_in_dim(segs, first, rows)
    own_bits = lax.dynamic_slice_in_dim(window, half * (rows // block_size), rows // block_size)
    bits = jnp.broadcast_to(own_bits[:, None], (rows // block_size, block_size)).reshape(rows)
    numbers = jnp.arange(globs.shape[0], dtype=jnp.int32)
    is_doc = seg_q[None, :] == numbers[:, None]
    bits = either(bits, jnp.sum(jnp.where(is_doc, glob_bits[:, None], 0), axis=0))
    row_info = jnp.concatenate(
        [seg_q[None], bits[None], jnp.zeros((6, rows), jnp.int32)], axis=0
    )
    key_info = jnp.where(pads == 1, segs, -2)[:, None]
    tiles = seg_q.reshape(rows // QT, QT)
    low = jnp.sum((segs[None, :] < tiles[:, :1]).astype(jnp.int32), axis=1)
    high = jnp.sum((segs[None, :] <= tiles[:, -1:]).astype(jnp.int32), axis=1)
    starts = first + QT * jnp.arange(rows // QT, dtype=jnp.int32)
    bounds = jnp.stack([low // KT, (high + KT - 1) // KT, starts, starts], axis=1)
    return bounds, row_info, key_info


TAIL_STEP = 0.47
TAIL = (0.266306628, 0.248031891, 0.336199252, -0.126105651, 0.607561554, -0.420410983, 0.0884173167)


def gelu_and_slope(pre):
    bell = jnp.exp(-0.5 * pre * pre)
    t = 1.0 / (1.0 + (TAIL_STEP * 0.5**0.5) * jnp.abs(pre))
    tail = TAIL[-1]
    for c in TAIL[-2::-1]:
        tail = tail * t + c
    tail = 0.5 * (tail * t) * bell
    cdf = jnp.where(pre < 0, tail, 1.0 - tail)
    return pre * cdf, cdf + pre * (bell * (2.0 * 3.141592653589793) ** -0.5)


def normalize(resid):
    center = resid - jnp.mean(resid, axis=1, keepdims=True)
    inverse = lax.rsqrt(jnp.mean(center * center, axis=1, keepdims=True) + EPSILON)
    return center * inverse, inverse


def norm_backward(grad_normed, normal_hat, inverse, gain):
    grad_hat = grad_normed * gain
    return inverse * (
        grad_hat
        - jnp.mean(grad_hat, axis=1, keepdims=True)
        - normal_hat * jnp.mean(grad_hat * normal_hat, axis=1, keepdims=True)
    )


def middle_kernel(
    x_ref, attn_ref, cot_ref, w_ref, blocks_ref, vec_ref,
    final_ref, first_grad, attn_grad, norm_low, unit_grad, proj_grad, out_grad,
    sums, unit_sums, slope, hidden, outer,
):
    width = x_ref.shape[1]
    third = width // 2
    wide = w_ref.shape[2] // 2
    proj_cols = [slice((y + 1) * wide - third, (y + 1) * wide) for y in range(2)]
    halves = [slice(y * third, (y + 1) * third) for y in range(2)]
    own_units = blocks_ref.shape[3] // 2
    chunks = [(t, slice(t * own_units, (t + 1) * own_units)) for t in range(blocks_ref.shape[1])]

    def w_in(t):
        return blocks_ref[:, t, :, :own_units].reshape(width, own_units)

    def w_out(t):
        return blocks_ref[:, t, :, own_units:].reshape(width, own_units)

    out_bias, last_bias, gain_1, shift_1, gain_2, shift_2 = (vec_ref[i : i + 1, :] for i in range(2, 8))

    @pl.when(pl.program_id(0) == 0)
    def _():
        sums[...] = jnp.zeros_like(sums)
        unit_sums[...] = jnp.zeros_like(unit_sums)
        outer[...] = jnp.zeros_like(outer)

    resid = x_ref[...].astype(F32) + out_bias
    for y in range(2):
        resid += nt(attn_ref[:, halves[y]], w_ref[0, :, proj_cols[y]])
    hat_1, inverse_1 = normalize(resid)
    first_norm = hat_1 * gain_1 + shift_1
    low = first_norm.astype(BF)
    norm_low[...] = low
    resid = first_norm + last_bias
    for t, cols in chunks:
        act, slope[:, cols] = gelu_and_slope(nn(low, w_in(t)) + vec_ref[8 + t : 9 + t, :own_units])
        act = act.astype(BF)
        hidden[:, cols] = act
        resid += nt(act, w_out(t))
    hat_2, inverse_2 = normalize(resid)
    final_ref[...] = (hat_2 * gain_2 + shift_2).astype(BF)

    cot = cot_ref[...].astype(F32)
    grad = norm_backward(cot, hat_2, inverse_2, gain_2)
    sums[6:7, :] += jnp.sum(cot * hat_2, axis=0, keepdims=True)
    sums[7:8, :] += jnp.sum(cot, axis=0, keepdims=True)
    sums[3:4, :] += jnp.sum(grad, axis=0, keepdims=True)
    low = grad.astype(BF)
    turned = low.T
    for t, cols in chunks:
        outer[t] += nn(turned, hidden[:, cols])
        act = (nn(low, w_out(t)) * slope[:, cols]).astype(BF)
        unit_grad[:, cols] = act
        unit_sums[0:1, cols] += jnp.sum(act.astype(F32), axis=0, keepdims=True)
        grad += nt(act, w_in(t))
    sums[4:5, :] += jnp.sum(grad * hat_1, axis=0, keepdims=True)
    sums[5:6, :] += jnp.sum(grad, axis=0, keepdims=True)
    grad = norm_backward(grad, hat_1, inverse_1, gain_1)
    sums[2:3, :] += jnp.sum(grad, axis=0, keepdims=True)
    first_grad[...] = grad
    low = grad.astype(BF)
    proj_grad[...] = low
    for y in range(2):
        attn_grad[:, halves[y]] = nn(low, w_ref[0, :, proj_cols[y]]).astype(BF)

    @pl.when(pl.program_id(0) == pl.num_programs(0) - 1)
    def _():
        for t, _ in chunks:
            out_grad[:, t] = outer[t].reshape(out_grad.shape[0], out_grad.shape[2], own_units).astype(BF)


def middle(layer_in, attn, output_grad, weights, blocks, vectors):
    rows, width = layer_in.shape
    units = blocks.shape[1] * blocks.shape[3] // 2
    tile = lambda w: pl.BlockSpec((ROWS, w), lambda i: (i, 0))
    whole = lambda a: pl.BlockSpec(a.shape, lambda i: (0,) * len(a.shape), pipeline_mode=pl.Buffered(1))
    fixed = lambda w: pl.BlockSpec((8, w), lambda i: (0, 0))
    shape = lambda w, t: jax.ShapeDtypeStruct((rows, w), t)
    out_grad = jax.ShapeDtypeStruct(blocks.shape[:3] + (blocks.shape[3] // 2,), BF)
    out_spec = pl.BlockSpec(out_grad.shape, lambda i: (0, 0, 0, 0), pipeline_mode=pl.Buffered(1))
    return pl.pallas_call(
        middle_kernel,
        name="middle",
        grid=(rows // ROWS,),
        in_specs=[tile(width)] * 3 + [whole(weights), whole(blocks), whole(vectors)],
        out_specs=[tile(width)] * 4 + [tile(units), tile(width), out_spec, fixed(width), fixed(units)],
        out_shape=[
            shape(width, BF), shape(width, F32), shape(width, BF), shape(width, BF), shape(units, BF), shape(width, BF),
            out_grad,
            jax.ShapeDtypeStruct((8, width), F32), jax.ShapeDtypeStruct((8, units), F32),
        ],
        scratch_shapes=[
            pltpu.VMEM((ROWS, units), F32),
            pltpu.VMEM((ROWS, units), BF),
            pltpu.VMEM((blocks.shape[1], width, units // blocks.shape[1]), F32),
        ],
        compiler_params=params_of(),
    )(layer_in, attn, output_grad, weights, blocks, vectors)


def finish_kernel(
    n, x_hbm, dq_hbm, dkv_hbm, w_hbm, first_hbm, low_hbm, unit_hbm, proj_hbm, attn_hbm, sums_ref, unit_sums,
    input_hbm, q_out, k_out, v_out, o_out, in_out, vec_out,
    rows_in, turned, unit, d_qkv, attn, far, w_all, tile_in, tile_out, grads, sib, from_b, from_a, from_low, from_high,
    result, vec_sent, vec_got,
    load, swap_s, swap_r, ss, sr, bs, br, as_, ar, zs, zr, es, er, vs, vr, tile_sem,
):
    w = places()
    dp, rank, core, y, z, x = (w[k] for k in ("dp", "rank", "core", "y", "z", "x"))
    rows, width = x_hbm.shape
    third = width // 2
    wide = unit.shape[1] // 2
    slab = result.shape[1] // 2
    up, down = {"dp": lax.rem(dp + 2, 2 * n), "tensor": rank}, {"dp": lax.rem(dp + 2 * n - 2, 2 * n), "tensor": rank}
    partners = [w["sibling"], w["second"], w["first"]] + line_jumps(dp, rank, z, n)
    barrier = pltpu.get_barrier_semaphore()
    for other in partners + [up, down]:
        pl.semaphore_signal(barrier, inc=1, device_id=other, device_id_type=MESH)

    def fetch(i, src, dst):
        return pltpu.make_async_copy(src, dst, load.at[i])

    fetch_low = fetch(0, low_hbm, rows_in.at[0])
    fetch_unit = fetch(1, unit_hbm, unit)
    fetch_x = fetch(2, x_hbm, rows_in.at[1])
    fetch_proj = fetch(3, proj_hbm, rows_in.at[2])
    fetch_attn = fetch(4, attn_hbm, attn)
    fetch_w = fetch(5, w_hbm.at[0], w_all)
    fetch_dq = [fetch(6 + h, dq_hbm.at[:, h * third : (h + 1) * third], d_qkv.at[:, 3 * h * third : (3 * h + 1) * third]) for h in range(2)]
    fetch_kv = [fetch(8 + h, dkv_hbm.at[core, :, 2 * h * third : 2 * (h + 1) * third], d_qkv.at[:, (3 * h + 1) * third : (3 * h + 3) * third]) for h in range(2)]
    for move in [fetch_low, fetch_unit, fetch_x, fetch_proj, fetch_attn] + fetch_dq + fetch_kv + [fetch_w]:
        move.start()
    pl.semaphore_wait(barrier, len(partners) + 2)

    def copy(src, dst, ssem, rsem, dev):
        return pltpu.make_async_remote_copy(src, dst, ssem, rsem, device_id=dev, device_id_type=MESH)

    swap = copy(dkv_hbm.at[1 - core], far, swap_s, swap_r, w["sibling"])
    swap.start()

    def turn_rows(i):
        for c in range(0, width, 128):
            turned[i, c : c + 128, :] = rows_in[i, :, c : c + 128].T

    places_of = [xd * 2 + yd for xd, yd in (
        (x, y), (w["xa"], w["ya"]), (w["xb"], w["yb"]), (w["xa"] + w["xb"] - x, w["ya"] + w["yb"] - y))]
    mine = grads.at[core]

    def keep(k, zd, yd, lane, value):
        for xd in range(2):
            for c in range(2):
                first = (xd * 2 + c) * slab
                grads[c, k, zd, xd * 2 + yd, :, lane : lane + value.shape[1]] = value[first : first + slab, :].astype(BF)

    def rows_of_line(i, zd):
        return turned[i, pl.ds(pl.multiple_of(zd * 4 * slab, 4 * slab), 4 * slab), :]

    def compute_inner(zd):
        left = rows_of_line(0, zd)
        for yd in range(2):
            for lane in range(0, wide, 768):
                keep(1, zd, yd, lane, nn(left, unit[:, yd * wide + lane : yd * wide + lane + 768]))

    def compute_others(zd):
        left = rows_of_line(1, zd)
        for yd in range(2):
            for i in range(3):
                at = (3 * yd + i) * third
                keep(0, zd, yd, i * third, nn(left, d_qkv[:, at : at + third]))
        left = rows_of_line(2, zd)
        for yd in range(2):
            keep(0, zd, yd, 3 * third, nn(left, attn[:, yd * third : (yd + 1) * third]))

    def to_sibling(k, zd):
        return copy(grads.at[1 - core, k, zd], sib.at[k, zd], ss.at[k, zd], sr.at[k, zd], w["sibling"])

    def over_b(k, far_side, zd):
        place = places_of[2 + far_side]
        return copy(mine.at[k, zd, place], from_b.at[k, far_side, zd], bs.at[k, far_side, zd], br.at[k, far_side, zd], w["second"])

    def over_a(k, zd):
        return copy(mine.at[k, zd, places_of[1]], from_a.at[k, zd], as_.at[k, zd], ar.at[k, zd], w["first"])

    def over_up(k, zd):
        return copy(mine.at[k, zd, places_of[0]], from_low.at[k, zd], zs.at[k, zd], zr.at[0, k, zd], up)

    def over_down(k, zd):
        return copy(mine.at[k, zd, places_of[0]], from_high.at[k, zd], zs.at[k, zd], zr.at[1, k, zd], down)

    def put(q, k, zd, more):
        place = places_of[q]
        total = grads[core, k, zd, place].astype(F32) + sib[k, zd, place].astype(F32)
        for term in more:
            total = total + term[...].astype(F32)
        grads[core, k, zd, place] = total.astype(BF)

    def stage_b(k, zd):
        to_sibling(k, zd).wait_recv()
        for far_side in (1, 0):
            put(2 + far_side, k, zd, ())
            over_b(k, far_side, zd).start()

    def stage_a(k, zd):
        over_b(k, 1, zd).wait_recv()
        put(1, k, zd, (from_b.at[k, 1, zd],))
        over_a(k, zd).start()

    def stage_line(k, zd):
        over_b(k, 0, zd).wait_recv()
        over_a(k, zd).wait_recv()
        put(0, k, zd, (from_b.at[k, 0, zd], from_a.at[k, zd]))

        @pl.when((zd > z) & (z == 0))
        def _():
            over_up(k, zd).start()

        @pl.when((zd < z) & (z == n - 1))
        def _():
            over_down(k, zd).start()

    def grow(k, zd, term):
        place = places_of[0]
        grads[core, k, zd, place] = (grads[core, k, zd, place].astype(F32) + term[...].astype(F32)).astype(BF)

    def stage_hop(k, zd):
        @pl.when((zd > z) & (z > 0))
        def _():
            over_up(k, zd).wait_recv()
            grow(k, zd, from_low.at[k, zd])
            over_up(k, zd).start()

        @pl.when((zd < z) & (z < n - 1))
        def _():
            over_down(k, zd).wait_recv()
            grow(k, zd, from_high.at[k, zd])
            over_down(k, zd).start()

    def turn(i):
        below, above = z, n - 1 - z
        near = jnp.minimum(below, above)
        only = jnp.maximum(below, above) - near
        side = jnp.where(above >= below, 1, -1)
        distance = jnp.where(i < only, only + near - i, near - (i - only) // 2)
        sign = jnp.where(i < only, side, jnp.where(lax.rem(i - only, 2) == 0, side, -side))
        return jnp.where(i == n - 1, z, z + sign * distance)

    def item(j):
        return 1 - j // n, turn(lax.rem(j, n))

    def small_send(step):
        return copy(vec_sent.at[step], vec_got.at[step], vs.at[step], vr.at[step], partners[step])

    def input_tile(t):
        at = pl.ds(pl.multiple_of(t * ROWS, ROWS), ROWS)
        return (pltpu.make_async_copy(first_hbm.at[at, :], tile_in.at[lax.rem(t, 2)], tile_sem.at[0, lax.rem(t, 2)]),
                pltpu.make_async_copy(tile_out.at[lax.rem(t, 2)], input_hbm.at[at, :], tile_sem.at[1, lax.rem(t, 2)]), at)

    def input_grad(t):
        into, out, at = input_tile(t)
        into.start()
        total = nt(d_qkv[at, : 3 * third], w_all[:, : 3 * third])
        total += nt(d_qkv[at, 3 * third :], w_all[:, wide : wide + 3 * third])
        into.wait()
        tile_out[lax.rem(t, 2)] = tile_in[lax.rem(t, 2)] + total
        out.start()

    tiles = rows // ROWS
    last_item = 2 * n

    fetch_low.wait()
    turn_rows(0)
    fetch_unit.wait()

    @pl.loop(0, last_item + 4)
    def _(j):
        @pl.when(j < n)
        def _():
            k, zd = item(j)
            compute_inner(zd)
            to_sibling(1, zd).start()

        @pl.when(j == n - 1)
        def _():
            fetch_x.wait()
            fetch_proj.wait()
            fetch_attn.wait()
            turn_rows(1)
            turn_rows(2)
            for move in fetch_dq + fetch_kv:
                move.wait()
            swap.wait_recv()
            for h in range(2):
                at = slice((3 * h + 1) * third, (3 * h + 3) * third)
                d_qkv[:, at] = (d_qkv[:, at].astype(F32) + far[:, 2 * h * third : 2 * (h + 1) * third].astype(F32)).astype(BF)
            vec_sent[0] = jnp.zeros_like(vec_sent[0])
            vec_sent[0, 2:8, :] = sums_ref[2:8, :]
            for h in range(2):
                for row, i in ((0, 0), (1, 2)):
                    cols = d_qkv[:, (3 * h + i) * third : (3 * h + i + 1) * third].astype(F32)
                    vec_sent[0, row : row + 1, h * third : (h + 1) * third] = jnp.sum(cols, axis=0, keepdims=True)
            for u in range(unit_sums.shape[1] // width):
                vec_sent[0, 8 + u : 9 + u, :] = unit_sums[0:1, u * width : (u + 1) * width]
            small_send(0).start()
            fetch_w.wait()

        @pl.when((j >= n) & (j < last_item))
        def _():
            k, zd = item(j)
            compute_others(zd)
            to_sibling(0, zd).start()

        @pl.when((j >= 1) & (j < last_item + 1))
        def _():
            stage_b(*item(j - 1))

        @pl.when((j >= 2) & (j < last_item + 2))
        def _():
            stage_a(*item(j - 2))

        @pl.when((j >= 3) & (j < last_item + 3))
        def _():
            stage_line(*item(j - 3))

        @pl.when(j >= 4)
        def _():
            stage_hop(*item(j - 4))

        for step in range(len(partners)):
            @pl.when(j == n + step)
            def _(step=step):
                small_send(step).wait_recv()
                vec_sent[step + 1] = vec_sent[step] + vec_got[step]
                if step + 1 < len(partners):
                    small_send(step + 1).start()

        @pl.when((j >= last_item - tiles) & (j < last_item))
        def _():
            t = j - (last_item - tiles)

            @pl.when(t >= 2)
            def _():
                input_tile(t - 2)[1].wait()
            input_grad(t)

    vec_out[...] = vec_sent[len(partners)]
    own = pl.ds(pl.multiple_of(core * slab, slab), slab)
    theirs = pl.ds(pl.multiple_of((1 - core) * slab, slab), slab)
    for k in (1, 0):
        result[k, own, :] = grads[core, k, z, places_of[0]].astype(F32)

        @pl.when(z > 0)
        def _():
            over_up(k, z).wait_recv()
            result[k, own, :] += from_low[k, z].astype(F32)

        @pl.when(z < n - 1)
        def _():
            over_down(k, z).wait_recv()
            result[k, own, :] += from_high[k, z].astype(F32)

        copy(result.at[k, own, :], result.at[k, own, :], es.at[k], er.at[k], w["sibling"]).start()
    for t in range(max(tiles - 2, 0), tiles):
        input_tile(t)[1].wait()
    swap.wait_send()
    for step in range(len(partners)):
        small_send(step).wait_send()

    @pl.loop(0, n)
    def _(zd):
        for k in range(2):
            to_sibling(k, zd).wait_send()
            over_b(k, 0, zd).wait_send()
            over_b(k, 1, zd).wait_send()
            over_a(k, zd).wait_send()

            @pl.when(zd > z)
            def _():
                over_up(k, zd).wait_send()

            @pl.when(zd < z)
            def _():
                over_down(k, zd).wait_send()
    for k in (1, 0):
        copy(result.at[k, theirs, :], result.at[k, theirs, :], es.at[k], er.at[k], w["sibling"]).wait()

    def chosen(k, lane, w_own):
        both = result[k, :, lane : lane + 2 * w_own]
        return jnp.where(core == 0, both[:, :w_own], both[:, w_own:])

    for i, out in enumerate((q_out, k_out, v_out, o_out)):
        out[...] = chosen(0, i * third, third // 2)
    in_out[...] = chosen(1, 0, wide // 2)


def finish(layer_in, dq, dkv, weights, grad_first, norm_low, unit_grad, proj_grad, attn, sums, unit_sums):
    rows, width = layer_in.shape
    units = unit_grad.shape[1]
    dp, tp = lax.axis_size("dp"), lax.axis_size("tensor")
    n = dp // 2
    block = width // dp
    slab, wide, third = block // 2, units // 2, width // 2
    steps = 3 + (n - 1).bit_length()
    dma = pltpu.SemaphoreType.DMA
    slabs = lambda *lead: pltpu.VMEM(lead + (slab, wide), BF)
    anywhere, inside = pl.BlockSpec(memory_space=pl.ANY), pl.BlockSpec(memory_space=pltpu.VMEM)
    result = lambda *shape: jax.ShapeDtypeStruct(shape, F32)
    return pl.pallas_call(
        partial(finish_kernel, n),
        name="finish",
        in_specs=[anywhere] * 9 + [inside] * 2,
        out_specs=[anywhere] + [inside] * 6,
        out_shape=[result(rows, width)] + [result(block, third // 2)] * 4 + [result(block, wide // 2), result(16, width)],
        scratch_shapes=[
            pltpu.VMEM((3, rows, width), BF),
            pltpu.VMEM((3, width, rows), BF),
            pltpu.VMEM((rows, units), BF),
            pltpu.VMEM((rows, 3 * width), BF),
            pltpu.VMEM((rows, width), BF),
            pltpu.VMEM((rows, 2 * width), BF),
            pltpu.VMEM((width, units), BF),
            pltpu.VMEM((2, ROWS, width), F32),
            pltpu.VMEM((2, ROWS, width), F32),
            slabs(2, 2, n, 4),
            slabs(2, n, 4),
            slabs(2, 2, n),
            slabs(2, n),
            slabs(2, n),
            slabs(2, n),
            pltpu.VMEM((2, block, wide), F32),
            pltpu.VMEM((steps + 1, 16, width), F32),
            pltpu.VMEM((steps, 16, width), F32),
            dma((10,)), dma(()), dma(()),
            dma((2, n)), dma((2, n)), dma((2, 2, n)), dma((2, 2, n)), dma((2, n)), dma((2, n)),
            dma((2, n)), dma((2, 2, n)), dma((2,)), dma((2,)), dma((steps,)), dma((steps,)), dma((2, 2)),
        ],
        compiler_params=pltpu.CompilerParams(
            collective_id=4, has_side_effects=True, vmem_limit_bytes=60 * 2**20
        ),
    )(layer_in, dq, dkv.reshape(2, rows, 2 * width), weights, grad_first, norm_low, unit_grad, proj_grad, attn, sums, unit_sums)


def finish_plainly(layer_in, dq, dkv, weights, grad_first, norm_low, unit_grad, proj_grad, attn, sums, unit_sums):
    rows, width = layer_in.shape
    units = unit_grad.shape[1]
    dp, tp = lax.axis_size("dp"), lax.axis_size("tensor")
    third, block, pairs = width // 2, width // dp, tp // 2
    half = lax.rem(lax.axis_index("tensor"), 2)
    both = dkv.reshape(2, rows, 2 * width)
    far = swap_pair(both)
    near = lax.dynamic_index_in_dim(both, half, 0, False)
    own = (near.astype(F32) + far.astype(F32)).astype(BF)
    d_qkv = jnp.concatenate([dq[:, :third], own[:, :width], dq[:, third:], own[:, width:]], axis=1)
    wqkv = weights[0].reshape(width, 2, 4 * third)[:, :, : 3 * third].reshape(width, 3 * width)
    input_grad = grad_first + nt(d_qkv, wqkv)
    grads = [g.astype(BF) for g in (tn(layer_in, d_qkv), tn(proj_grad, attn), tn(norm_low, unit_grad))]
    joined = jnp.concatenate([g.reshape(width, pairs, -1) for g in grads[:2]], axis=2)
    every = jnp.stack([joined.reshape(width, units), grads[2]])
    every = every.reshape(2, dp, block, pairs, 1, units // pairs).transpose(1, 3, 4, 0, 2, 5)
    every = jnp.broadcast_to(every, (dp, pairs, 2, 2, block, units // pairs))
    total = lax.psum_scatter(
        every.reshape(dp * tp, 2, block, units // pairs), ("dp", "tensor"), scatter_dimension=0, tiled=False
    ).astype(F32)
    d_bias = jnp.sum(d_qkv.astype(F32), axis=0).reshape(2, 3, third)
    vec = jnp.concatenate(
        [d_bias[:, 0].reshape(1, width), d_bias[:, 2].reshape(1, width), sums[2:],
         unit_sums[0].reshape(-1, width), jnp.zeros((8 - units // width, width), F32)], axis=0,
    )
    vec = lax.psum(vec, ("dp", "tensor"))

    def chosen(k, lane, w_own):
        return lax.dynamic_slice_in_dim(total[k], lane + half * w_own, w_own, axis=1)

    return (input_grad,) + tuple(chosen(0, i * third, third // 2) for i in range(4)) + (
        chosen(1, 0, units // tp), vec)


def on_device(
    layer_in, query_weight, key_weight, value_weight, output_weight, inner_weight, outer_weight,
    query_bias, value_bias, output_bias, inner_bias, outer_bias, first_gain, first_shift,
    second_gain, second_shift, segment_ids, pad_mask, random_blocks, global_blocks, output_grad,
):
    rows, width = layer_in.shape
    dp, tp = lax.axis_size("dp"), lax.axis_size("tensor")
    own_rows, own_cols = query_weight.shape
    own_units = inner_weight.shape[1]
    third = width // 2
    half = lax.rem(lax.axis_index("tensor"), 2)

    def beside(own):
        zero = jnp.zeros_like(own)
        return jnp.concatenate(
            [jnp.where(half == 0, own, zero), jnp.where(half == 0, zero, own)], axis=1
        )

    units_own = jnp.concatenate([inner_weight, outer_weight.T], axis=1)
    blocks = lax.all_gather(units_own, ("dp", "tensor"), axis=0, tiled=False)
    blocks = blocks.reshape(dp, tp, own_rows, 2 * own_units)
    mine = jnp.concatenate(
        [beside(w) for w in (query_weight, key_weight, value_weight, output_weight.T)], axis=1
    )[None]
    place = lax.axis_index("dp") * tp + lax.axis_index("tensor")
    one, own_bias = query_bias.shape[0], inner_bias.shape[0]
    small = jnp.stack([query_bias, value_bias, output_bias, outer_bias, first_gain, first_shift,
                       second_gain, second_shift])
    eight = lax.dynamic_update_slice(jnp.zeros((8, width), F32), small, (0, place * one))
    unit = lax.dynamic_update_slice(jnp.zeros((8 * width,), F32), inner_bias, (place * own_bias,))
    vec = jnp.concatenate([eight, unit.reshape(8, width)], axis=0)
    begin = start if in_tiles(own_rows) else start_plainly
    weights, qkv, other, vectors = begin(mine, vec, layer_in)

    bounds, row_info, key_info = attention_plan(
        segment_ids, pad_mask, random_blocks, global_blocks, rows
    )
    attn, logs = attend_forward(bounds, qkv, other, row_info, key_info)
    (layer_out, grad_first, grad_attn, norm_low, unit_grad, proj_grad, out_grad, sums, unit_sums) = middle(
        layer_in, attn, output_grad, weights, blocks, vectors
    )
    d_outer = lax.psum_scatter(
        out_grad.reshape((dp * tp,) + out_grad.shape[2:]), ("dp", "tensor"), scatter_dimension=0, tiled=False
    )
    dq, dkv = attend_backward(bounds, qkv, other, row_info, key_info, attn, logs, grad_attn)
    end = finish if in_tiles(own_rows) else finish_plainly
    input_grad, d_q, d_k, d_v, d_o, d_inner, vec = end(
        layer_in, dq, dkv, weights, grad_first, norm_low, unit_grad, proj_grad, attn, sums, unit_sums
    )
    pieces = lax.dynamic_slice_in_dim(vec[:8], place * one, one, axis=1)
    (r_bq, r_bv, r_bo, r_bout, r_g1, r_s1, r_g2, r_s2) = (pieces[i] for i in range(8))
    d_bin = lax.dynamic_slice_in_dim(vec[8:].reshape(-1), place * own_bias, own_bias)
    return (
        layer_out, input_grad, d_q, d_k, d_v, d_o.T, d_inner, d_outer.astype(F32).T,
        r_bq, r_bv, r_bo, d_bin, r_bout, r_g1, r_s1, r_g2, r_s2,
    )


def solution(mesh):
    tokens = P(("dp", "tensor"), None)
    vector = P(("dp", "tensor"))
    cols, turned = P("dp", "tensor"), P("tensor", "dp")
    return jax.shard_map(
        on_device,
        mesh=mesh,
        in_specs=(tokens, cols, cols, cols, turned, cols, turned)
        + (vector,) * 9
        + (P("dp"), P("dp"), P("dp", None, None), P("dp", None, None), tokens),
        out_specs=(tokens, tokens, cols, cols, cols, turned, cols, turned) + (vector,) * 9,
        check_vma=False,
    )
```

```python
from functools import partial

import jax
import jax.numpy as jnp
from jax import lax
from jax.experimental import pallas as pl
from jax.experimental.pallas import tpu as pltpu
from jax.sharding import PartitionSpec as P

HD = 64
PAIR = 2 * HD
QT = 256
KT = 128
ROWS = 256
BACK_ROWS = 256
EPSILON = 1e-06
NEGATIVE = -1e30
MESH = pl.DeviceIdType.MESH
VMEM_LIMIT = 56 * 2**20
BF = jnp.bfloat16
F32 = jnp.float32


def params_of(collective_id=None):
    if collective_id is None:
        return pltpu.CompilerParams(vmem_limit_bytes=VMEM_LIMIT)
    return pltpu.CompilerParams(
        vmem_limit_bytes=VMEM_LIMIT, collective_id=collective_id, has_side_effects=True
    )


def nt(left, right, **more):
    return lax.dot_general(
        left, right, (((1,), (1,)), ((), ())), preferred_element_type=F32, **more
    )


def nn(left, right):
    return lax.dot_general(left, right, (((1,), (0,)), ((), ())), preferred_element_type=F32)


def tn(left, right):
    return lax.dot_general(left, right, (((0,), (0,)), ((), ())), preferred_element_type=F32)


def sibling_of():
    rank = lax.axis_index("tensor")
    half = lax.rem(rank, 2)
    return half, {"tensor": rank + 1 - 2 * half}


def meet(others):
    barrier = pltpu.get_barrier_semaphore()
    for other in others:
        pl.semaphore_signal(barrier, inc=1, device_id=other, device_id_type=MESH)
    pl.semaphore_wait(barrier, len(others))


def swap_keys_kernel(qkv_ref, other_ref, send_sem, recv_sem):
    half, sibling = sibling_of()
    meet([sibling])
    third = qkv_ref.shape[1] // 6
    moves = [
        pltpu.make_async_remote_copy(
            qkv_ref.at[:, (3 * y + 1) * third : (3 * y + 3) * third],
            other_ref.at[:, 2 * y * third : 2 * (y + 1) * third],
            send_sem.at[y], recv_sem.at[y], device_id=sibling, device_id_type=MESH,
        )
        for y in range(2)
    ]
    for move in moves:
        move.start()
    for move in moves:
        move.wait()


def swap_keys(qkv):
    rows, width = qkv.shape
    return pl.pallas_call(
        swap_keys_kernel,
        name="swap_keys",
        out_shape=jax.ShapeDtypeStruct((rows, width * 2 // 3), qkv.dtype),
        in_specs=[pl.BlockSpec(memory_space=pl.ANY)],
        out_specs=pl.BlockSpec(memory_space=pl.ANY),
        scratch_shapes=[pltpu.SemaphoreType.DMA((2,))] * 2,
        compiler_params=params_of(1),
    )(qkv)


def swap_pair_kernel(both_ref, other_ref, send_sem, recv_sem):
    half, sibling = sibling_of()
    meet([sibling])
    away = pltpu.make_async_remote_copy(
        both_ref.at[1 - half], other_ref, send_sem, recv_sem,
        device_id=sibling, device_id_type=MESH,
    )
    away.start()
    away.wait()


def swap_pair(both):
    return pl.pallas_call(
        swap_pair_kernel,
        name="swap_pair",
        out_shape=jax.ShapeDtypeStruct(both.shape[1:], both.dtype),
        in_specs=[pl.BlockSpec(memory_space=pl.ANY)],
        out_specs=pl.BlockSpec(memory_space=pl.ANY),
        scratch_shapes=[pltpu.SemaphoreType.DMA(())] * 2,
        compiler_params=params_of(2),
    )(both)


def places():
    dp, rank = lax.axis_index("dp"), lax.axis_index("tensor")
    core, y = lax.rem(rank, 2), rank // 2
    z, x = dp // 2, lax.rem(dp, 2)
    sibling = {"dp": dp, "tensor": rank + 1 - 2 * core}
    near_x = {"dp": dp + 1 - 2 * x, "tensor": rank}
    near_y = {"dp": dp, "tensor": rank + 2 - 4 * y}
    first = {"dp": dp + (1 - core) * (1 - 2 * x), "tensor": rank + core * (2 - 4 * y)}
    second = {"dp": dp + core * (1 - 2 * x), "tensor": rank + (1 - core) * (2 - 4 * y)}
    xa, ya = x + (1 - core) * (1 - 2 * x), y + core * (1 - 2 * y)
    xb, yb = x + core * (1 - 2 * x), y + (1 - core) * (1 - 2 * y)
    return dict(dp=dp, rank=rank, core=core, y=y, z=z, x=x, sibling=sibling, first=first, second=second,
                xa=xa, ya=ya, xb=xb, yb=yb)


def line_jumps(dp, rank, z, n):
    jumps, hop = [], 1
    while hop < n:
        bit = lax.rem(z // hop, 2)
        jumps.append({"dp": dp + 2 * hop * (1 - 2 * bit), "tensor": rank})
        hop *= 2
    return jumps


def start_kernel(
    n, mine_ref, vec_ref, x_ref, w_hbm, qkv_hbm, other_hbm, vec_out,
    out_ref, chip, sib, qkv, vec_sent, vec_got,
    local_sem, pair_sem, zs, zr, as_, ar, bs, br, ss, sr, ks, kr, vs, vr,
):
    w = places()
    dp, rank, core, y, z, x = (w[k] for k in ("dp", "rank", "core", "y", "z", "x"))
    block, wide = mine_ref.shape[1], mine_ref.shape[2]
    slab = block // 2
    up, down = {"dp": lax.rem(dp + 2, 2 * n), "tensor": rank}, {"dp": lax.rem(dp + 2 * n - 2, 2 * n), "tensor": rank}
    partners = [w["sibling"], w["second"], w["first"]] + line_jumps(dp, rank, z, n)
    meet([up, down] + partners)

    pair = pltpu.make_async_remote_copy(mine_ref, sib, pair_sem.at[0], pair_sem.at[1], device_id=w["sibling"], device_id_type=MESH)
    pair.start()

    def small_send(step):
        return pltpu.make_async_remote_copy(vec_sent.at[step], vec_got.at[step], vs.at[step], vr.at[step], device_id=partners[step], device_id_type=MESH)

    def small_step(step):
        small_send(step).wait_recv()
        vec_sent[step + 1] = vec_sent[step] + vec_got[step]
        if step + 1 < len(partners):
            small_send(step + 1).start()

    vec_sent[0] = vec_ref[...]
    small_send(0).start()
    pair.wait()
    chip[...] = mine_ref[...] + sib[...]
    rows_own = pl.ds(pl.multiple_of(core * slab, slab), slab)
    own_at = pl.ds(pl.multiple_of(dp * block, block), block)
    cols_own = pl.ds(pl.multiple_of(y * wide, wide), wide)
    keep = pltpu.make_async_copy(chip, out_ref.at[:, own_at, cols_own], local_sem.at[0])
    keep.start()

    def spot(g, zi, xi, yi):
        d = zi * 2 + xi
        rows = pl.ds(pl.multiple_of(d * block + core * slab, slab), slab)
        cols = pl.ds(pl.multiple_of(yi * wide, wide), wide)
        return out_ref.at[:, rows, cols]

    def own(g):
        return chip.at[:, rows_own, :]

    def move(g, zi, xi, yi, dev, ssem, rsem, source=None):
        at = spot(g, zi, xi, yi)
        return pltpu.make_async_remote_copy(at if source is None else source, at, ssem, rsem, device_id=dev, device_id_type=MESH)

    def line_up(g, s):
        return move(g, z - s, x, y, up, zs.at[g, 0, s], zr.at[g, 0, s], own(g) if s == 0 else None)

    def line_down(g, s):
        return move(g, z + s, x, y, down, zs.at[g, 1, s], zr.at[g, 1, s], own(g) if s == 0 else None)

    def to_first(g, zi, source=None):
        return move(g, zi, x, y, w["first"], as_.at[g, zi], ar.at[g, zi], source)

    def to_second(g, zi, far, source=None):
        xi, yi = (w["xa"], w["ya"]) if far else (x, y)
        return move(g, zi, xi, yi, w["second"], bs.at[g, far, zi], br.at[g, far, zi], source)

    def to_sibling(g, zi, quarter, source=None):
        xi = (x, w["xa"], w["xb"], w["xa"] + w["xb"] - x)[quarter]
        yi = (y, w["ya"], w["yb"], w["ya"] + w["yb"] - y)[quarter]
        return move(g, zi, xi, yi, w["sibling"], ss.at[g, quarter, zi], sr.at[g, quarter, zi], source)

    def begin(g):
        @pl.when(z < n - 1)
        def _():
            line_up(g, 0).start()

        @pl.when(z > 0)
        def _():
            line_down(g, 0).start()

        to_first(g, z, own(g)).start()
        to_second(g, z, 0, own(g)).start()

    def first_in(g, zi):
        got = move(g, zi, w["xa"], w["ya"], w["first"], as_.at[g, zi], ar.at[g, zi])
        got.wait_recv()
        to_second(g, zi, 1).start()
        to_sibling(g, zi, 1).start()

    def second_in(g, zi, far):
        q = 2 + far
        xi = (w["xb"], w["xa"] + w["xb"] - x)[far]
        yi = (w["yb"], w["ya"] + w["yb"] - y)[far]
        move(g, zi, xi, yi, w["second"], bs.at[g, far, zi], br.at[g, far, zi]).wait_recv()
        to_sibling(g, zi, q).start()

    def below_in(g, s):
        zi = z - 1 - s
        move(g, zi, x, y, up, zs.at[g, 0, s], zr.at[g, 0, s]).wait_recv()
        if s + 1 < n - 1:
            @pl.when(z < n - 1)
            def _():
                line_up(g, s + 1).start()
        to_first(g, zi).start()
        to_second(g, zi, 0).start()
        to_sibling(g, zi, 0).start()

    def above_in(g, s):
        zi = z + 1 + s
        move(g, zi, x, y, down, zs.at[g, 1, s], zr.at[g, 1, s]).wait_recv()
        if s + 1 < n - 1:
            @pl.when(z > 0)
            def _():
                line_down(g, s + 1).start()
        to_first(g, zi).start()
        to_second(g, zi, 0).start()
        to_sibling(g, zi, 0).start()

    def steps(gs):
        for g in gs:
            first_in(g, z)
        for s in range(n - 1):
            @pl.when(z - 1 - s >= 0)
            def _(s=s):
                for g in gs:
                    below_in(g, s)

            @pl.when(z + 1 + s < n)
            def _(s=s):
                for g in gs:
                    above_in(g, s)
            if s > 0:
                both(s, lambda g, zi: first_in(g, zi), gs)
        both(n - 1, lambda g, zi: first_in(g, zi), gs)
        for g in gs:
            second_in(g, z, 0)
        for g in gs:
            second_in(g, z, 1)
        for s in range(1, n):
            both(s, lambda g, zi: second_in(g, zi, 0), gs)
            both(s, lambda g, zi: second_in(g, zi, 1), gs)

    def both(s, what, gs):
        @pl.when(z - s >= 0)
        def _():
            for g in gs:
                what(g, z - s)

        @pl.when(z + s < n)
        def _():
            for g in gs:
                what(g, z + s)

    begin(0)
    small_step(0)
    steps((0,))
    for step in range(1, len(partners)):
        small_step(step)

    keep.wait()
    for zi in range(n):
        for q in range(1, 4):
            to_sibling(0, zi, q).wait_recv()

        @pl.when(zi != z)
        def _(zi=zi):
            to_sibling(0, zi, 0).wait_recv()
    save_w = pltpu.make_async_copy(out_ref, w_hbm, local_sem.at[1])
    save_w.start()

    width = x_ref.shape[1]
    third = width // 2
    vec_out[...] = vec_sent[len(partners)]

    def keys_of(yi):
        return pltpu.make_async_remote_copy(
            qkv.at[:, (3 * yi + 1) * third : (3 * yi + 3) * third],
            other_hbm.at[:, 2 * yi * third : 2 * (yi + 1) * third],
            ks.at[yi], kr.at[yi], device_id=w["sibling"], device_id_type=MESH,
        )

    for yi in range(2):
        first = (3 * yi + 1) * third
        both = nn(x_ref[...], out_ref[0, :, yi * wide + third : yi * wide + 3 * third])
        qkv[:, first : first + third] = both[:, :third].astype(BF)
        bias = vec_out[1:2, yi * third : (yi + 1) * third]
        qkv[:, first + third : first + 2 * third] = (both[:, third:] + bias).astype(BF)
        keys_of(yi).start()
    for yi in range(2):
        first = 3 * yi * third
        bias = vec_out[0:1, yi * third : (yi + 1) * third]
        qkv[:, first : first + third] = (nn(x_ref[...], out_ref[0, :, yi * wide : yi * wide + third]) + bias).astype(BF)

    save_qkv = pltpu.make_async_copy(qkv, qkv_hbm, local_sem.at[2])
    save_qkv.start()
    for g in (0,):
        @pl.when(z < n - 1)
        def _(g=g):
            line_up(g, 0).wait_send()

        @pl.when(z > 0)
        def _(g=g):
            line_down(g, 0).wait_send()
        for s in range(1, n - 1):
            @pl.when((z < n - 1) & (z - s >= 0))
            def _(g=g, s=s):
                line_up(g, s).wait_send()

            @pl.when((z > 0) & (z + s < n))
            def _(g=g, s=s):
                line_down(g, s).wait_send()
        for zi in range(n):
            to_first(g, zi).wait_send()
            for far in range(2):
                to_second(g, zi, far).wait_send()
            for q in range(1, 4):
                to_sibling(g, zi, q).wait_send()
        for zi in range(n):
            @pl.when(zi != z)
            def _(g=g, zi=zi):
                to_sibling(g, zi, 0).wait_send()


    for step in range(len(partners)):
        small_send(step).wait_send()

    for yi in range(2):
        keys_of(yi).wait()
    save_w.wait()
    save_qkv.wait()


def start(mine, vec, layer_in):
    dp, tp = lax.axis_size("dp"), lax.axis_size("tensor")
    n = dp // 2
    parts, block, wide = mine.shape
    rows, width = layer_in.shape
    steps = 3 + (n - 1).bit_length()
    dma = pltpu.SemaphoreType.DMA
    anywhere, inside = pl.BlockSpec(memory_space=pl.ANY), pl.BlockSpec(memory_space=pltpu.VMEM)
    whole = (parts, dp * block, wide * tp // 2)
    return pl.pallas_call(
        partial(start_kernel, n),
        name="start",
        in_specs=[inside] * 3,
        out_specs=[anywhere] * 3 + [inside],
        out_shape=[
            jax.ShapeDtypeStruct(whole, BF),
            jax.ShapeDtypeStruct((rows, 3 * width), BF),
            jax.ShapeDtypeStruct((rows, 2 * width), BF),
            jax.ShapeDtypeStruct(vec.shape, F32),
        ],
        scratch_shapes=[
            pltpu.VMEM(whole, BF), pltpu.VMEM(mine.shape, BF), pltpu.VMEM(mine.shape, BF),
            pltpu.VMEM((rows, 3 * width), BF),
            pltpu.VMEM((steps + 1,) + vec.shape, F32), pltpu.VMEM((steps,) + vec.shape, F32),
            dma((3,)), dma((2,)), dma((1, 2, n)), dma((1, 2, n)), dma((1, n)), dma((1, n)),
            dma((1, 2, n)), dma((1, 2, n)), dma((1, 4, n)), dma((1, 4, n)), dma((2,)), dma((2,)),
            dma((steps,)), dma((steps,)),
        ],
        compiler_params=params_of(3),
    )(mine, vec, layer_in)


def in_tiles(block):
    return block % 32 == 0


def start_plainly(mine, vec, layer_in):
    dp, tp = lax.axis_size("dp"), lax.axis_size("tensor")
    parts, block, wide = mine.shape
    width = layer_in.shape[1]
    third = width // 2
    every = lax.all_gather(mine, ("dp", "tensor"), axis=0, tiled=False)
    every = every.reshape(dp, tp // 2, 2, parts, block, wide).sum(axis=2)
    weights = every.transpose(2, 0, 3, 1, 4).reshape(parts, dp * block, tp // 2 * wide)
    vec = lax.psum(vec, ("dp", "tensor"))
    zero = jnp.zeros((1, third), F32)
    bias = jnp.concatenate(
        [v for y in range(2) for v in (vec[:1, y * third : (y + 1) * third], zero,
                                       vec[1:2, y * third : (y + 1) * third])], axis=1,
    )
    wqkv = weights[0].reshape(width, 2, 4 * third)[:, :, : 3 * third].reshape(width, 3 * width)
    qkv = (nn(layer_in, wqkv) + bias).astype(BF)
    return weights, qkv, swap_keys(qkv), vec


def q_lanes(p, pairs):
    third = pairs // 2 * PAIR
    first = p // (pairs // 2) * 3 * third + p % (pairs // 2) * PAIR
    return slice(first, first + PAIR)


def k_lanes(p, pairs):
    third = pairs // 2 * PAIR
    first = p // (pairs // 2) * 2 * third + p % (pairs // 2) * PAIR
    return slice(first, first + PAIR)


def v_lanes(p, pairs):
    third = pairs // 2 * PAIR
    lanes = k_lanes(p, pairs)
    return slice(lanes.start + third, lanes.stop + third)


def key_tile(j, qkv_ref, other_ref, kv, sems):
    rows, third = other_ref.shape[0], other_ref.shape[1] // 4
    here = pl.ds(pl.multiple_of(j * KT, KT), KT)
    from_row = pl.ds(pl.multiple_of(lax.rem(j * KT, rows), KT), KT)
    own = [
        pltpu.make_async_copy(
            qkv_ref.at[from_row, (3 * y + 1) * third : (3 * y + 3) * third],
            kv.at[here, 2 * y * third : 2 * (y + 1) * third],
            sems.at[y, j],
        )
        for y in range(2)
    ]
    far = pltpu.make_async_copy(other_ref.at[from_row, :], kv.at[here, :], sems.at[0, j])
    is_own = (j * KT) // rows == lax.rem(lax.axis_index("tensor"), 2)
    return is_own, own, far


def fetch_keys(low, high, qkv_ref, other_ref, kv, sems, use):
    @pl.loop(low, high)
    def _(j):
        is_own, own, far = key_tile(j, qkv_ref, other_ref, kv, sems)

        @pl.when(is_own)
        def _():
            for move in own:
                move.start()

        @pl.when(jnp.logical_not(is_own))
        def _():
            far.start()

    @pl.loop(low, high)
    def _(j):
        is_own, own, far = key_tile(j, qkv_ref, other_ref, kv, sems)

        @pl.when(is_own)
        def _():
            for move in own:
                move.wait()

        @pl.when(jnp.logical_not(is_own))
        def _():
            far.wait()
        use(j)


def masked_pairs(source, target, lanes_of, pairs, scale):
    rows = source.shape[0]
    low_lanes = lax.broadcasted_iota(jnp.int32, (rows, PAIR), 1) < HD
    for p in range(pairs):
        both = source[:, lanes_of(p)]
        if scale is not None:
            both = both * jnp.asarray(scale, both.dtype)
        zero = jnp.zeros_like(both)
        target[p, :rows, :] = jnp.where(low_lanes, both, zero)
        target[p, rows:, :] = jnp.where(low_lanes, zero, both)


def tile_bias(j, q_first, row_info, key_info, bias):
    seg_q, bits_q = row_info[0:1, :], row_info[1:2, :]
    queries = bias.shape[1]
    for part in range(KT // HD):
        block = j * (KT // HD) + part
        bit = jnp.bitwise_and(
            lax.shift_right_logical(bits_q, jnp.full_like(bits_q, block)), 1
        )
        wanted = jnp.where(bit == 1, seg_q, -1)
        base = pl.multiple_of(j * KT + part * HD, HD)
        seg_k = key_info[pl.ds(base, HD), :]
        key_at = base + lax.broadcasted_iota(jnp.int32, (HD, queries), 0)
        query_at = q_first + lax.broadcasted_iota(jnp.int32, (HD, queries), 1)
        allowed = (seg_k == wanted) | (key_at == query_at)
        bias[part * HD : (part + 1) * HD, :] = jnp.where(allowed, 0.0, NEGATIVE)


def attend_forward_kernel(
    bounds, q_ref, qkv_ref, other_ref, row_info, key_info, out_ref, log_ref,
    q_pairs, kv_ref, v_turned, bias, top, total, acc, scores, fades, lows, sems,
):
    step = pl.program_id(0)
    rows, width = out_ref.shape
    pairs = width // PAIR
    tiles = kv_ref.shape[0] // KT

    @pl.when(step == 0)
    def _():
        def turn(j):
            for p in range(pairs):
                span = slice(p * PAIR, (p + 1) * PAIR)
                v_turned[j, span, :] = kv_ref[pl.ds(pl.multiple_of(j * KT, KT), KT), v_lanes(p, pairs)].T

        fetch_keys(bounds[0, 0], bounds[pl.num_programs(0) - 1, 1], qkv_ref, other_ref, kv_ref, sems, turn)

    masked_pairs(q_ref, q_pairs, partial(q_lanes, pairs=pairs), pairs, HD**-0.5)
    top[...] = jnp.full_like(top, NEGATIVE)
    total[...] = jnp.zeros_like(total)
    acc[...] = jnp.zeros_like(acc)
    q_first = bounds[step, 2]

    @pl.loop(bounds[step, 0], bounds[step, 1])
    def _(j):
        tile_bias(j, q_first, row_info, key_info, bias)
        keys_at = pl.multiple_of(j * KT, KT)
        for p in range(pairs):
            keys = kv_ref[pl.ds(keys_at, KT), k_lanes(p, pairs)]
            scores[p] = nt(keys, q_pairs[p])
        for h in range(2 * pairs):
            p, e = divmod(h, 2)
            mine = scores[p, :, e * rows : (e + 1) * rows] + bias[...]
            before = top[h : h + 1, :]
            now = jnp.maximum(before, jnp.max(mine, axis=0, keepdims=True))
            fade = jnp.exp(before - now)
            expos = jnp.exp(mine - now)
            top[h : h + 1, :] = now
            fades[h : h + 1, :] = fade
            total[h : h + 1, :] = fade * total[h : h + 1, :] + jnp.sum(
                expos, axis=0, keepdims=True
            )
            lows[h] = expos.astype(BF)
        for h in range(2 * pairs):
            span = slice(h * HD, (h + 1) * HD)
            acc[span, :] = acc[span, :] * fades[h : h + 1, :] + nn(v_turned[j, span, :], lows[h])

    heads = width // HD
    for h in range(heads):
        span = slice(h * HD, (h + 1) * HD)
        acc[span, :] = acc[span, :] / total[h : h + 1, :]
    out_ref[...] = acc[...].T.astype(BF)
    log_ref[...] = top[...] + jnp.log(jnp.maximum(total[...], 1e-37))


def attend_forward(bounds, qkv, other, row_info, key_info):
    rows, width = qkv.shape[0], qkv.shape[1] // 3
    keys = 2 * rows
    stat_rows = 16
    return pl.pallas_call(
        attend_forward_kernel,
        name="attend_forward",
        grid_spec=pltpu.PrefetchScalarGridSpec(
            num_scalar_prefetch=1,
            grid=(rows // QT,),
            in_specs=[
                pl.BlockSpec((QT, 3 * width), lambda i, b: (i, 0)),
                pl.BlockSpec(memory_space=pl.ANY),
                pl.BlockSpec(memory_space=pl.ANY),
                pl.BlockSpec((8, QT), lambda i, b: (0, i)),
                pl.BlockSpec((keys, 1), lambda i, b: (0, 0), pipeline_mode=pl.Buffered(1)),
            ],
            out_specs=[
                pl.BlockSpec((QT, width), lambda i, b: (i, 0)),
                pl.BlockSpec((stat_rows, QT), lambda i, b: (0, i)),
            ],
            scratch_shapes=[
                pltpu.VMEM((width // PAIR, 2 * QT, PAIR), BF),
                pltpu.VMEM((keys, 2 * width), BF),
                pltpu.VMEM((keys // KT, width, KT), BF),
                pltpu.VMEM((KT, QT), F32),
                pltpu.VMEM((stat_rows, QT), F32),
                pltpu.VMEM((stat_rows, QT), F32),
                pltpu.VMEM((width, QT), F32),
                pltpu.VMEM((width // PAIR, KT, 2 * QT), F32),
                pltpu.VMEM((stat_rows, QT), F32),
                pltpu.VMEM((width // HD, KT, QT), BF),
                pltpu.SemaphoreType.DMA((2, keys // KT)),
            ],
        ),
        out_shape=[
            jax.ShapeDtypeStruct((rows, width), BF),
            jax.ShapeDtypeStruct((stat_rows, rows), F32),
        ],
        compiler_params=params_of(),
    )(bounds, qkv, qkv, other, row_info, key_info)


def attend_backward_kernel(
    bounds, q_ref, qkv_ref, other_ref, row_info, key_info, out_ref, log_ref, grad_ref,
    dq_ref, dkv_ref, q_pairs, g_pairs, kv_ref, k_turned, bias, inner, dq_acc, dkv_acc,
    scores, changes, probs, grads, sems,
):
    step = pl.program_id(0)
    rows, width = out_ref.shape
    pairs = width // PAIR
    tiles = kv_ref.shape[0] // KT

    @pl.when(step == 0)
    def _():
        def turn(j):
            for p in range(pairs):
                span = slice(p * PAIR, (p + 1) * PAIR)
                k_turned[j, span, :] = kv_ref[pl.ds(pl.multiple_of(j * KT, KT), KT), k_lanes(p, pairs)].T

        fetch_keys(bounds[0, 0], bounds[pl.num_programs(0) - 1, 1], qkv_ref, other_ref, kv_ref, sems, turn)
        dkv_acc[...] = jnp.zeros_like(dkv_acc)

    masked_pairs(q_ref, q_pairs, partial(q_lanes, pairs=pairs), pairs, HD**-0.5)
    masked_pairs(grad_ref, g_pairs, lambda p: slice(p * PAIR, (p + 1) * PAIR), pairs, None)
    dq_acc[...] = (out_ref[...].astype(F32) * grad_ref[...].astype(F32)).T
    for h in range(2 * pairs):
        inner[h : h + 1, :] = jnp.sum(dq_acc[h * HD : (h + 1) * HD, :], axis=0, keepdims=True)
    dq_acc[...] = jnp.zeros_like(dq_acc)
    q_first = bounds[step, 2]

    @pl.loop(bounds[step, 0], bounds[step, 1])
    def _(j):
        tile_bias(j, q_first, row_info, key_info, bias)
        here = pl.ds(pl.multiple_of(j * KT, KT), KT)
        for p in range(pairs):
            scores[p] = nt(kv_ref[here, k_lanes(p, pairs)], q_pairs[p])
            changes[p] = nt(kv_ref[here, v_lanes(p, pairs)], g_pairs[p])
        for h in range(2 * pairs):
            p, e = divmod(h, 2)
            cols = slice(e * rows, (e + 1) * rows)
            prob = jnp.exp(scores[p, :, cols] + bias[...] - log_ref[h : h + 1, :])
            probs[p, :, cols] = prob.astype(BF)
            grads[p, :, cols] = (prob * (changes[p, :, cols] - inner[h : h + 1, :])).astype(BF)
        for p in range(pairs):
            dkv_acc[here, k_lanes(p, pairs)] += nn(grads[p], q_pairs[p])
            dkv_acc[here, v_lanes(p, pairs)] += nn(probs[p], g_pairs[p])
        for h in range(2 * pairs):
            p, e = divmod(h, 2)
            span = slice(h * HD, (h + 1) * HD)
            dq_acc[span, :] += nn(k_turned[j, span, :], grads[p, :, e * rows : (e + 1) * rows])

    dq_ref[...] = (dq_acc[...] * HD**-0.5).T.astype(BF)

    @pl.when(step == pl.num_programs(0) - 1)
    def _():
        dkv_ref[...] = dkv_acc[...].astype(BF)


def attend_backward(bounds, qkv, other, row_info, key_info, attn, logs, grad_attn):
    rows, width = attn.shape
    keys = 2 * rows
    stat_rows = logs.shape[0]
    whole = dict(pipeline_mode=pl.Buffered(1))
    return pl.pallas_call(
        attend_backward_kernel,
        name="attend_backward",
        grid_spec=pltpu.PrefetchScalarGridSpec(
            num_scalar_prefetch=1,
            grid=(rows // QT,),
            in_specs=[
                pl.BlockSpec((QT, 3 * width), lambda i, b: (i, 0)),
                pl.BlockSpec(memory_space=pl.ANY),
                pl.BlockSpec(memory_space=pl.ANY),
                pl.BlockSpec((8, QT), lambda i, b: (0, i)),
                pl.BlockSpec((keys, 1), lambda i, b: (0, 0), **whole),
                pl.BlockSpec((QT, width), lambda i, b: (i, 0)),
                pl.BlockSpec((stat_rows, QT), lambda i, b: (0, i)),
                pl.BlockSpec((QT, width), lambda i, b: (i, 0)),
            ],
            out_specs=[
                pl.BlockSpec((QT, width), lambda i, b: (i, 0)),
                pl.BlockSpec((keys, 2 * width), lambda i, b: (0, 0), **whole),
            ],
            scratch_shapes=[
                pltpu.VMEM((width // PAIR, 2 * QT, PAIR), BF),
                pltpu.VMEM((width // PAIR, 2 * QT, PAIR), BF),
                pltpu.VMEM((keys, 2 * width), BF),
                pltpu.VMEM((keys // KT, width, KT), BF),
                pltpu.VMEM((KT, QT), F32),
                pltpu.VMEM((stat_rows, QT), F32),
                pltpu.VMEM((width, QT), F32),
                pltpu.VMEM((keys, 2 * width), F32),
                pltpu.VMEM((width // PAIR, KT, 2 * QT), F32),
                pltpu.VMEM((width // PAIR, KT, 2 * QT), F32),
                pltpu.VMEM((width // PAIR, KT, 2 * QT), BF),
                pltpu.VMEM((width // PAIR, KT, 2 * QT), BF),
                pltpu.SemaphoreType.DMA((2, keys // KT)),
            ],
        ),
        out_shape=[
            jax.ShapeDtypeStruct((rows, width), BF),
            jax.ShapeDtypeStruct((keys, 2 * width), BF),
        ],
        compiler_params=params_of(),
    )(bounds, qkv, qkv, other, row_info, key_info, attn, logs, grad_attn)


def attention_plan(segment_ids, pad_mask, random_blocks, global_blocks, rows):
    seq_count, nblocks = random_blocks.shape[0], random_blocks.shape[1]
    seq_len = segment_ids.shape[0] // seq_count
    rank = lax.axis_index("tensor")
    seq, half = rank // 2, lax.rem(rank, 2)
    segs = lax.dynamic_index_in_dim(segment_ids.reshape(seq_count, seq_len), seq, 0, False)
    pads = lax.dynamic_index_in_dim(pad_mask.reshape(seq_count, seq_len), seq, 0, False)
    randoms = lax.dynamic_index_in_dim(random_blocks, seq, 0, False)
    globs = lax.dynamic_index_in_dim(global_blocks, seq, 0, False)
    block_size = seq_len // nblocks
    one = jnp.int32(1)
    block = jnp.arange(nblocks, dtype=jnp.int32)

    def either(a, b):
        return jnp.bitwise_or(a, b)

    block_bits = lax.shift_left(one, block)
    window = either(
        block_bits,
        either(
            jnp.where(block > 0, lax.shift_left(one, jnp.maximum(block - 1, 0)), 0),
            jnp.where(
                block < nblocks - 1, lax.shift_left(one, jnp.minimum(block + 1, nblocks - 1)), 0
            ),
        ),
    )
    for r in range(randoms.shape[1]):
        window = either(window, lax.shift_left(one, randoms[:, r]))
    glob_bits = either(lax.shift_left(one, globs[:, 0]), lax.shift_left(one, globs[:, 1]))
    first = half * rows
    seg_q = lax.dynamic_slice_in_dim(segs, first, rows)
    own_bits = lax.dynamic_slice_in_dim(window, half * (rows // block_size), rows // block_size)
    bits = jnp.broadcast_to(own_bits[:, None], (rows // block_size, block_size)).reshape(rows)
    numbers = jnp.arange(globs.shape[0], dtype=jnp.int32)
    is_doc = seg_q[None, :] == numbers[:, None]
    bits = either(bits, jnp.sum(jnp.where(is_doc, glob_bits[:, None], 0), axis=0))
    row_info = jnp.concatenate(
        [seg_q[None], bits[None], jnp.zeros((6, rows), jnp.int32)], axis=0
    )
    key_info = jnp.where(pads == 1, segs, -2)[:, None]
    tiles = seg_q.reshape(rows // QT, QT)
    low = jnp.sum((segs[None, :] < tiles[:, :1]).astype(jnp.int32), axis=1)
    high = jnp.sum((segs[None, :] <= tiles[:, -1:]).astype(jnp.int32), axis=1)
    starts = first + QT * jnp.arange(rows // QT, dtype=jnp.int32)
    bounds = jnp.stack([low // KT, (high + KT - 1) // KT, starts, starts], axis=1)
    return bounds, row_info, key_info


TAIL_STEP = 0.47
TAIL = (0.266306628, 0.248031891, 0.336199252, -0.126105651, 0.607561554, -0.420410983, 0.0884173167)


def gelu_and_slope(pre):
    bell = jnp.exp(-0.5 * pre * pre)
    t = 1.0 / (1.0 + (TAIL_STEP * 0.5**0.5) * jnp.abs(pre))
    tail = TAIL[-1]
    for c in TAIL[-2::-1]:
        tail = tail * t + c
    tail = 0.5 * (tail * t) * bell
    cdf = jnp.where(pre < 0, tail, 1.0 - tail)
    return pre * cdf, cdf + pre * (bell * (2.0 * 3.141592653589793) ** -0.5)


def normalize(resid):
    center = resid - jnp.mean(resid, axis=1, keepdims=True)
    inverse = lax.rsqrt(jnp.mean(center * center, axis=1, keepdims=True) + EPSILON)
    return center * inverse, inverse


def norm_backward(grad_normed, normal_hat, inverse, gain):
    grad_hat = grad_normed * gain
    return inverse * (
        grad_hat
        - jnp.mean(grad_hat, axis=1, keepdims=True)
        - normal_hat * jnp.mean(grad_hat * normal_hat, axis=1, keepdims=True)
    )


def fetch_blocks(blocks_hbm, blocks_ref, sems):
    return [
        pltpu.make_async_copy(blocks_hbm.at[:, t], blocks_ref.at[:, t], sems.at[t])
        for t in range(blocks_ref.shape[1])
    ]


def begin_fetch(blocks_hbm, blocks_ref, sems):
    @pl.when(pl.program_id(0) == 0)
    def _():
        for move in fetch_blocks(blocks_hbm, blocks_ref, sems):
            move.start()


def end_fetch(blocks_hbm, blocks_ref, sems):
    @pl.when(pl.program_id(0) == 0)
    def _():
        for move in fetch_blocks(blocks_hbm, blocks_ref, sems):
            move.wait()


def unit_chunks(blocks_ref):
    dp, tp, own_rows, both = blocks_ref.shape
    units = both // 2
    for t in range(tp):
        w_in = lambda t=t: blocks_ref[:, t, :, :units].reshape(dp * own_rows, units)
        w_out = lambda t=t: blocks_ref[:, t, :, units:].reshape(dp * own_rows, units)
        yield t, slice(t * units, (t + 1) * units), w_in, w_out


def forth_kernel(
    x_ref, attn_ref, cot_ref, proj_0, proj_1, blocks_hbm, vec_ref,
    final_ref, resid_out, grad_out, norm_low, slope, ffn_grad, out_grad, sums, hidden, outer, blocks_ref, sems,
):
    begin_fetch(blocks_hbm, blocks_ref, sems)
    out_bias, last_bias, gain_1, shift_1, gain_2, shift_2 = (vec_ref[i : i + 1, :] for i in range(2, 8))

    @pl.when(pl.program_id(0) == 0)
    def _():
        sums[...] = jnp.zeros_like(sums)
        outer[...] = jnp.zeros_like(outer)

    resid = x_ref[...].astype(F32) + out_bias
    third = proj_0.shape[2]
    resid += nt(attn_ref[:, :third], proj_0[0]) + nt(attn_ref[:, third:], proj_1[0])
    resid_out[...] = resid
    hat, _ = normalize(resid)
    first_norm = hat * gain_1 + shift_1
    low = first_norm.astype(BF)
    norm_low[...] = low
    resid = first_norm + last_bias
    end_fetch(blocks_hbm, blocks_ref, sems)
    for t, cols, w_in, w_out in unit_chunks(blocks_ref):
        act, slope[:, cols] = gelu_and_slope(nn(low, w_in()) + vec_ref[8 + t : 9 + t, :])
        act = act.astype(BF)
        hidden[:, cols] = act
        resid += nt(act, w_out())
    hat, inverse = normalize(resid)
    final_ref[...] = (hat * gain_2 + shift_2).astype(BF)
    cot = cot_ref[...].astype(F32)
    grad = norm_backward(cot, hat, inverse, gain_2)
    sums[6:7, :] += jnp.sum(cot * hat, axis=0, keepdims=True)
    sums[7:8, :] += jnp.sum(cot, axis=0, keepdims=True)
    sums[3:4, :] += jnp.sum(grad, axis=0, keepdims=True)
    grad_out[...] = grad
    low = grad.astype(BF)
    ffn_grad[...] = low
    turned = low.T
    for t, cols, _, _ in unit_chunks(blocks_ref):
        outer[t] += nn(turned, hidden[:, cols])

    @pl.when(pl.program_id(0) == pl.num_programs(0) - 1)
    def _():
        for t in range(out_grad.shape[1]):
            out_grad[:, t] = outer[t].reshape(out_grad.shape[0], out_grad.shape[2], out_grad.shape[3]).astype(BF)


def back_kernel(
    resid_ref, grad_ref, ffn_grad, slope, proj_0, proj_1, blocks_hbm, vec_ref, sums_ref,
    first_grad, attn_grad, unit_grad, proj_grad, sums, unit_sums, blocks_ref, sems,
):
    begin_fetch(blocks_hbm, blocks_ref, sems)
    @pl.when(pl.program_id(0) == 0)
    def _():
        sums[...] = sums_ref[...]
        unit_sums[...] = jnp.zeros_like(unit_sums)

    hat, inverse = normalize(resid_ref[...])
    low = ffn_grad[...]
    grad = grad_ref[...]
    end_fetch(blocks_hbm, blocks_ref, sems)
    for t, cols, w_in, w_out in unit_chunks(blocks_ref):
        act = (nn(low, w_out()) * slope[:, cols]).astype(BF)
        unit_grad[:, cols] = act
        unit_sums[0:1, cols] += jnp.sum(act.astype(F32), axis=0, keepdims=True)
        grad += nt(act, w_in())
    sums[4:5, :] += jnp.sum(grad * hat, axis=0, keepdims=True)
    sums[5:6, :] += jnp.sum(grad, axis=0, keepdims=True)
    grad = norm_backward(grad, hat, inverse, vec_ref[4:5, :])
    sums[2:3, :] += jnp.sum(grad, axis=0, keepdims=True)
    first_grad[...] = grad
    low = grad.astype(BF)
    proj_grad[...] = low
    third = proj_0.shape[2]
    attn_grad[:, :third] = nn(low, proj_0[0]).astype(BF)
    attn_grad[:, third:] = nn(low, proj_1[0]).astype(BF)


def middle(layer_in, attn, output_grad, weights, blocks, vectors):
    rows, width = layer_in.shape
    tp, own_units = blocks.shape[1], blocks.shape[3] // 2
    units = tp * own_units
    once = dict(pipeline_mode=pl.Buffered(1))
    whole = lambda a: pl.BlockSpec(a.shape, lambda i: (0,) * len(a.shape), **once)
    fixed = lambda w: pl.BlockSpec((8, w), lambda i: (0, 0))
    shape = lambda w, t: jax.ShapeDtypeStruct((rows, w), t)
    sums_of = lambda w: jax.ShapeDtypeStruct((8, w), F32)
    out_grad = jax.ShapeDtypeStruct(blocks.shape[:3] + (own_units,), BF)
    third = width // 2
    proj = [pl.BlockSpec((1, width, third), lambda i, y=y: (0, 0, 4 * y + 3), **once) for y in range(2)]
    held = [pltpu.VMEM(blocks.shape, BF), pltpu.SemaphoreType.DMA((tp,))]
    tile = lambda w: pl.BlockSpec((ROWS, w), lambda i: (i, 0))
    layer_out, resid, grad_second, norm_low, slope, ffn_grad, out_grad, sums = pl.pallas_call(
        forth_kernel,
        name="middle_forth",
        grid=(rows // ROWS,),
        in_specs=[tile(width)] * 3 + proj + [pl.BlockSpec(memory_space=pl.ANY), whole(vectors)],
        out_specs=[tile(width)] * 4 + [tile(units), tile(width), whole(out_grad), fixed(width)],
        out_shape=[
            shape(width, BF), shape(width, F32), shape(width, F32), shape(width, BF), shape(units, F32),
            shape(width, BF), out_grad, sums_of(width),
        ],
        scratch_shapes=[pltpu.VMEM((ROWS, units), BF), pltpu.VMEM((tp, width, own_units), F32)] + held,
        compiler_params=params_of(),
    )(layer_in, attn, output_grad, weights, weights, blocks, vectors)
    tile = lambda w: pl.BlockSpec((BACK_ROWS, w), lambda i: (i, 0))
    first_grad, attn_grad, unit_grad, proj_grad, sums, unit_sums = pl.pallas_call(
        back_kernel,
        name="middle_back",
        grid=(rows // BACK_ROWS,),
        in_specs=[tile(width)] * 3 + [tile(units)] + proj + [pl.BlockSpec(memory_space=pl.ANY), whole(vectors), whole(sums)],
        out_specs=[tile(width)] * 2 + [tile(units), tile(width), fixed(width), fixed(units)],
        out_shape=[
            shape(width, F32), shape(width, BF), shape(units, BF), shape(width, BF), sums_of(width), sums_of(units),
        ],
        scratch_shapes=held,
        compiler_params=params_of(),
    )(resid, grad_second, ffn_grad, slope, weights, weights, blocks, vectors, sums)
    return layer_out, first_grad, attn_grad, norm_low, unit_grad, proj_grad, out_grad, sums, unit_sums


def finish_kernel(
    n, x_hbm, dq_hbm, dkv_hbm, w_hbm, first_hbm, low_hbm, unit_hbm, proj_hbm, attn_hbm, sums_ref, unit_sums,
    input_hbm, q_out, k_out, v_out, o_out, in_out, vec_out,
    rows_in, turned, unit, d_qkv, attn, far, w_all, tile_in, tile_out, grads, sib, from_b, from_a, from_low, from_high,
    result, vec_sent, vec_got,
    load, swap_s, swap_r, ss, sr, bs, br, as_, ar, zs, zr, es, er, vs, vr, tile_sem,
):
    w = places()
    dp, rank, core, y, z, x = (w[k] for k in ("dp", "rank", "core", "y", "z", "x"))
    rows, width = x_hbm.shape
    third = width // 2
    wide = unit.shape[1] // 2
    slab = result.shape[1] // 2
    up, down = {"dp": lax.rem(dp + 2, 2 * n), "tensor": rank}, {"dp": lax.rem(dp + 2 * n - 2, 2 * n), "tensor": rank}
    partners = [w["sibling"], w["second"], w["first"]] + line_jumps(dp, rank, z, n)
    barrier = pltpu.get_barrier_semaphore()
    for other in partners + [up, down]:
        pl.semaphore_signal(barrier, inc=1, device_id=other, device_id_type=MESH)

    def fetch(i, src, dst):
        return pltpu.make_async_copy(src, dst, load.at[i])

    fetch_low = fetch(0, low_hbm, rows_in.at[0])
    fetch_unit = fetch(1, unit_hbm, unit)
    fetch_x = fetch(2, x_hbm, rows_in.at[1])
    fetch_proj = fetch(3, proj_hbm, rows_in.at[2])
    fetch_attn = fetch(4, attn_hbm, attn)
    fetch_w = fetch(5, w_hbm.at[0], w_all)
    fetch_dq = [fetch(6 + h, dq_hbm.at[:, h * third : (h + 1) * third], d_qkv.at[:, 3 * h * third : (3 * h + 1) * third]) for h in range(2)]
    fetch_kv = [fetch(8 + h, dkv_hbm.at[core, :, 2 * h * third : 2 * (h + 1) * third], d_qkv.at[:, (3 * h + 1) * third : (3 * h + 3) * third]) for h in range(2)]
    for move in [fetch_low, fetch_unit, fetch_x, fetch_proj, fetch_attn] + fetch_dq + fetch_kv + [fetch_w]:
        move.start()
    pl.semaphore_wait(barrier, len(partners) + 2)

    def copy(src, dst, ssem, rsem, dev):
        return pltpu.make_async_remote_copy(src, dst, ssem, rsem, device_id=dev, device_id_type=MESH)

    swap = copy(dkv_hbm.at[1 - core], far, swap_s, swap_r, w["sibling"])
    swap.start()

    def turn_rows(i):
        for c in range(0, width, 128):
            turned[i, c : c + 128, :] = rows_in[i, :, c : c + 128].T

    places_of = [xd * 2 + yd for xd, yd in (
        (x, y), (w["xa"], w["ya"]), (w["xb"], w["yb"]), (w["xa"] + w["xb"] - x, w["ya"] + w["yb"] - y))]
    mine = grads.at[core]

    def keep(k, zd, yd, lane, value):
        for xd in range(2):
            for c in range(2):
                first = (xd * 2 + c) * slab
                grads[c, k, zd, xd * 2 + yd, :, lane : lane + value.shape[1]] = value[first : first + slab, :].astype(BF)

    def rows_of_line(i, zd):
        return turned[i, pl.ds(pl.multiple_of(zd * 4 * slab, 4 * slab), 4 * slab), :]

    def compute_inner(zd):
        left = rows_of_line(0, zd)
        for yd in range(2):
            for lane in range(0, wide, 768):
                keep(1, zd, yd, lane, nn(left, unit[:, yd * wide + lane : yd * wide + lane + 768]))

    def compute_others(zd):
        left = rows_of_line(1, zd)
        for yd in range(2):
            for i in range(3):
                at = (3 * yd + i) * third
                keep(0, zd, yd, i * third, nn(left, d_qkv[:, at : at + third]))
        left = rows_of_line(2, zd)
        for yd in range(2):
            keep(0, zd, yd, 3 * third, nn(left, attn[:, yd * third : (yd + 1) * third]))

    def to_sibling(k, zd):
        return copy(grads.at[1 - core, k, zd], sib.at[k, zd], ss.at[k, zd], sr.at[k, zd], w["sibling"])

    def over_b(k, far_side, zd):
        place = places_of[2 + far_side]
        return copy(mine.at[k, zd, place], from_b.at[k, far_side, zd], bs.at[k, far_side, zd], br.at[k, far_side, zd], w["second"])

    def over_a(k, zd):
        return copy(mine.at[k, zd, places_of[1]], from_a.at[k, zd], as_.at[k, zd], ar.at[k, zd], w["first"])

    def over_up(k, zd):
        return copy(mine.at[k, zd, places_of[0]], from_low.at[k, zd], zs.at[k, zd], zr.at[0, k, zd], up)

    def over_down(k, zd):
        return copy(mine.at[k, zd, places_of[0]], from_high.at[k, zd], zs.at[k, zd], zr.at[1, k, zd], down)

    def put(q, k, zd, more):
        place = places_of[q]
        total = grads[core, k, zd, place].astype(F32) + sib[k, zd, place].astype(F32)
        for term in more:
            total = total + term[...].astype(F32)
        grads[core, k, zd, place] = total.astype(BF)

    def stage_b(k, zd):
        to_sibling(k, zd).wait_recv()
        for far_side in (1, 0):
            put(2 + far_side, k, zd, ())
            over_b(k, far_side, zd).start()

    def stage_a(k, zd):
        over_b(k, 1, zd).wait_recv()
        put(1, k, zd, (from_b.at[k, 1, zd],))
        over_a(k, zd).start()

    def stage_line(k, zd):
        over_b(k, 0, zd).wait_recv()
        over_a(k, zd).wait_recv()
        put(0, k, zd, (from_b.at[k, 0, zd], from_a.at[k, zd]))

        @pl.when((zd > z) & (z == 0))
        def _():
            over_up(k, zd).start()

        @pl.when((zd < z) & (z == n - 1))
        def _():
            over_down(k, zd).start()

    def grow(k, zd, term):
        place = places_of[0]
        grads[core, k, zd, place] = (grads[core, k, zd, place].astype(F32) + term[...].astype(F32)).astype(BF)

    def stage_hop(k, zd):
        @pl.when((zd > z) & (z > 0))
        def _():
            over_up(k, zd).wait_recv()
            grow(k, zd, from_low.at[k, zd])
            over_up(k, zd).start()

        @pl.when((zd < z) & (z < n - 1))
        def _():
            over_down(k, zd).wait_recv()
            grow(k, zd, from_high.at[k, zd])
            over_down(k, zd).start()

    def turn(i):
        below, above = z, n - 1 - z
        near = jnp.minimum(below, above)
        only = jnp.maximum(below, above) - near
        side = jnp.where(above >= below, 1, -1)
        distance = jnp.where(i < only, only + near - i, near - (i - only) // 2)
        sign = jnp.where(i < only, side, jnp.where(lax.rem(i - only, 2) == 0, side, -side))
        return jnp.where(i == n - 1, z, z + sign * distance)

    def item(j):
        return 1 - j // n, turn(lax.rem(j, n))

    def small_send(step):
        return copy(vec_sent.at[step], vec_got.at[step], vs.at[step], vr.at[step], partners[step])

    def input_tile(t):
        at = pl.ds(pl.multiple_of(t * ROWS, ROWS), ROWS)
        return (pltpu.make_async_copy(first_hbm.at[at, :], tile_in.at[lax.rem(t, 2)], tile_sem.at[0, lax.rem(t, 2)]),
                pltpu.make_async_copy(tile_out.at[lax.rem(t, 2)], input_hbm.at[at, :], tile_sem.at[1, lax.rem(t, 2)]), at)

    def input_grad(t):
        into, out, at = input_tile(t)
        into.start()
        total = nt(d_qkv[at, : 3 * third], w_all[:, : 3 * third])
        total += nt(d_qkv[at, 3 * third :], w_all[:, wide : wide + 3 * third])
        into.wait()
        tile_out[lax.rem(t, 2)] = tile_in[lax.rem(t, 2)] + total
        out.start()

    tiles = rows // ROWS
    last_item = 2 * n

    fetch_low.wait()
    turn_rows(0)
    fetch_unit.wait()

    @pl.loop(0, last_item + 4)
    def _(j):
        @pl.when(j < n)
        def _():
            k, zd = item(j)
            compute_inner(zd)
            to_sibling(1, zd).start()

        @pl.when(j == n - 1)
        def _():
            fetch_x.wait()
            fetch_proj.wait()
            fetch_attn.wait()
            turn_rows(1)
            turn_rows(2)
            for move in fetch_dq + fetch_kv:
                move.wait()
            swap.wait_recv()
            for h in range(2):
                at = slice((3 * h + 1) * third, (3 * h + 3) * third)
                d_qkv[:, at] = (d_qkv[:, at].astype(F32) + far[:, 2 * h * third : 2 * (h + 1) * third].astype(F32)).astype(BF)
            vec_sent[0] = jnp.zeros_like(vec_sent[0])
            vec_sent[0, 2:8, :] = sums_ref[2:8, :]
            for h in range(2):
                for row, i in ((0, 0), (1, 2)):
                    cols = d_qkv[:, (3 * h + i) * third : (3 * h + i + 1) * third].astype(F32)
                    vec_sent[0, row : row + 1, h * third : (h + 1) * third] = jnp.sum(cols, axis=0, keepdims=True)
            for u in range(unit_sums.shape[1] // width):
                vec_sent[0, 8 + u : 9 + u, :] = unit_sums[0:1, u * width : (u + 1) * width]
            small_send(0).start()
            fetch_w.wait()

        @pl.when((j >= n) & (j < last_item))
        def _():
            k, zd = item(j)
            compute_others(zd)
            to_sibling(0, zd).start()

        @pl.when((j >= 1) & (j < last_item + 1))
        def _():
            stage_b(*item(j - 1))

        @pl.when((j >= 2) & (j < last_item + 2))
        def _():
            stage_a(*item(j - 2))

        @pl.when((j >= 3) & (j < last_item + 3))
        def _():
            stage_line(*item(j - 3))

        @pl.when(j >= 4)
        def _():
            stage_hop(*item(j - 4))

        for step in range(len(partners)):
            @pl.when(j == n + step)
            def _(step=step):
                small_send(step).wait_recv()
                vec_sent[step + 1] = vec_sent[step] + vec_got[step]
                if step + 1 < len(partners):
                    small_send(step + 1).start()

        @pl.when((j >= last_item - tiles) & (j < last_item))
        def _():
            t = j - (last_item - tiles)

            @pl.when(t >= 2)
            def _():
                input_tile(t - 2)[1].wait()
            input_grad(t)

    vec_out[...] = vec_sent[len(partners)]
    own = pl.ds(pl.multiple_of(core * slab, slab), slab)
    theirs = pl.ds(pl.multiple_of((1 - core) * slab, slab), slab)
    for k in (1, 0):
        result[k, own, :] = grads[core, k, z, places_of[0]].astype(F32)

        @pl.when(z > 0)
        def _():
            over_up(k, z).wait_recv()
            result[k, own, :] += from_low[k, z].astype(F32)

        @pl.when(z < n - 1)
        def _():
            over_down(k, z).wait_recv()
            result[k, own, :] += from_high[k, z].astype(F32)

        copy(result.at[k, own, :], result.at[k, own, :], es.at[k], er.at[k], w["sibling"]).start()
    for t in range(max(tiles - 2, 0), tiles):
        input_tile(t)[1].wait()
    swap.wait_send()
    for step in range(len(partners)):
        small_send(step).wait_send()

    @pl.loop(0, n)
    def _(zd):
        for k in range(2):
            to_sibling(k, zd).wait_send()
            over_b(k, 0, zd).wait_send()
            over_b(k, 1, zd).wait_send()
            over_a(k, zd).wait_send()

            @pl.when(zd > z)
            def _():
                over_up(k, zd).wait_send()

            @pl.when(zd < z)
            def _():
                over_down(k, zd).wait_send()
    for k in (1, 0):
        copy(result.at[k, theirs, :], result.at[k, theirs, :], es.at[k], er.at[k], w["sibling"]).wait()

    def chosen(k, lane, w_own):
        both = result[k, :, lane : lane + 2 * w_own]
        return jnp.where(core == 0, both[:, :w_own], both[:, w_own:])

    for i, out in enumerate((q_out, k_out, v_out, o_out)):
        out[...] = chosen(0, i * third, third // 2)
    in_out[...] = chosen(1, 0, wide // 2)


def finish(layer_in, dq, dkv, weights, grad_first, norm_low, unit_grad, proj_grad, attn, sums, unit_sums):
    rows, width = layer_in.shape
    units = unit_grad.shape[1]
    dp, tp = lax.axis_size("dp"), lax.axis_size("tensor")
    n = dp // 2
    block = width // dp
    slab, wide, third = block // 2, units // 2, width // 2
    steps = 3 + (n - 1).bit_length()
    dma = pltpu.SemaphoreType.DMA
    slabs = lambda *lead: pltpu.VMEM(lead + (slab, wide), BF)
    anywhere, inside = pl.BlockSpec(memory_space=pl.ANY), pl.BlockSpec(memory_space=pltpu.VMEM)
    result = lambda *shape: jax.ShapeDtypeStruct(shape, F32)
    return pl.pallas_call(
        partial(finish_kernel, n),
        name="finish",
        in_specs=[anywhere] * 9 + [inside] * 2,
        out_specs=[anywhere] + [inside] * 6,
        out_shape=[result(rows, width)] + [result(block, third // 2)] * 4 + [result(block, wide // 2), result(16, width)],
        scratch_shapes=[
            pltpu.VMEM((3, rows, width), BF),
            pltpu.VMEM((3, width, rows), BF),
            pltpu.VMEM((rows, units), BF),
            pltpu.VMEM((rows, 3 * width), BF),
            pltpu.VMEM((rows, width), BF),
            pltpu.VMEM((rows, 2 * width), BF),
            pltpu.VMEM((width, units), BF),
            pltpu.VMEM((2, ROWS, width), F32),
            pltpu.VMEM((2, ROWS, width), F32),
            slabs(2, 2, n, 4),
            slabs(2, n, 4),
            slabs(2, 2, n),
            slabs(2, n),
            slabs(2, n),
            slabs(2, n),
            pltpu.VMEM((2, block, wide), F32),
            pltpu.VMEM((steps + 1, 16, width), F32),
            pltpu.VMEM((steps, 16, width), F32),
            dma((10,)), dma(()), dma(()),
            dma((2, n)), dma((2, n)), dma((2, 2, n)), dma((2, 2, n)), dma((2, n)), dma((2, n)),
            dma((2, n)), dma((2, 2, n)), dma((2,)), dma((2,)), dma((steps,)), dma((steps,)), dma((2, 2)),
        ],
        compiler_params=pltpu.CompilerParams(
            collective_id=4, has_side_effects=True, vmem_limit_bytes=60 * 2**20
        ),
    )(layer_in, dq, dkv.reshape(2, rows, 2 * width), weights, grad_first, norm_low, unit_grad, proj_grad, attn, sums, unit_sums)


def finish_plainly(layer_in, dq, dkv, weights, grad_first, norm_low, unit_grad, proj_grad, attn, sums, unit_sums):
    rows, width = layer_in.shape
    units = unit_grad.shape[1]
    dp, tp = lax.axis_size("dp"), lax.axis_size("tensor")
    third, block, pairs = width // 2, width // dp, tp // 2
    half = lax.rem(lax.axis_index("tensor"), 2)
    both = dkv.reshape(2, rows, 2 * width)
    far = swap_pair(both)
    near = lax.dynamic_index_in_dim(both, half, 0, False)
    own = (near.astype(F32) + far.astype(F32)).astype(BF)
    d_qkv = jnp.concatenate([dq[:, :third], own[:, :width], dq[:, third:], own[:, width:]], axis=1)
    wqkv = weights[0].reshape(width, 2, 4 * third)[:, :, : 3 * third].reshape(width, 3 * width)
    input_grad = grad_first + nt(d_qkv, wqkv)
    grads = [g.astype(BF) for g in (tn(layer_in, d_qkv), tn(proj_grad, attn), tn(norm_low, unit_grad))]
    joined = jnp.concatenate([g.reshape(width, pairs, -1) for g in grads[:2]], axis=2)
    every = jnp.stack([joined.reshape(width, units), grads[2]])
    every = every.reshape(2, dp, block, pairs, 1, units // pairs).transpose(1, 3, 4, 0, 2, 5)
    every = jnp.broadcast_to(every, (dp, pairs, 2, 2, block, units // pairs))
    total = lax.psum_scatter(
        every.reshape(dp * tp, 2, block, units // pairs), ("dp", "tensor"), scatter_dimension=0, tiled=False
    ).astype(F32)
    d_bias = jnp.sum(d_qkv.astype(F32), axis=0).reshape(2, 3, third)
    vec = jnp.concatenate(
        [d_bias[:, 0].reshape(1, width), d_bias[:, 2].reshape(1, width), sums[2:],
         unit_sums[0].reshape(-1, width), jnp.zeros((8 - units // width, width), F32)], axis=0,
    )
    vec = lax.psum(vec, ("dp", "tensor"))

    def chosen(k, lane, w_own):
        return lax.dynamic_slice_in_dim(total[k], lane + half * w_own, w_own, axis=1)

    return (input_grad,) + tuple(chosen(0, i * third, third // 2) for i in range(4)) + (
        chosen(1, 0, units // tp), vec)


def on_device(
    layer_in, query_weight, key_weight, value_weight, output_weight, inner_weight, outer_weight,
    query_bias, value_bias, output_bias, inner_bias, outer_bias, first_gain, first_shift,
    second_gain, second_shift, segment_ids, pad_mask, random_blocks, global_blocks, output_grad,
):
    rows, width = layer_in.shape
    dp, tp = lax.axis_size("dp"), lax.axis_size("tensor")
    own_rows, own_cols = query_weight.shape
    own_units = inner_weight.shape[1]
    third = width // 2
    half = lax.rem(lax.axis_index("tensor"), 2)

    def beside(own):
        zero = jnp.zeros_like(own)
        return jnp.concatenate(
            [jnp.where(half == 0, own, zero), jnp.where(half == 0, zero, own)], axis=1
        )

    units_own = jnp.concatenate([inner_weight, outer_weight.T], axis=1)
    blocks = lax.all_gather(units_own, ("dp", "tensor"), axis=0, tiled=False)
    blocks = blocks.reshape(dp, tp, own_rows, 2 * own_units)
    mine = jnp.concatenate(
        [beside(w) for w in (query_weight, key_weight, value_weight, output_weight.T)], axis=1
    )[None]
    place = lax.axis_index("dp") * tp + lax.axis_index("tensor")
    one, own_bias = query_bias.shape[0], inner_bias.shape[0]
    small = jnp.stack([query_bias, value_bias, output_bias, outer_bias, first_gain, first_shift,
                       second_gain, second_shift])
    eight = lax.dynamic_update_slice(jnp.zeros((8, width), F32), small, (0, place * one))
    unit = lax.dynamic_update_slice(jnp.zeros((8 * width,), F32), inner_bias, (place * own_bias,))
    vec = jnp.concatenate([eight, unit.reshape(8, width)], axis=0)
    begin = start if in_tiles(own_rows) else start_plainly
    weights, qkv, other, vectors = begin(mine, vec, layer_in)

    bounds, row_info, key_info = attention_plan(
        segment_ids, pad_mask, random_blocks, global_blocks, rows
    )
    attn, logs = attend_forward(bounds, qkv, other, row_info, key_info)
    (layer_out, grad_first, grad_attn, norm_low, unit_grad, proj_grad, out_grad, sums, unit_sums) = middle(
        layer_in, attn, output_grad, weights, blocks, vectors
    )
    d_outer = lax.psum_scatter(
        out_grad.reshape((dp * tp,) + out_grad.shape[2:]), ("dp", "tensor"), scatter_dimension=0, tiled=False
    )
    dq, dkv = attend_backward(bounds, qkv, other, row_info, key_info, attn, logs, grad_attn)
    end = finish if in_tiles(own_rows) else finish_plainly
    input_grad, d_q, d_k, d_v, d_o, d_inner, vec = end(
        layer_in, dq, dkv, weights, grad_first, norm_low, unit_grad, proj_grad, attn, sums, unit_sums
    )
    pieces = lax.dynamic_slice_in_dim(vec[:8], place * one, one, axis=1)
    (r_bq, r_bv, r_bo, r_bout, r_g1, r_s1, r_g2, r_s2) = (pieces[i] for i in range(8))
    d_bin = lax.dynamic_slice_in_dim(vec[8:].reshape(-1), place * own_bias, own_bias)
    return (
        layer_out, input_grad, d_q, d_k, d_v, d_o.T, d_inner, d_outer.astype(F32).T,
        r_bq, r_bv, r_bo, d_bin, r_bout, r_g1, r_s1, r_g2, r_s2,
    )


def solution(mesh):
    tokens = P(("dp", "tensor"), None)
    vector = P(("dp", "tensor"))
    cols, turned = P("dp", "tensor"), P("tensor", "dp")
    return jax.shard_map(
        on_device,
        mesh=mesh,
        in_specs=(tokens, cols, cols, cols, turned, cols, turned)
        + (vector,) * 9
        + (P("dp"), P("dp"), P("dp", None, None), P("dp", None, None), tokens),
        out_specs=(tokens, tokens, cols, cols, cols, turned, cols, turned) + (vector,) * 9,
        check_vma=False,
    )
```

```python
from functools import partial

import jax
import jax.numpy as jnp
from jax import lax
from jax.experimental import pallas as pl
from jax.experimental.pallas import tpu as pltpu
from jax.sharding import PartitionSpec as P

HD = 64
PAIR = 2 * HD
QT = 256
KT = 128
ROWS = 256
BACK_ROWS = 256
EPSILON = 1e-06
NEGATIVE = -1e30
MESH = pl.DeviceIdType.MESH
VMEM_LIMIT = 56 * 2**20
BF = jnp.bfloat16
F32 = jnp.float32


def params_of(collective_id=None):
    if collective_id is None:
        return pltpu.CompilerParams(vmem_limit_bytes=VMEM_LIMIT)
    return pltpu.CompilerParams(
        vmem_limit_bytes=VMEM_LIMIT, collective_id=collective_id, has_side_effects=True
    )


def nt(left, right, **more):
    return lax.dot_general(
        left, right, (((1,), (1,)), ((), ())), preferred_element_type=F32, **more
    )


def nn(left, right):
    return lax.dot_general(left, right, (((1,), (0,)), ((), ())), preferred_element_type=F32)


def tn(left, right):
    return lax.dot_general(left, right, (((0,), (0,)), ((), ())), preferred_element_type=F32)


def sibling_of():
    rank = lax.axis_index("tensor")
    half = lax.rem(rank, 2)
    return half, {"tensor": rank + 1 - 2 * half}


def meet(others):
    barrier = pltpu.get_barrier_semaphore()
    for other in others:
        pl.semaphore_signal(barrier, inc=1, device_id=other, device_id_type=MESH)
    pl.semaphore_wait(barrier, len(others))


def swap_keys_kernel(qkv_ref, other_ref, send_sem, recv_sem):
    half, sibling = sibling_of()
    meet([sibling])
    third = qkv_ref.shape[1] // 6
    moves = [
        pltpu.make_async_remote_copy(
            qkv_ref.at[:, (3 * y + 1) * third : (3 * y + 3) * third],
            other_ref.at[:, 2 * y * third : 2 * (y + 1) * third],
            send_sem.at[y], recv_sem.at[y], device_id=sibling, device_id_type=MESH,
        )
        for y in range(2)
    ]
    for move in moves:
        move.start()
    for move in moves:
        move.wait()


def swap_keys(qkv):
    rows, width = qkv.shape
    return pl.pallas_call(
        swap_keys_kernel,
        name="swap_keys",
        out_shape=jax.ShapeDtypeStruct((rows, width * 2 // 3), qkv.dtype),
        in_specs=[pl.BlockSpec(memory_space=pl.ANY)],
        out_specs=pl.BlockSpec(memory_space=pl.ANY),
        scratch_shapes=[pltpu.SemaphoreType.DMA((2,))] * 2,
        compiler_params=params_of(1),
    )(qkv)


def swap_pair_kernel(both_ref, other_ref, send_sem, recv_sem):
    half, sibling = sibling_of()
    meet([sibling])
    away = pltpu.make_async_remote_copy(
        both_ref.at[1 - half], other_ref, send_sem, recv_sem,
        device_id=sibling, device_id_type=MESH,
    )
    away.start()
    away.wait()


def swap_pair(both):
    return pl.pallas_call(
        swap_pair_kernel,
        name="swap_pair",
        out_shape=jax.ShapeDtypeStruct(both.shape[1:], both.dtype),
        in_specs=[pl.BlockSpec(memory_space=pl.ANY)],
        out_specs=pl.BlockSpec(memory_space=pl.ANY),
        scratch_shapes=[pltpu.SemaphoreType.DMA(())] * 2,
        compiler_params=params_of(2),
    )(both)


def places():
    dp, rank = lax.axis_index("dp"), lax.axis_index("tensor")
    core, y = lax.rem(rank, 2), rank // 2
    z, x = dp // 2, lax.rem(dp, 2)
    sibling = {"dp": dp, "tensor": rank + 1 - 2 * core}
    near_x = {"dp": dp + 1 - 2 * x, "tensor": rank}
    near_y = {"dp": dp, "tensor": rank + 2 - 4 * y}
    first = {"dp": dp + (1 - core) * (1 - 2 * x), "tensor": rank + core * (2 - 4 * y)}
    second = {"dp": dp + core * (1 - 2 * x), "tensor": rank + (1 - core) * (2 - 4 * y)}
    xa, ya = x + (1 - core) * (1 - 2 * x), y + core * (1 - 2 * y)
    xb, yb = x + core * (1 - 2 * x), y + (1 - core) * (1 - 2 * y)
    return dict(dp=dp, rank=rank, core=core, y=y, z=z, x=x, sibling=sibling, first=first, second=second,
                xa=xa, ya=ya, xb=xb, yb=yb)


def line_jumps(dp, rank, z, n):
    jumps, hop = [], 1
    while hop < n:
        bit = lax.rem(z // hop, 2)
        jumps.append({"dp": dp + 2 * hop * (1 - 2 * bit), "tensor": rank})
        hop *= 2
    return jumps


def start_kernel(
    n, query_ref, key_ref, value_ref, proj_ref, vec_ref, x_ref, w_hbm, qkv_hbm, other_hbm, vec_out,
    out_ref, chip, sib, mine_ref, qkv, vec_sent, vec_got,
    local_sem, pair_sem, zs, zr, as_, ar, bs, br, ss, sr, ks, kr, vs, vr,
):
    w = places()
    dp, rank, core, y, z, x = (w[k] for k in ("dp", "rank", "core", "y", "z", "x"))
    block, wide = mine_ref.shape[1], mine_ref.shape[2]
    slab = block // 2
    up, down = {"dp": lax.rem(dp + 2, 2 * n), "tensor": rank}, {"dp": lax.rem(dp + 2 * n - 2, 2 * n), "tensor": rank}
    partners = [w["sibling"], w["second"], w["first"]] + line_jumps(dp, rank, z, n)
    own_cols = query_ref.shape[1]
    for i, ref in enumerate((query_ref, key_ref, value_ref, proj_ref)):
        own_w = ref[...]
        zero = jnp.zeros_like(own_w)
        mine_ref[0, :, 2 * i * own_cols : 2 * (i + 1) * own_cols] = jnp.where(
            core == 0, jnp.concatenate([own_w, zero], axis=1), jnp.concatenate([zero, own_w], axis=1)
        )
    meet([up, down] + partners)

    pair = pltpu.make_async_remote_copy(mine_ref, sib, pair_sem.at[0], pair_sem.at[1], device_id=w["sibling"], device_id_type=MESH)
    pair.start()

    def small_send(step):
        return pltpu.make_async_remote_copy(vec_sent.at[step], vec_got.at[step], vs.at[step], vr.at[step], device_id=partners[step], device_id_type=MESH)

    def small_step(step):
        small_send(step).wait_recv()
        vec_sent[step + 1] = vec_sent[step] + vec_got[step]
        if step + 1 < len(partners):
            small_send(step + 1).start()

    vec_sent[0] = vec_ref[...]
    small_send(0).start()
    pair.wait()
    chip[...] = mine_ref[...] + sib[...]
    rows_own = pl.ds(pl.multiple_of(core * slab, slab), slab)
    own_at = pl.ds(pl.multiple_of(dp * block, block), block)
    cols_own = pl.ds(pl.multiple_of(y * wide, wide), wide)
    keep = pltpu.make_async_copy(chip, out_ref.at[:, own_at, cols_own], local_sem.at[0])
    keep.start()

    def spot(g, zi, xi, yi):
        d = zi * 2 + xi
        rows = pl.ds(pl.multiple_of(d * block + core * slab, slab), slab)
        cols = pl.ds(pl.multiple_of(yi * wide, wide), wide)
        return out_ref.at[:, rows, cols]

    def own(g):
        return chip.at[:, rows_own, :]

    def move(g, zi, xi, yi, dev, ssem, rsem, source=None):
        at = spot(g, zi, xi, yi)
        return pltpu.make_async_remote_copy(at if source is None else source, at, ssem, rsem, device_id=dev, device_id_type=MESH)

    def line_up(g, s):
        return move(g, z - s, x, y, up, zs.at[g, 0, s], zr.at[g, 0, s], own(g) if s == 0 else None)

    def line_down(g, s):
        return move(g, z + s, x, y, down, zs.at[g, 1, s], zr.at[g, 1, s], own(g) if s == 0 else None)

    def to_first(g, zi, source=None):
        return move(g, zi, x, y, w["first"], as_.at[g, zi], ar.at[g, zi], source)

    def to_second(g, zi, far, source=None):
        xi, yi = (w["xa"], w["ya"]) if far else (x, y)
        return move(g, zi, xi, yi, w["second"], bs.at[g, far, zi], br.at[g, far, zi], source)

    def to_sibling(g, zi, quarter, source=None):
        xi = (x, w["xa"], w["xb"], w["xa"] + w["xb"] - x)[quarter]
        yi = (y, w["ya"], w["yb"], w["ya"] + w["yb"] - y)[quarter]
        return move(g, zi, xi, yi, w["sibling"], ss.at[g, quarter, zi], sr.at[g, quarter, zi], source)

    def begin(g):
        @pl.when(z < n - 1)
        def _():
            line_up(g, 0).start()

        @pl.when(z > 0)
        def _():
            line_down(g, 0).start()

        to_first(g, z, own(g)).start()
        to_second(g, z, 0, own(g)).start()

    def first_in(g, zi):
        got = move(g, zi, w["xa"], w["ya"], w["first"], as_.at[g, zi], ar.at[g, zi])
        got.wait_recv()
        to_second(g, zi, 1).start()
        to_sibling(g, zi, 1).start()

    def second_in(g, zi, far):
        q = 2 + far
        xi = (w["xb"], w["xa"] + w["xb"] - x)[far]
        yi = (w["yb"], w["ya"] + w["yb"] - y)[far]
        move(g, zi, xi, yi, w["second"], bs.at[g, far, zi], br.at[g, far, zi]).wait_recv()
        to_sibling(g, zi, q).start()

    def below_in(g, s):
        zi = z - 1 - s
        move(g, zi, x, y, up, zs.at[g, 0, s], zr.at[g, 0, s]).wait_recv()
        if s + 1 < n - 1:
            @pl.when(z < n - 1)
            def _():
                line_up(g, s + 1).start()
        to_first(g, zi).start()
        to_second(g, zi, 0).start()
        to_sibling(g, zi, 0).start()

    def above_in(g, s):
        zi = z + 1 + s
        move(g, zi, x, y, down, zs.at[g, 1, s], zr.at[g, 1, s]).wait_recv()
        if s + 1 < n - 1:
            @pl.when(z > 0)
            def _():
                line_down(g, s + 1).start()
        to_first(g, zi).start()
        to_second(g, zi, 0).start()
        to_sibling(g, zi, 0).start()

    def steps(gs):
        for g in gs:
            first_in(g, z)
        for s in range(n - 1):
            @pl.when(z - 1 - s >= 0)
            def _(s=s):
                for g in gs:
                    below_in(g, s)

            @pl.when(z + 1 + s < n)
            def _(s=s):
                for g in gs:
                    above_in(g, s)
            if s > 0:
                both(s, lambda g, zi: first_in(g, zi), gs)
        both(n - 1, lambda g, zi: first_in(g, zi), gs)
        for g in gs:
            second_in(g, z, 0)
        for g in gs:
            second_in(g, z, 1)
        for s in range(1, n):
            both(s, lambda g, zi: second_in(g, zi, 0), gs)
            both(s, lambda g, zi: second_in(g, zi, 1), gs)

    def both(s, what, gs):
        @pl.when(z - s >= 0)
        def _():
            for g in gs:
                what(g, z - s)

        @pl.when(z + s < n)
        def _():
            for g in gs:
                what(g, z + s)

    begin(0)
    small_step(0)
    steps((0,))
    for step in range(1, len(partners)):
        small_step(step)

    keep.wait()
    for zi in range(n):
        for q in range(1, 4):
            to_sibling(0, zi, q).wait_recv()

        @pl.when(zi != z)
        def _(zi=zi):
            to_sibling(0, zi, 0).wait_recv()
    save_w = pltpu.make_async_copy(out_ref, w_hbm, local_sem.at[1])
    save_w.start()

    width = x_ref.shape[1]
    third = width // 2
    vec_out[...] = vec_sent[len(partners)]

    def keys_of(yi):
        return pltpu.make_async_remote_copy(
            qkv.at[:, (3 * yi + 1) * third : (3 * yi + 3) * third],
            other_hbm.at[:, 2 * yi * third : 2 * (yi + 1) * third],
            ks.at[yi], kr.at[yi], device_id=w["sibling"], device_id_type=MESH,
        )

    for yi in range(2):
        first = (3 * yi + 1) * third
        both = nn(x_ref[...], out_ref[0, :, yi * wide + third : yi * wide + 3 * third])
        qkv[:, first : first + third] = both[:, :third].astype(BF)
        bias = vec_out[1:2, yi * third : (yi + 1) * third]
        qkv[:, first + third : first + 2 * third] = (both[:, third:] + bias).astype(BF)
        keys_of(yi).start()
    for yi in range(2):
        first = 3 * yi * third
        bias = vec_out[0:1, yi * third : (yi + 1) * third]
        qkv[:, first : first + third] = (nn(x_ref[...], out_ref[0, :, yi * wide : yi * wide + third]) + bias).astype(BF)

    save_qkv = pltpu.make_async_copy(qkv, qkv_hbm, local_sem.at[2])
    save_qkv.start()
    for g in (0,):
        @pl.when(z < n - 1)
        def _(g=g):
            line_up(g, 0).wait_send()

        @pl.when(z > 0)
        def _(g=g):
            line_down(g, 0).wait_send()
        for s in range(1, n - 1):
            @pl.when((z < n - 1) & (z - s >= 0))
            def _(g=g, s=s):
                line_up(g, s).wait_send()

            @pl.when((z > 0) & (z + s < n))
            def _(g=g, s=s):
                line_down(g, s).wait_send()
        for zi in range(n):
            to_first(g, zi).wait_send()
            for far in range(2):
                to_second(g, zi, far).wait_send()
            for q in range(1, 4):
                to_sibling(g, zi, q).wait_send()
        for zi in range(n):
            @pl.when(zi != z)
            def _(g=g, zi=zi):
                to_sibling(g, zi, 0).wait_send()


    for step in range(len(partners)):
        small_send(step).wait_send()

    for yi in range(2):
        keys_of(yi).wait()
    save_w.wait()
    save_qkv.wait()


def start(own, vec, layer_in):
    dp, tp = lax.axis_size("dp"), lax.axis_size("tensor")
    n = dp // 2
    block, own_cols = own[0].shape
    parts, wide = 1, 2 * len(own) * own_cols
    piece = pltpu.VMEM((parts, block, wide), BF)
    rows, width = layer_in.shape
    steps = 3 + (n - 1).bit_length()
    dma = pltpu.SemaphoreType.DMA
    anywhere, inside = pl.BlockSpec(memory_space=pl.ANY), pl.BlockSpec(memory_space=pltpu.VMEM)
    whole = (parts, dp * block, wide * tp // 2)
    return pl.pallas_call(
        partial(start_kernel, n),
        name="start",
        in_specs=[inside] * 6,
        out_specs=[anywhere] * 3 + [inside],
        out_shape=[
            jax.ShapeDtypeStruct(whole, BF),
            jax.ShapeDtypeStruct((rows, 3 * width), BF),
            jax.ShapeDtypeStruct((rows, 2 * width), BF),
            jax.ShapeDtypeStruct(vec.shape, F32),
        ],
        scratch_shapes=[
            pltpu.VMEM(whole, BF), piece, piece, piece,
            pltpu.VMEM((rows, 3 * width), BF),
            pltpu.VMEM((steps + 1,) + vec.shape, F32), pltpu.VMEM((steps,) + vec.shape, F32),
            dma((3,)), dma((2,)), dma((1, 2, n)), dma((1, 2, n)), dma((1, n)), dma((1, n)),
            dma((1, 2, n)), dma((1, 2, n)), dma((1, 4, n)), dma((1, 4, n)), dma((2,)), dma((2,)),
            dma((steps,)), dma((steps,)),
        ],
        compiler_params=params_of(3),
    )(*own, vec, layer_in)


def in_tiles(block):
    return block % 32 == 0


def start_plainly(own, vec, layer_in):
    dp, tp = lax.axis_size("dp"), lax.axis_size("tensor")
    half = lax.rem(lax.axis_index("tensor"), 2)

    def beside(one):
        zero = jnp.zeros_like(one)
        return jnp.concatenate(
            [jnp.where(half == 0, one, zero), jnp.where(half == 0, zero, one)], axis=1
        )

    mine = jnp.concatenate([beside(one) for one in own], axis=1)[None]
    parts, block, wide = mine.shape
    width = layer_in.shape[1]
    third = width // 2
    every = lax.all_gather(mine, ("dp", "tensor"), axis=0, tiled=False)
    every = every.reshape(dp, tp // 2, 2, parts, block, wide).sum(axis=2)
    weights = every.transpose(2, 0, 3, 1, 4).reshape(parts, dp * block, tp // 2 * wide)
    vec = lax.psum(vec, ("dp", "tensor"))
    zero = jnp.zeros((1, third), F32)
    bias = jnp.concatenate(
        [v for y in range(2) for v in (vec[:1, y * third : (y + 1) * third], zero,
                                       vec[1:2, y * third : (y + 1) * third])], axis=1,
    )
    wqkv = weights[0].reshape(width, 2, 4 * third)[:, :, : 3 * third].reshape(width, 3 * width)
    qkv = (nn(layer_in, wqkv) + bias).astype(BF)
    return weights, qkv, swap_keys(qkv), vec


def q_lanes(p, pairs):
    third = pairs // 2 * PAIR
    first = p // (pairs // 2) * 3 * third + p % (pairs // 2) * PAIR
    return slice(first, first + PAIR)


def k_lanes(p, pairs):
    third = pairs // 2 * PAIR
    first = p // (pairs // 2) * 2 * third + p % (pairs // 2) * PAIR
    return slice(first, first + PAIR)


def v_lanes(p, pairs):
    third = pairs // 2 * PAIR
    lanes = k_lanes(p, pairs)
    return slice(lanes.start + third, lanes.stop + third)


def key_tile(j, qkv_ref, other_ref, kv, sems):
    rows, third = other_ref.shape[0], other_ref.shape[1] // 4
    here = pl.ds(pl.multiple_of(j * KT, KT), KT)
    from_row = pl.ds(pl.multiple_of(lax.rem(j * KT, rows), KT), KT)
    own = [
        pltpu.make_async_copy(
            qkv_ref.at[from_row, (3 * y + 1) * third : (3 * y + 3) * third],
            kv.at[here, 2 * y * third : 2 * (y + 1) * third],
            sems.at[y, j],
        )
        for y in range(2)
    ]
    far = pltpu.make_async_copy(other_ref.at[from_row, :], kv.at[here, :], sems.at[0, j])
    is_own = (j * KT) // rows == lax.rem(lax.axis_index("tensor"), 2)
    return is_own, own, far


def fetch_keys(low, high, qkv_ref, other_ref, kv, sems, use):
    @pl.loop(low, high)
    def _(j):
        is_own, own, far = key_tile(j, qkv_ref, other_ref, kv, sems)

        @pl.when(is_own)
        def _():
            for move in own:
                move.start()

        @pl.when(jnp.logical_not(is_own))
        def _():
            far.start()

    @pl.loop(low, high)
    def _(j):
        is_own, own, far = key_tile(j, qkv_ref, other_ref, kv, sems)

        @pl.when(is_own)
        def _():
            for move in own:
                move.wait()

        @pl.when(jnp.logical_not(is_own))
        def _():
            far.wait()
        use(j)


def masked_pairs(source, target, lanes_of, pairs, scale):
    rows = source.shape[0]
    low_lanes = lax.broadcasted_iota(jnp.int32, (rows, PAIR), 1) < HD
    for p in range(pairs):
        both = source[:, lanes_of(p)]
        if scale is not None:
            both = both * jnp.asarray(scale, both.dtype)
        zero = jnp.zeros_like(both)
        target[p, :rows, :] = jnp.where(low_lanes, both, zero)
        target[p, rows:, :] = jnp.where(low_lanes, zero, both)


def tile_bias(j, q_first, row_info, key_info, bias):
    seg_q, bits_q = row_info[0:1, :], row_info[1:2, :]
    queries = bias.shape[1]
    for part in range(KT // HD):
        block = j * (KT // HD) + part
        bit = jnp.bitwise_and(
            lax.shift_right_logical(bits_q, jnp.full_like(bits_q, block)), 1
        )
        wanted = jnp.where(bit == 1, seg_q, -1)
        base = pl.multiple_of(j * KT + part * HD, HD)
        seg_k = key_info[pl.ds(base, HD), :]
        key_at = base + lax.broadcasted_iota(jnp.int32, (HD, queries), 0)
        query_at = q_first + lax.broadcasted_iota(jnp.int32, (HD, queries), 1)
        allowed = (seg_k == wanted) | (key_at == query_at)
        bias[part * HD : (part + 1) * HD, :] = jnp.where(allowed, 0.0, NEGATIVE)


def attend_forward_kernel(
    bounds, q_ref, qkv_ref, other_ref, row_info, key_info, out_ref, log_ref,
    q_pairs, kv_ref, v_turned, bias, top, total, acc, scores, fades, lows, sems,
):
    step = pl.program_id(0)
    rows, width = out_ref.shape
    pairs = width // PAIR
    tiles = kv_ref.shape[0] // KT

    @pl.when(step == 0)
    def _():
        def turn(j):
            for p in range(pairs):
                span = slice(p * PAIR, (p + 1) * PAIR)
                v_turned[j, span, :] = kv_ref[pl.ds(pl.multiple_of(j * KT, KT), KT), v_lanes(p, pairs)].T

        fetch_keys(bounds[0, 0], bounds[pl.num_programs(0) - 1, 1], qkv_ref, other_ref, kv_ref, sems, turn)

    masked_pairs(q_ref, q_pairs, partial(q_lanes, pairs=pairs), pairs, HD**-0.5)
    top[...] = jnp.full_like(top, NEGATIVE)
    total[...] = jnp.zeros_like(total)
    acc[...] = jnp.zeros_like(acc)
    q_first = bounds[step, 2]

    @pl.loop(bounds[step, 0], bounds[step, 1])
    def _(j):
        tile_bias(j, q_first, row_info, key_info, bias)
        keys_at = pl.multiple_of(j * KT, KT)
        for p in range(pairs):
            keys = kv_ref[pl.ds(keys_at, KT), k_lanes(p, pairs)]
            scores[p] = nt(keys, q_pairs[p])
        for h in range(2 * pairs):
            p, e = divmod(h, 2)
            mine = scores[p, :, e * rows : (e + 1) * rows] + bias[...]
            before = top[h : h + 1, :]
            now = jnp.maximum(before, jnp.max(mine, axis=0, keepdims=True))
            fade = jnp.exp(before - now)
            expos = jnp.exp(mine - now)
            top[h : h + 1, :] = now
            fades[h : h + 1, :] = fade
            total[h : h + 1, :] = fade * total[h : h + 1, :] + jnp.sum(
                expos, axis=0, keepdims=True
            )
            lows[h] = expos.astype(BF)
        for h in range(2 * pairs):
            span = slice(h * HD, (h + 1) * HD)
            acc[span, :] = acc[span, :] * fades[h : h + 1, :] + nn(v_turned[j, span, :], lows[h])

    heads = width // HD
    for h in range(heads):
        span = slice(h * HD, (h + 1) * HD)
        acc[span, :] = acc[span, :] / total[h : h + 1, :]
    out_ref[...] = acc[...].T.astype(BF)
    log_ref[...] = top[...] + jnp.log(jnp.maximum(total[...], 1e-37))


def attend_forward(bounds, qkv, other, row_info, key_info):
    rows, width = qkv.shape[0], qkv.shape[1] // 3
    keys = 2 * rows
    stat_rows = 16
    return pl.pallas_call(
        attend_forward_kernel,
        name="attend_forward",
        grid_spec=pltpu.PrefetchScalarGridSpec(
            num_scalar_prefetch=1,
            grid=(rows // QT,),
            in_specs=[
                pl.BlockSpec((QT, 3 * width), lambda i, b: (i, 0)),
                pl.BlockSpec(memory_space=pl.ANY),
                pl.BlockSpec(memory_space=pl.ANY),
                pl.BlockSpec((8, QT), lambda i, b: (0, i)),
                pl.BlockSpec((keys, 1), lambda i, b: (0, 0), pipeline_mode=pl.Buffered(1)),
            ],
            out_specs=[
                pl.BlockSpec((QT, width), lambda i, b: (i, 0)),
                pl.BlockSpec((stat_rows, QT), lambda i, b: (0, i)),
            ],
            scratch_shapes=[
                pltpu.VMEM((width // PAIR, 2 * QT, PAIR), BF),
                pltpu.VMEM((keys, 2 * width), BF),
                pltpu.VMEM((keys // KT, width, KT), BF),
                pltpu.VMEM((KT, QT), F32),
                pltpu.VMEM((stat_rows, QT), F32),
                pltpu.VMEM((stat_rows, QT), F32),
                pltpu.VMEM((width, QT), F32),
                pltpu.VMEM((width // PAIR, KT, 2 * QT), F32),
                pltpu.VMEM((stat_rows, QT), F32),
                pltpu.VMEM((width // HD, KT, QT), BF),
                pltpu.SemaphoreType.DMA((2, keys // KT)),
            ],
        ),
        out_shape=[
            jax.ShapeDtypeStruct((rows, width), BF),
            jax.ShapeDtypeStruct((stat_rows, rows), F32),
        ],
        compiler_params=params_of(),
    )(bounds, qkv, qkv, other, row_info, key_info)


def attend_backward_kernel(
    bounds, q_ref, qkv_ref, other_ref, row_info, key_info, out_ref, log_ref, grad_ref,
    dq_ref, dkv_ref, q_pairs, g_pairs, kv_ref, k_turned, bias, inner, dq_acc, dkv_acc,
    scores, changes, probs, grads, sems,
):
    step = pl.program_id(0)
    rows, width = out_ref.shape
    pairs = width // PAIR
    tiles = kv_ref.shape[0] // KT

    @pl.when(step == 0)
    def _():
        def turn(j):
            for p in range(pairs):
                span = slice(p * PAIR, (p + 1) * PAIR)
                k_turned[j, span, :] = kv_ref[pl.ds(pl.multiple_of(j * KT, KT), KT), k_lanes(p, pairs)].T

        fetch_keys(bounds[0, 0], bounds[pl.num_programs(0) - 1, 1], qkv_ref, other_ref, kv_ref, sems, turn)
        dkv_acc[...] = jnp.zeros_like(dkv_acc)

    masked_pairs(q_ref, q_pairs, partial(q_lanes, pairs=pairs), pairs, HD**-0.5)
    masked_pairs(grad_ref, g_pairs, lambda p: slice(p * PAIR, (p + 1) * PAIR), pairs, None)
    dq_acc[...] = (out_ref[...].astype(F32) * grad_ref[...].astype(F32)).T
    for h in range(2 * pairs):
        inner[h : h + 1, :] = jnp.sum(dq_acc[h * HD : (h + 1) * HD, :], axis=0, keepdims=True)
    dq_acc[...] = jnp.zeros_like(dq_acc)
    q_first = bounds[step, 2]

    @pl.loop(bounds[step, 0], bounds[step, 1])
    def _(j):
        tile_bias(j, q_first, row_info, key_info, bias)
        here = pl.ds(pl.multiple_of(j * KT, KT), KT)
        for p in range(pairs):
            scores[p] = nt(kv_ref[here, k_lanes(p, pairs)], q_pairs[p])
            changes[p] = nt(kv_ref[here, v_lanes(p, pairs)], g_pairs[p])
        for h in range(2 * pairs):
            p, e = divmod(h, 2)
            cols = slice(e * rows, (e + 1) * rows)
            prob = jnp.exp(scores[p, :, cols] + bias[...] - log_ref[h : h + 1, :])
            probs[p, :, cols] = prob.astype(BF)
            grads[p, :, cols] = (prob * (changes[p, :, cols] - inner[h : h + 1, :])).astype(BF)
        for p in range(pairs):
            dkv_acc[here, k_lanes(p, pairs)] += nn(grads[p], q_pairs[p])
            dkv_acc[here, v_lanes(p, pairs)] += nn(probs[p], g_pairs[p])
        for h in range(2 * pairs):
            p, e = divmod(h, 2)
            span = slice(h * HD, (h + 1) * HD)
            dq_acc[span, :] += nn(k_turned[j, span, :], grads[p, :, e * rows : (e + 1) * rows])

    dq_ref[...] = (dq_acc[...] * HD**-0.5).T.astype(BF)

    @pl.when(step == pl.num_programs(0) - 1)
    def _():
        dkv_ref[...] = dkv_acc[...].astype(BF)


def attend_backward(bounds, qkv, other, row_info, key_info, attn, logs, grad_attn):
    rows, width = attn.shape
    keys = 2 * rows
    stat_rows = logs.shape[0]
    whole = dict(pipeline_mode=pl.Buffered(1))
    return pl.pallas_call(
        attend_backward_kernel,
        name="attend_backward",
        grid_spec=pltpu.PrefetchScalarGridSpec(
            num_scalar_prefetch=1,
            grid=(rows // QT,),
            in_specs=[
                pl.BlockSpec((QT, 3 * width), lambda i, b: (i, 0)),
                pl.BlockSpec(memory_space=pl.ANY),
                pl.BlockSpec(memory_space=pl.ANY),
                pl.BlockSpec((8, QT), lambda i, b: (0, i)),
                pl.BlockSpec((keys, 1), lambda i, b: (0, 0), **whole),
                pl.BlockSpec((QT, width), lambda i, b: (i, 0)),
                pl.BlockSpec((stat_rows, QT), lambda i, b: (0, i)),
                pl.BlockSpec((QT, width), lambda i, b: (i, 0)),
            ],
            out_specs=[
                pl.BlockSpec((QT, width), lambda i, b: (i, 0)),
                pl.BlockSpec((keys, 2 * width), lambda i, b: (0, 0), **whole),
            ],
            scratch_shapes=[
                pltpu.VMEM((width // PAIR, 2 * QT, PAIR), BF),
                pltpu.VMEM((width // PAIR, 2 * QT, PAIR), BF),
                pltpu.VMEM((keys, 2 * width), BF),
                pltpu.VMEM((keys // KT, width, KT), BF),
                pltpu.VMEM((KT, QT), F32),
                pltpu.VMEM((stat_rows, QT), F32),
                pltpu.VMEM((width, QT), F32),
                pltpu.VMEM((keys, 2 * width), F32),
                pltpu.VMEM((width // PAIR, KT, 2 * QT), F32),
                pltpu.VMEM((width // PAIR, KT, 2 * QT), F32),
                pltpu.VMEM((width // PAIR, KT, 2 * QT), BF),
                pltpu.VMEM((width // PAIR, KT, 2 * QT), BF),
                pltpu.SemaphoreType.DMA((2, keys // KT)),
            ],
        ),
        out_shape=[
            jax.ShapeDtypeStruct((rows, width), BF),
            jax.ShapeDtypeStruct((keys, 2 * width), BF),
        ],
        compiler_params=params_of(),
    )(bounds, qkv, qkv, other, row_info, key_info, attn, logs, grad_attn)


def attention_plan(segment_ids, pad_mask, random_blocks, global_blocks, rows):
    seq_count, nblocks = random_blocks.shape[0], random_blocks.shape[1]
    seq_len = segment_ids.shape[0] // seq_count
    rank = lax.axis_index("tensor")
    seq, half = rank // 2, lax.rem(rank, 2)
    segs = lax.dynamic_index_in_dim(segment_ids.reshape(seq_count, seq_len), seq, 0, False)
    pads = lax.dynamic_index_in_dim(pad_mask.reshape(seq_count, seq_len), seq, 0, False)
    randoms = lax.dynamic_index_in_dim(random_blocks, seq, 0, False)
    globs = lax.dynamic_index_in_dim(global_blocks, seq, 0, False)
    block_size = seq_len // nblocks
    one = jnp.int32(1)
    block = jnp.arange(nblocks, dtype=jnp.int32)

    def either(a, b):
        return jnp.bitwise_or(a, b)

    block_bits = lax.shift_left(one, block)
    window = either(
        block_bits,
        either(
            jnp.where(block > 0, lax.shift_left(one, jnp.maximum(block - 1, 0)), 0),
            jnp.where(
                block < nblocks - 1, lax.shift_left(one, jnp.minimum(block + 1, nblocks - 1)), 0
            ),
        ),
    )
    for r in range(randoms.shape[1]):
        window = either(window, lax.shift_left(one, randoms[:, r]))
    glob_bits = either(lax.shift_left(one, globs[:, 0]), lax.shift_left(one, globs[:, 1]))
    first = half * rows
    seg_q = lax.dynamic_slice_in_dim(segs, first, rows)
    own_bits = lax.dynamic_slice_in_dim(window, half * (rows // block_size), rows // block_size)
    bits = jnp.broadcast_to(own_bits[:, None], (rows // block_size, block_size)).reshape(rows)
    numbers = jnp.arange(globs.shape[0], dtype=jnp.int32)
    is_doc = seg_q[None, :] == numbers[:, None]
    bits = either(bits, jnp.sum(jnp.where(is_doc, glob_bits[:, None], 0), axis=0))
    row_info = jnp.concatenate(
        [seg_q[None], bits[None], jnp.zeros((6, rows), jnp.int32)], axis=0
    )
    key_info = jnp.where(pads == 1, segs, -2)[:, None]
    tiles = seg_q.reshape(rows // QT, QT)
    low = jnp.sum((segs[None, :] < tiles[:, :1]).astype(jnp.int32), axis=1)
    high = jnp.sum((segs[None, :] <= tiles[:, -1:]).astype(jnp.int32), axis=1)
    starts = first + QT * jnp.arange(rows // QT, dtype=jnp.int32)
    bounds = jnp.stack([low // KT, (high + KT - 1) // KT, starts, starts], axis=1)
    return bounds, row_info, key_info


TAIL_STEP = 0.47
TAIL = (0.266306628, 0.248031891, 0.336199252, -0.126105651, 0.607561554, -0.420410983, 0.0884173167)


def gelu_and_slope(pre):
    bell = jnp.exp(-0.5 * pre * pre)
    t = 1.0 / (1.0 + (TAIL_STEP * 0.5**0.5) * jnp.abs(pre))
    tail = TAIL[-1]
    for c in TAIL[-2::-1]:
        tail = tail * t + c
    tail = 0.5 * (tail * t) * bell
    cdf = jnp.where(pre < 0, tail, 1.0 - tail)
    return pre * cdf, cdf + pre * (bell * (2.0 * 3.141592653589793) ** -0.5)


def normalize(resid):
    center = resid - jnp.mean(resid, axis=1, keepdims=True)
    inverse = lax.rsqrt(jnp.mean(center * center, axis=1, keepdims=True) + EPSILON)
    return center * inverse, inverse


def norm_backward(grad_normed, normal_hat, inverse, gain):
    grad_hat = grad_normed * gain
    return inverse * (
        grad_hat
        - jnp.mean(grad_hat, axis=1, keepdims=True)
        - normal_hat * jnp.mean(grad_hat * normal_hat, axis=1, keepdims=True)
    )


def fetch_blocks(blocks_hbm, blocks_ref, sems):
    return [
        pltpu.make_async_copy(blocks_hbm.at[:, t], blocks_ref.at[:, t], sems.at[t])
        for t in range(blocks_ref.shape[1])
    ]


def begin_fetch(blocks_hbm, blocks_ref, sems):
    @pl.when(pl.program_id(0) == 0)
    def _():
        for move in fetch_blocks(blocks_hbm, blocks_ref, sems):
            move.start()


def end_fetch(blocks_hbm, blocks_ref, sems):
    @pl.when(pl.program_id(0) == 0)
    def _():
        for move in fetch_blocks(blocks_hbm, blocks_ref, sems):
            move.wait()


def unit_chunks(blocks_ref):
    dp, tp, own_rows, both = blocks_ref.shape
    units = both // 2
    for t in range(tp):
        w_in = lambda t=t: blocks_ref[:, t, :, :units].reshape(dp * own_rows, units)
        w_out = lambda t=t: blocks_ref[:, t, :, units:].reshape(dp * own_rows, units)
        yield t, slice(t * units, (t + 1) * units), w_in, w_out


def forth_kernel(
    x_ref, attn_ref, cot_ref, proj_0, proj_1, blocks_hbm, vec_ref,
    final_ref, resid_out, grad_out, norm_low, slope, ffn_grad, out_grad, sums, hidden, outer, blocks_ref, sems,
):
    begin_fetch(blocks_hbm, blocks_ref, sems)
    out_bias, last_bias, gain_1, shift_1, gain_2, shift_2 = (vec_ref[i : i + 1, :] for i in range(2, 8))

    @pl.when(pl.program_id(0) == 0)
    def _():
        sums[...] = jnp.zeros_like(sums)
        outer[...] = jnp.zeros_like(outer)

    resid = x_ref[...].astype(F32) + out_bias
    third = proj_0.shape[2]
    resid += nt(attn_ref[:, :third], proj_0[0]) + nt(attn_ref[:, third:], proj_1[0])
    resid_out[...] = resid
    hat, _ = normalize(resid)
    first_norm = hat * gain_1 + shift_1
    low = first_norm.astype(BF)
    norm_low[...] = low
    resid = first_norm + last_bias
    end_fetch(blocks_hbm, blocks_ref, sems)
    chunks = list(unit_chunks(blocks_ref))
    dp, tp, own_rows, both = blocks_ref.shape
    units, sub = both // 2, 256
    per = units // sub

    def before(c):
        first = c % per * sub
        left = blocks_ref[:, c // per, :, first : first + sub].reshape(dp * own_rows, sub)
        return nn(low, left) + vec_ref[8 + c // per : 9 + c // per, first : first + sub]

    pre = before(0)
    for c in range(tp * per):
        after = before(c + 1) if c + 1 < tp * per else None
        here = slice(c * sub, (c + 1) * sub)
        act, slope[:, here] = gelu_and_slope(pre)
        hidden[:, here] = act.astype(BF)
        pre = after
        done = c - 0
        if done >= 0 and done % per == per - 1:
            t, cols, _, w_out = chunks[done // per]
            resid += nt(hidden[:, cols], w_out())
    for c in range(tp * per - 0, tp * per):
        if c % per == per - 1:
            t, cols, _, w_out = chunks[c // per]
            resid += nt(hidden[:, cols], w_out())
    hat, inverse = normalize(resid)
    final_ref[...] = (hat * gain_2 + shift_2).astype(BF)
    cot = cot_ref[...].astype(F32)
    grad = norm_backward(cot, hat, inverse, gain_2)
    sums[6:7, :] += jnp.sum(cot * hat, axis=0, keepdims=True)
    sums[7:8, :] += jnp.sum(cot, axis=0, keepdims=True)
    sums[3:4, :] += jnp.sum(grad, axis=0, keepdims=True)
    grad_out[...] = grad
    low = grad.astype(BF)
    ffn_grad[...] = low
    turned = low.T
    for t, cols, _, _ in unit_chunks(blocks_ref):
        outer[t] += nn(turned, hidden[:, cols])

    @pl.when(pl.program_id(0) == pl.num_programs(0) - 1)
    def _():
        for t in range(out_grad.shape[1]):
            out_grad[:, t] = outer[t].reshape(out_grad.shape[0], out_grad.shape[2], out_grad.shape[3]).astype(BF)


def back_kernel(
    resid_ref, grad_ref, ffn_grad, slope, proj_0, proj_1, blocks_hbm, vec_ref, sums_ref,
    first_grad, attn_grad, unit_grad, proj_grad, sums, unit_sums, blocks_ref, sems,
):
    begin_fetch(blocks_hbm, blocks_ref, sems)
    @pl.when(pl.program_id(0) == 0)
    def _():
        sums[...] = sums_ref[...]
        unit_sums[...] = jnp.zeros_like(unit_sums)

    hat, inverse = normalize(resid_ref[...])
    low = ffn_grad[...]
    grad = grad_ref[...]
    end_fetch(blocks_hbm, blocks_ref, sems)
    for t, cols, w_in, w_out in unit_chunks(blocks_ref):
        act = (nn(low, w_out()) * slope[:, cols]).astype(BF)
        unit_grad[:, cols] = act
        unit_sums[0:1, cols] += jnp.sum(act.astype(F32), axis=0, keepdims=True)
        grad += nt(act, w_in())
    sums[4:5, :] += jnp.sum(grad * hat, axis=0, keepdims=True)
    sums[5:6, :] += jnp.sum(grad, axis=0, keepdims=True)
    grad = norm_backward(grad, hat, inverse, vec_ref[4:5, :])
    sums[2:3, :] += jnp.sum(grad, axis=0, keepdims=True)
    first_grad[...] = grad
    low = grad.astype(BF)
    proj_grad[...] = low
    third = proj_0.shape[2]
    attn_grad[:, :third] = nn(low, proj_0[0]).astype(BF)
    attn_grad[:, third:] = nn(low, proj_1[0]).astype(BF)


def middle(layer_in, attn, output_grad, weights, blocks, vectors):
    rows, width = layer_in.shape
    tp, own_units = blocks.shape[1], blocks.shape[3] // 2
    units = tp * own_units
    once = dict(pipeline_mode=pl.Buffered(1))
    whole = lambda a: pl.BlockSpec(a.shape, lambda i: (0,) * len(a.shape), **once)
    fixed = lambda w: pl.BlockSpec((8, w), lambda i: (0, 0))
    shape = lambda w, t: jax.ShapeDtypeStruct((rows, w), t)
    sums_of = lambda w: jax.ShapeDtypeStruct((8, w), F32)
    out_grad = jax.ShapeDtypeStruct(blocks.shape[:3] + (own_units,), BF)
    third = width // 2
    proj = [pl.BlockSpec((1, width, third), lambda i, y=y: (0, 0, 4 * y + 3), **once) for y in range(2)]
    held = [pltpu.VMEM(blocks.shape, BF), pltpu.SemaphoreType.DMA((tp,))]
    tile = lambda w: pl.BlockSpec((ROWS, w), lambda i: (i, 0))
    layer_out, resid, grad_second, norm_low, slope, ffn_grad, out_grad, sums = pl.pallas_call(
        forth_kernel,
        name="middle_forth",
        grid=(rows // ROWS,),
        in_specs=[tile(width)] * 3 + proj + [pl.BlockSpec(memory_space=pl.ANY), whole(vectors)],
        out_specs=[tile(width)] * 4 + [tile(units), tile(width), whole(out_grad), fixed(width)],
        out_shape=[
            shape(width, BF), shape(width, F32), shape(width, F32), shape(width, BF), shape(units, F32),
            shape(width, BF), out_grad, sums_of(width),
        ],
        scratch_shapes=[pltpu.VMEM((ROWS, units), BF), pltpu.VMEM((tp, width, own_units), F32)] + held,
        compiler_params=params_of(),
    )(layer_in, attn, output_grad, weights, weights, blocks, vectors)
    tile = lambda w: pl.BlockSpec((BACK_ROWS, w), lambda i: (i, 0))
    first_grad, attn_grad, unit_grad, proj_grad, sums, unit_sums = pl.pallas_call(
        back_kernel,
        name="middle_back",
        grid=(rows // BACK_ROWS,),
        in_specs=[tile(width)] * 3 + [tile(units)] + proj + [pl.BlockSpec(memory_space=pl.ANY), whole(vectors), whole(sums)],
        out_specs=[tile(width)] * 2 + [tile(units), tile(width), fixed(width), fixed(units)],
        out_shape=[
            shape(width, F32), shape(width, BF), shape(units, BF), shape(width, BF), sums_of(width), sums_of(units),
        ],
        scratch_shapes=held,
        compiler_params=params_of(),
    )(resid, grad_second, ffn_grad, slope, weights, weights, blocks, vectors, sums)
    return layer_out, first_grad, attn_grad, norm_low, unit_grad, proj_grad, out_grad, sums, unit_sums


def finish_kernel(
    n, x_hbm, dq_hbm, dkv_hbm, w_hbm, first_hbm, low_hbm, unit_hbm, proj_hbm, attn_hbm, sums_ref, unit_sums,
    input_hbm, q_out, k_out, v_out, o_out, in_out, vec_out,
    rows_in, turned, unit, d_qkv, attn, far, w_all, tile_in, tile_out, grads, sib, from_b, from_a, from_low, from_high,
    result, vec_sent, vec_got,
    load, swap_s, swap_r, ss, sr, bs, br, as_, ar, zs, zr, es, er, vs, vr, tile_sem,
):
    w = places()
    dp, rank, core, y, z, x = (w[k] for k in ("dp", "rank", "core", "y", "z", "x"))
    rows, width = x_hbm.shape
    third = width // 2
    wide = unit.shape[1] // 2
    slab = result.shape[1] // 2
    up, down = {"dp": lax.rem(dp + 2, 2 * n), "tensor": rank}, {"dp": lax.rem(dp + 2 * n - 2, 2 * n), "tensor": rank}
    partners = [w["sibling"], w["second"], w["first"]] + line_jumps(dp, rank, z, n)
    barrier = pltpu.get_barrier_semaphore()
    for other in partners + [up, down]:
        pl.semaphore_signal(barrier, inc=1, device_id=other, device_id_type=MESH)

    def fetch(i, src, dst):
        return pltpu.make_async_copy(src, dst, load.at[i])

    fetch_low = fetch(0, low_hbm, rows_in.at[0])
    fetch_unit = fetch(1, unit_hbm, unit)
    fetch_x = fetch(2, x_hbm, rows_in.at[1])
    fetch_proj = fetch(3, proj_hbm, rows_in.at[2])
    fetch_attn = fetch(4, attn_hbm, attn)
    fetch_w = fetch(5, w_hbm.at[0], w_all)
    fetch_dq = [fetch(6 + h, dq_hbm.at[:, h * third : (h + 1) * third], d_qkv.at[:, 3 * h * third : (3 * h + 1) * third]) for h in range(2)]
    fetch_kv = [fetch(8 + h, dkv_hbm.at[core, :, 2 * h * third : 2 * (h + 1) * third], d_qkv.at[:, (3 * h + 1) * third : (3 * h + 3) * third]) for h in range(2)]
    for move in [fetch_low, fetch_unit, fetch_x, fetch_proj, fetch_attn] + fetch_dq + fetch_kv + [fetch_w]:
        move.start()
    pl.semaphore_wait(barrier, len(partners) + 2)

    def copy(src, dst, ssem, rsem, dev):
        return pltpu.make_async_remote_copy(src, dst, ssem, rsem, device_id=dev, device_id_type=MESH)

    swap = copy(dkv_hbm.at[1 - core], far, swap_s, swap_r, w["sibling"])
    swap.start()

    def turn_rows(i):
        for c in range(0, width, 128):
            turned[i, c : c + 128, :] = rows_in[i, :, c : c + 128].T

    places_of = [xd * 2 + yd for xd, yd in (
        (x, y), (w["xa"], w["ya"]), (w["xb"], w["yb"]), (w["xa"] + w["xb"] - x, w["ya"] + w["yb"] - y))]
    mine = grads.at[core]

    def keep(k, zd, yd, lane, value):
        for xd in range(2):
            for c in range(2):
                first = (xd * 2 + c) * slab
                grads[c, k, zd, xd * 2 + yd, :, lane : lane + value.shape[1]] = value[first : first + slab, :].astype(BF)

    def rows_of_line(i, zd):
        return turned[i, pl.ds(pl.multiple_of(zd * 4 * slab, 4 * slab), 4 * slab), :]

    def compute_inner(zd):
        left = rows_of_line(0, zd)
        for yd in range(2):
            for lane in range(0, wide, 768):
                keep(1, zd, yd, lane, nn(left, unit[:, yd * wide + lane : yd * wide + lane + 768]))

    def compute_others(zd):
        left = rows_of_line(1, zd)
        for yd in range(2):
            for i in range(3):
                at = (3 * yd + i) * third
                keep(0, zd, yd, i * third, nn(left, d_qkv[:, at : at + third]))
        left = rows_of_line(2, zd)
        for yd in range(2):
            keep(0, zd, yd, 3 * third, nn(left, attn[:, yd * third : (yd + 1) * third]))

    def to_sibling(k, zd):
        return copy(grads.at[1 - core, k, zd], sib.at[k, zd], ss.at[k, zd], sr.at[k, zd], w["sibling"])

    def over_b(k, far_side, zd):
        place = places_of[2 + far_side]
        return copy(mine.at[k, zd, place], from_b.at[k, far_side, zd], bs.at[k, far_side, zd], br.at[k, far_side, zd], w["second"])

    def over_a(k, zd):
        return copy(mine.at[k, zd, places_of[1]], from_a.at[k, zd], as_.at[k, zd], ar.at[k, zd], w["first"])

    def over_up(k, zd):
        return copy(mine.at[k, zd, places_of[0]], from_low.at[k, zd], zs.at[k, zd], zr.at[0, k, zd], up)

    def over_down(k, zd):
        return copy(mine.at[k, zd, places_of[0]], from_high.at[k, zd], zs.at[k, zd], zr.at[1, k, zd], down)

    def put(q, k, zd, more):
        place = places_of[q]
        total = grads[core, k, zd, place].astype(F32) + sib[k, zd, place].astype(F32)
        for term in more:
            total = total + term[...].astype(F32)
        grads[core, k, zd, place] = total.astype(BF)

    def stage_b(k, zd):
        to_sibling(k, zd).wait_recv()
        for far_side in (1, 0):
            put(2 + far_side, k, zd, ())
            over_b(k, far_side, zd).start()

    def stage_a(k, zd):
        over_b(k, 1, zd).wait_recv()
        put(1, k, zd, (from_b.at[k, 1, zd],))
        over_a(k, zd).start()

    def stage_line(k, zd):
        over_b(k, 0, zd).wait_recv()
        over_a(k, zd).wait_recv()
        put(0, k, zd, (from_b.at[k, 0, zd], from_a.at[k, zd]))

        @pl.when((zd > z) & (z == 0))
        def _():
            over_up(k, zd).start()

        @pl.when((zd < z) & (z == n - 1))
        def _():
            over_down(k, zd).start()

    def grow(k, zd, term):
        place = places_of[0]
        grads[core, k, zd, place] = (grads[core, k, zd, place].astype(F32) + term[...].astype(F32)).astype(BF)

    def stage_hop(k, zd):
        @pl.when((zd > z) & (z > 0))
        def _():
            over_up(k, zd).wait_recv()
            grow(k, zd, from_low.at[k, zd])
            over_up(k, zd).start()

        @pl.when((zd < z) & (z < n - 1))
        def _():
            over_down(k, zd).wait_recv()
            grow(k, zd, from_high.at[k, zd])
            over_down(k, zd).start()

    def turn(i):
        below, above = z, n - 1 - z
        near = jnp.minimum(below, above)
        only = jnp.maximum(below, above) - near
        side = jnp.where(above >= below, 1, -1)
        distance = jnp.where(i < only, only + near - i, near - (i - only) // 2)
        sign = jnp.where(i < only, side, jnp.where(lax.rem(i - only, 2) == 0, side, -side))
        return jnp.where(i == n - 1, z, z + sign * distance)

    def item(j):
        return 1 - j // n, turn(lax.rem(j, n))

    def small_send(step):
        return copy(vec_sent.at[step], vec_got.at[step], vs.at[step], vr.at[step], partners[step])

    def input_tile(t):
        at = pl.ds(pl.multiple_of(t * ROWS, ROWS), ROWS)
        return (pltpu.make_async_copy(first_hbm.at[at, :], tile_in.at[lax.rem(t, 2)], tile_sem.at[0, lax.rem(t, 2)]),
                pltpu.make_async_copy(tile_out.at[lax.rem(t, 2)], input_hbm.at[at, :], tile_sem.at[1, lax.rem(t, 2)]), at)

    def input_grad(t):
        into, out, at = input_tile(t)
        into.start()
        total = nt(d_qkv[at, : 3 * third], w_all[:, : 3 * third])
        total += nt(d_qkv[at, 3 * third :], w_all[:, wide : wide + 3 * third])
        into.wait()
        tile_out[lax.rem(t, 2)] = tile_in[lax.rem(t, 2)] + total
        out.start()

    tiles = rows // ROWS
    last_item = 2 * n

    fetch_low.wait()
    turn_rows(0)
    fetch_unit.wait()

    @pl.loop(0, last_item + 4)
    def _(j):
        @pl.when(j < n)
        def _():
            k, zd = item(j)
            compute_inner(zd)
            to_sibling(1, zd).start()

        @pl.when(j == n - 1)
        def _():
            fetch_x.wait()
            fetch_proj.wait()
            fetch_attn.wait()
            turn_rows(1)
            turn_rows(2)
            for move in fetch_dq + fetch_kv:
                move.wait()
            swap.wait_recv()
            for h in range(2):
                at = slice((3 * h + 1) * third, (3 * h + 3) * third)
                d_qkv[:, at] = (d_qkv[:, at].astype(F32) + far[:, 2 * h * third : 2 * (h + 1) * third].astype(F32)).astype(BF)
            vec_sent[0] = jnp.zeros_like(vec_sent[0])
            vec_sent[0, 2:8, :] = sums_ref[2:8, :]
            for h in range(2):
                for row, i in ((0, 0), (1, 2)):
                    cols = d_qkv[:, (3 * h + i) * third : (3 * h + i + 1) * third].astype(F32)
                    vec_sent[0, row : row + 1, h * third : (h + 1) * third] = jnp.sum(cols, axis=0, keepdims=True)
            for u in range(unit_sums.shape[1] // width):
                vec_sent[0, 8 + u : 9 + u, :] = unit_sums[0:1, u * width : (u + 1) * width]
            small_send(0).start()
            fetch_w.wait()

        @pl.when((j >= n) & (j < last_item))
        def _():
            k, zd = item(j)
            compute_others(zd)
            to_sibling(0, zd).start()

        @pl.when((j >= 1) & (j < last_item + 1))
        def _():
            stage_b(*item(j - 1))

        @pl.when((j >= 2) & (j < last_item + 2))
        def _():
            stage_a(*item(j - 2))

        @pl.when((j >= 3) & (j < last_item + 3))
        def _():
            stage_line(*item(j - 3))

        @pl.when(j >= 4)
        def _():
            stage_hop(*item(j - 4))

        for step in range(len(partners)):
            @pl.when(j == n + step)
            def _(step=step):
                small_send(step).wait_recv()
                vec_sent[step + 1] = vec_sent[step] + vec_got[step]
                if step + 1 < len(partners):
                    small_send(step + 1).start()

        @pl.when((j >= last_item - tiles) & (j < last_item))
        def _():
            t = j - (last_item - tiles)

            @pl.when(t >= 2)
            def _():
                input_tile(t - 2)[1].wait()
            input_grad(t)

    vec_out[...] = vec_sent[len(partners)]
    own = pl.ds(pl.multiple_of(core * slab, slab), slab)
    theirs = pl.ds(pl.multiple_of((1 - core) * slab, slab), slab)
    for k in (1, 0):
        result[k, own, :] = grads[core, k, z, places_of[0]].astype(F32)

        @pl.when(z > 0)
        def _():
            over_up(k, z).wait_recv()
            result[k, own, :] += from_low[k, z].astype(F32)

        @pl.when(z < n - 1)
        def _():
            over_down(k, z).wait_recv()
            result[k, own, :] += from_high[k, z].astype(F32)

        copy(result.at[k, own, :], result.at[k, own, :], es.at[k], er.at[k], w["sibling"]).start()
    for t in range(max(tiles - 2, 0), tiles):
        input_tile(t)[1].wait()
    swap.wait_send()
    for step in range(len(partners)):
        small_send(step).wait_send()

    @pl.loop(0, n)
    def _(zd):
        for k in range(2):
            to_sibling(k, zd).wait_send()
            over_b(k, 0, zd).wait_send()
            over_b(k, 1, zd).wait_send()
            over_a(k, zd).wait_send()

            @pl.when(zd > z)
            def _():
                over_up(k, zd).wait_send()

            @pl.when(zd < z)
            def _():
                over_down(k, zd).wait_send()
    for k in (1, 0):
        copy(result.at[k, theirs, :], result.at[k, theirs, :], es.at[k], er.at[k], w["sibling"]).wait()

    def chosen(k, lane, w_own):
        both = result[k, :, lane : lane + 2 * w_own]
        return jnp.where(core == 0, both[:, :w_own], both[:, w_own:])

    for i, out in enumerate((q_out, k_out, v_out, o_out)):
        out[...] = chosen(0, i * third, third // 2)
    in_out[...] = chosen(1, 0, wide // 2)


def finish(layer_in, dq, dkv, weights, grad_first, norm_low, unit_grad, proj_grad, attn, sums, unit_sums):
    rows, width = layer_in.shape
    units = unit_grad.shape[1]
    dp, tp = lax.axis_size("dp"), lax.axis_size("tensor")
    n = dp // 2
    block = width // dp
    slab, wide, third = block // 2, units // 2, width // 2
    steps = 3 + (n - 1).bit_length()
    dma = pltpu.SemaphoreType.DMA
    slabs = lambda *lead: pltpu.VMEM(lead + (slab, wide), BF)
    anywhere, inside = pl.BlockSpec(memory_space=pl.ANY), pl.BlockSpec(memory_space=pltpu.VMEM)
    result = lambda *shape: jax.ShapeDtypeStruct(shape, F32)
    return pl.pallas_call(
        partial(finish_kernel, n),
        name="finish",
        in_specs=[anywhere] * 9 + [inside] * 2,
        out_specs=[anywhere] + [inside] * 6,
        out_shape=[result(rows, width)] + [result(block, third // 2)] * 4 + [result(block, wide // 2), result(16, width)],
        scratch_shapes=[
            pltpu.VMEM((3, rows, width), BF),
            pltpu.VMEM((3, width, rows), BF),
            pltpu.VMEM((rows, units), BF),
            pltpu.VMEM((rows, 3 * width), BF),
            pltpu.VMEM((rows, width), BF),
            pltpu.VMEM((rows, 2 * width), BF),
            pltpu.VMEM((width, units), BF),
            pltpu.VMEM((2, ROWS, width), F32),
            pltpu.VMEM((2, ROWS, width), F32),
            slabs(2, 2, n, 4),
            slabs(2, n, 4),
            slabs(2, 2, n),
            slabs(2, n),
            slabs(2, n),
            slabs(2, n),
            pltpu.VMEM((2, block, wide), F32),
            pltpu.VMEM((steps + 1, 16, width), F32),
            pltpu.VMEM((steps, 16, width), F32),
            dma((10,)), dma(()), dma(()),
            dma((2, n)), dma((2, n)), dma((2, 2, n)), dma((2, 2, n)), dma((2, n)), dma((2, n)),
            dma((2, n)), dma((2, 2, n)), dma((2,)), dma((2,)), dma((steps,)), dma((steps,)), dma((2, 2)),
        ],
        compiler_params=pltpu.CompilerParams(
            collective_id=4, has_side_effects=True, vmem_limit_bytes=60 * 2**20
        ),
    )(layer_in, dq, dkv.reshape(2, rows, 2 * width), weights, grad_first, norm_low, unit_grad, proj_grad, attn, sums, unit_sums)


def finish_plainly(layer_in, dq, dkv, weights, grad_first, norm_low, unit_grad, proj_grad, attn, sums, unit_sums):
    rows, width = layer_in.shape
    units = unit_grad.shape[1]
    dp, tp = lax.axis_size("dp"), lax.axis_size("tensor")
    third, block, pairs = width // 2, width // dp, tp // 2
    half = lax.rem(lax.axis_index("tensor"), 2)
    both = dkv.reshape(2, rows, 2 * width)
    far = swap_pair(both)
    near = lax.dynamic_index_in_dim(both, half, 0, False)
    own = (near.astype(F32) + far.astype(F32)).astype(BF)
    d_qkv = jnp.concatenate([dq[:, :third], own[:, :width], dq[:, third:], own[:, width:]], axis=1)
    wqkv = weights[0].reshape(width, 2, 4 * third)[:, :, : 3 * third].reshape(width, 3 * width)
    input_grad = grad_first + nt(d_qkv, wqkv)
    grads = [g.astype(BF) for g in (tn(layer_in, d_qkv), tn(proj_grad, attn), tn(norm_low, unit_grad))]
    joined = jnp.concatenate([g.reshape(width, pairs, -1) for g in grads[:2]], axis=2)
    every = jnp.stack([joined.reshape(width, units), grads[2]])
    every = every.reshape(2, dp, block, pairs, 1, units // pairs).transpose(1, 3, 4, 0, 2, 5)
    every = jnp.broadcast_to(every, (dp, pairs, 2, 2, block, units // pairs))
    total = lax.psum_scatter(
        every.reshape(dp * tp, 2, block, units // pairs), ("dp", "tensor"), scatter_dimension=0, tiled=False
    ).astype(F32)
    d_bias = jnp.sum(d_qkv.astype(F32), axis=0).reshape(2, 3, third)
    vec = jnp.concatenate(
        [d_bias[:, 0].reshape(1, width), d_bias[:, 2].reshape(1, width), sums[2:],
         unit_sums[0].reshape(-1, width), jnp.zeros((8 - units // width, width), F32)], axis=0,
    )
    vec = lax.psum(vec, ("dp", "tensor"))

    def chosen(k, lane, w_own):
        return lax.dynamic_slice_in_dim(total[k], lane + half * w_own, w_own, axis=1)

    return (input_grad,) + tuple(chosen(0, i * third, third // 2) for i in range(4)) + (
        chosen(1, 0, units // tp), vec)


def on_device(
    layer_in, query_weight, key_weight, value_weight, output_weight, inner_weight, outer_weight,
    query_bias, value_bias, output_bias, inner_bias, outer_bias, first_gain, first_shift,
    second_gain, second_shift, segment_ids, pad_mask, random_blocks, global_blocks, output_grad,
):
    rows, width = layer_in.shape
    dp, tp = lax.axis_size("dp"), lax.axis_size("tensor")
    own_rows, own_cols = query_weight.shape
    own_units = inner_weight.shape[1]
    third = width // 2
    half = lax.rem(lax.axis_index("tensor"), 2)

    units_own = jnp.concatenate([inner_weight, outer_weight.T], axis=1)
    blocks = lax.all_gather(units_own, ("dp", "tensor"), axis=0, tiled=False)
    blocks = blocks.reshape(dp, tp, own_rows, 2 * own_units)
    mine = (query_weight, key_weight, value_weight, output_weight.T)
    place = lax.axis_index("dp") * tp + lax.axis_index("tensor")
    one, own_bias = query_bias.shape[0], inner_bias.shape[0]
    small = jnp.stack([query_bias, value_bias, output_bias, outer_bias, first_gain, first_shift,
                       second_gain, second_shift])
    eight = lax.dynamic_update_slice(jnp.zeros((8, width), F32), small, (0, place * one))
    unit = lax.dynamic_update_slice(jnp.zeros((8 * width,), F32), inner_bias, (place * own_bias,))
    vec = jnp.concatenate([eight, unit.reshape(8, width)], axis=0)
    begin = start if in_tiles(own_rows) else start_plainly
    weights, qkv, other, vectors = begin(mine, vec, layer_in)

    bounds, row_info, key_info = attention_plan(
        segment_ids, pad_mask, random_blocks, global_blocks, rows
    )
    attn, logs = attend_forward(bounds, qkv, other, row_info, key_info)
    (layer_out, grad_first, grad_attn, norm_low, unit_grad, proj_grad, out_grad, sums, unit_sums) = middle(
        layer_in, attn, output_grad, weights, blocks, vectors
    )
    d_outer = lax.psum_scatter(
        out_grad.reshape((dp * tp,) + out_grad.shape[2:]), ("dp", "tensor"), scatter_dimension=0, tiled=False
    )
    dq, dkv = attend_backward(bounds, qkv, other, row_info, key_info, attn, logs, grad_attn)
    end = finish if in_tiles(own_rows) else finish_plainly
    input_grad, d_q, d_k, d_v, d_o, d_inner, vec = end(
        layer_in, dq, dkv, weights, grad_first, norm_low, unit_grad, proj_grad, attn, sums, unit_sums
    )
    pieces = lax.dynamic_slice_in_dim(vec[:8], place * one, one, axis=1)
    (r_bq, r_bv, r_bo, r_bout, r_g1, r_s1, r_g2, r_s2) = (pieces[i] for i in range(8))
    d_bin = lax.dynamic_slice_in_dim(vec[8:].reshape(-1), place * own_bias, own_bias)
    return (
        layer_out, input_grad, d_q, d_k, d_v, d_o.T, d_inner, d_outer.astype(F32).T,
        r_bq, r_bv, r_bo, d_bin, r_bout, r_g1, r_s1, r_g2, r_s2,
    )


def solution(mesh):
    tokens = P(("dp", "tensor"), None)
    vector = P(("dp", "tensor"))
    cols, turned = P("dp", "tensor"), P("tensor", "dp")
    return jax.shard_map(
        on_device,
        mesh=mesh,
        in_specs=(tokens, cols, cols, cols, turned, cols, turned)
        + (vector,) * 9
        + (P("dp"), P("dp"), P("dp", None, None), P("dp", None, None), tokens),
        out_specs=(tokens, tokens, cols, cols, cols, turned, cols, turned) + (vector,) * 9,
        check_vma=False,
    )
```

```python
from functools import partial

import jax
import jax.numpy as jnp
from jax import lax
from jax.experimental import pallas as pl
from jax.experimental.pallas import tpu as pltpu
from jax.sharding import PartitionSpec as P

HD = 64
PAIR = 2 * HD
QT = 256
KT = 128
ROWS = 256
BACK_ROWS = 256
EPSILON = 1e-06
NEGATIVE = -1e30
MESH = pl.DeviceIdType.MESH
VMEM_LIMIT = 56 * 2**20
BF = jnp.bfloat16
F32 = jnp.float32


def params_of(collective_id=None):
    if collective_id is None:
        return pltpu.CompilerParams(vmem_limit_bytes=VMEM_LIMIT)
    return pltpu.CompilerParams(
        vmem_limit_bytes=VMEM_LIMIT, collective_id=collective_id, has_side_effects=True
    )


def nt(left, right, **more):
    return lax.dot_general(
        left, right, (((1,), (1,)), ((), ())), preferred_element_type=F32, **more
    )


def nn(left, right):
    return lax.dot_general(left, right, (((1,), (0,)), ((), ())), preferred_element_type=F32)


def tn(left, right):
    return lax.dot_general(left, right, (((0,), (0,)), ((), ())), preferred_element_type=F32)


def sibling_of():
    rank = lax.axis_index("tensor")
    half = lax.rem(rank, 2)
    return half, {"tensor": rank + 1 - 2 * half}


def meet(others):
    barrier = pltpu.get_barrier_semaphore()
    for other in others:
        pl.semaphore_signal(barrier, inc=1, device_id=other, device_id_type=MESH)
    pl.semaphore_wait(barrier, len(others))


def swap_keys_kernel(qkv_ref, other_ref, send_sem, recv_sem):
    half, sibling = sibling_of()
    meet([sibling])
    third = qkv_ref.shape[1] // 6
    moves = [
        pltpu.make_async_remote_copy(
            qkv_ref.at[:, (3 * y + 1) * third : (3 * y + 3) * third],
            other_ref.at[:, 2 * y * third : 2 * (y + 1) * third],
            send_sem.at[y], recv_sem.at[y], device_id=sibling, device_id_type=MESH,
        )
        for y in range(2)
    ]
    for move in moves:
        move.start()
    for move in moves:
        move.wait()


def swap_keys(qkv):
    rows, width = qkv.shape
    return pl.pallas_call(
        swap_keys_kernel,
        name="swap_keys",
        out_shape=jax.ShapeDtypeStruct((rows, width * 2 // 3), qkv.dtype),
        in_specs=[pl.BlockSpec(memory_space=pl.ANY)],
        out_specs=pl.BlockSpec(memory_space=pl.ANY),
        scratch_shapes=[pltpu.SemaphoreType.DMA((2,))] * 2,
        compiler_params=params_of(1),
    )(qkv)


def swap_pair_kernel(both_ref, other_ref, send_sem, recv_sem):
    half, sibling = sibling_of()
    meet([sibling])
    away = pltpu.make_async_remote_copy(
        both_ref.at[1 - half], other_ref, send_sem, recv_sem,
        device_id=sibling, device_id_type=MESH,
    )
    away.start()
    away.wait()


def swap_pair(both):
    return pl.pallas_call(
        swap_pair_kernel,
        name="swap_pair",
        out_shape=jax.ShapeDtypeStruct(both.shape[1:], both.dtype),
        in_specs=[pl.BlockSpec(memory_space=pl.ANY)],
        out_specs=pl.BlockSpec(memory_space=pl.ANY),
        scratch_shapes=[pltpu.SemaphoreType.DMA(())] * 2,
        compiler_params=params_of(2),
    )(both)


def places():
    dp, rank = lax.axis_index("dp"), lax.axis_index("tensor")
    core, y = lax.rem(rank, 2), rank // 2
    z, x = dp // 2, lax.rem(dp, 2)
    sibling = {"dp": dp, "tensor": rank + 1 - 2 * core}
    near_x = {"dp": dp + 1 - 2 * x, "tensor": rank}
    near_y = {"dp": dp, "tensor": rank + 2 - 4 * y}
    first = {"dp": dp + (1 - core) * (1 - 2 * x), "tensor": rank + core * (2 - 4 * y)}
    second = {"dp": dp + core * (1 - 2 * x), "tensor": rank + (1 - core) * (2 - 4 * y)}
    xa, ya = x + (1 - core) * (1 - 2 * x), y + core * (1 - 2 * y)
    xb, yb = x + core * (1 - 2 * x), y + (1 - core) * (1 - 2 * y)
    return dict(dp=dp, rank=rank, core=core, y=y, z=z, x=x, sibling=sibling, first=first, second=second,
                xa=xa, ya=ya, xb=xb, yb=yb)


def line_jumps(dp, rank, z, n):
    jumps, hop = [], 1
    while hop < n:
        bit = lax.rem(z // hop, 2)
        jumps.append({"dp": dp + 2 * hop * (1 - 2 * bit), "tensor": rank})
        hop *= 2
    return jumps


def start_kernel(
    n, query_ref, key_ref, value_ref, proj_ref, vec_ref, x_ref, w_hbm, qkv_hbm, other_hbm, vec_out,
    out_ref, chip, sib, mine_ref, qkv, vec_sent, vec_got,
    local_sem, pair_sem, zs, zr, as_, ar, bs, br, ss, sr, ks, kr, vs, vr,
):
    w = places()
    dp, rank, core, y, z, x = (w[k] for k in ("dp", "rank", "core", "y", "z", "x"))
    block, wide = mine_ref.shape[1], mine_ref.shape[2]
    slab = block // 2
    up, down = {"dp": lax.rem(dp + 2, 2 * n), "tensor": rank}, {"dp": lax.rem(dp + 2 * n - 2, 2 * n), "tensor": rank}
    partners = [w["sibling"], w["second"], w["first"]] + line_jumps(dp, rank, z, n)
    own_cols = query_ref.shape[1]
    for i, ref in enumerate((query_ref, key_ref, value_ref, proj_ref)):
        own_w = ref[...]
        zero = jnp.zeros_like(own_w)
        mine_ref[0, :, 2 * i * own_cols : 2 * (i + 1) * own_cols] = jnp.where(
            core == 0, jnp.concatenate([own_w, zero], axis=1), jnp.concatenate([zero, own_w], axis=1)
        )
    meet([up, down] + partners)

    pair = pltpu.make_async_remote_copy(mine_ref, sib, pair_sem.at[0], pair_sem.at[1], device_id=w["sibling"], device_id_type=MESH)
    pair.start()

    def small_send(step):
        return pltpu.make_async_remote_copy(vec_sent.at[step], vec_got.at[step], vs.at[step], vr.at[step], device_id=partners[step], device_id_type=MESH)

    def small_step(step):
        small_send(step).wait_recv()
        vec_sent[step + 1] = vec_sent[step] + vec_got[step]
        if step + 1 < len(partners):
            small_send(step + 1).start()

    vec_sent[0] = vec_ref[...]
    small_send(0).start()
    pair.wait()
    chip[...] = mine_ref[...] + sib[...]
    rows_own = pl.ds(pl.multiple_of(core * slab, slab), slab)
    own_at = pl.ds(pl.multiple_of(dp * block, block), block)
    cols_own = pl.ds(pl.multiple_of(y * wide, wide), wide)
    keep = pltpu.make_async_copy(chip, out_ref.at[:, own_at, cols_own], local_sem.at[0])
    keep.start()

    def spot(g, zi, xi, yi):
        d = zi * 2 + xi
        rows = pl.ds(pl.multiple_of(d * block + core * slab, slab), slab)
        cols = pl.ds(pl.multiple_of(yi * wide, wide), wide)
        return out_ref.at[:, rows, cols]

    def own(g):
        return chip.at[:, rows_own, :]

    def move(g, zi, xi, yi, dev, ssem, rsem, source=None):
        at = spot(g, zi, xi, yi)
        return pltpu.make_async_remote_copy(at if source is None else source, at, ssem, rsem, device_id=dev, device_id_type=MESH)

    def line_up(g, s):
        return move(g, z - s, x, y, up, zs.at[g, 0, s], zr.at[g, 0, s], own(g) if s == 0 else None)

    def line_down(g, s):
        return move(g, z + s, x, y, down, zs.at[g, 1, s], zr.at[g, 1, s], own(g) if s == 0 else None)

    def to_first(g, zi, source=None):
        return move(g, zi, x, y, w["first"], as_.at[g, zi], ar.at[g, zi], source)

    def to_second(g, zi, far, source=None):
        xi, yi = (w["xa"], w["ya"]) if far else (x, y)
        return move(g, zi, xi, yi, w["second"], bs.at[g, far, zi], br.at[g, far, zi], source)

    def to_sibling(g, zi, quarter, source=None):
        xi = (x, w["xa"], w["xb"], w["xa"] + w["xb"] - x)[quarter]
        yi = (y, w["ya"], w["yb"], w["ya"] + w["yb"] - y)[quarter]
        return move(g, zi, xi, yi, w["sibling"], ss.at[g, quarter, zi], sr.at[g, quarter, zi], source)

    def begin(g):
        @pl.when(z < n - 1)
        def _():
            line_up(g, 0).start()

        @pl.when(z > 0)
        def _():
            line_down(g, 0).start()

        to_first(g, z, own(g)).start()
        to_second(g, z, 0, own(g)).start()

    def first_in(g, zi):
        got = move(g, zi, w["xa"], w["ya"], w["first"], as_.at[g, zi], ar.at[g, zi])
        got.wait_recv()
        to_second(g, zi, 1).start()
        to_sibling(g, zi, 1).start()

    def second_in(g, zi, far):
        q = 2 + far
        xi = (w["xb"], w["xa"] + w["xb"] - x)[far]
        yi = (w["yb"], w["ya"] + w["yb"] - y)[far]
        move(g, zi, xi, yi, w["second"], bs.at[g, far, zi], br.at[g, far, zi]).wait_recv()
        to_sibling(g, zi, q).start()

    def below_in(g, s):
        zi = z - 1 - s
        move(g, zi, x, y, up, zs.at[g, 0, s], zr.at[g, 0, s]).wait_recv()
        if s + 1 < n - 1:
            @pl.when(z < n - 1)
            def _():
                line_up(g, s + 1).start()
        to_first(g, zi).start()
        to_second(g, zi, 0).start()
        to_sibling(g, zi, 0).start()

    def above_in(g, s):
        zi = z + 1 + s
        move(g, zi, x, y, down, zs.at[g, 1, s], zr.at[g, 1, s]).wait_recv()
        if s + 1 < n - 1:
            @pl.when(z > 0)
            def _():
                line_down(g, s + 1).start()
        to_first(g, zi).start()
        to_second(g, zi, 0).start()
        to_sibling(g, zi, 0).start()

    def steps(gs):
        for g in gs:
            first_in(g, z)
        for s in range(n - 1):
            @pl.when(z - 1 - s >= 0)
            def _(s=s):
                for g in gs:
                    below_in(g, s)

            @pl.when(z + 1 + s < n)
            def _(s=s):
                for g in gs:
                    above_in(g, s)
            if s > 0:
                both(s, lambda g, zi: first_in(g, zi), gs)
        both(n - 1, lambda g, zi: first_in(g, zi), gs)
        for g in gs:
            second_in(g, z, 0)
        for g in gs:
            second_in(g, z, 1)
        for s in range(1, n):
            both(s, lambda g, zi: second_in(g, zi, 0), gs)
            both(s, lambda g, zi: second_in(g, zi, 1), gs)

    def both(s, what, gs):
        @pl.when(z - s >= 0)
        def _():
            for g in gs:
                what(g, z - s)

        @pl.when(z + s < n)
        def _():
            for g in gs:
                what(g, z + s)

    begin(0)
    small_step(0)
    steps((0,))
    for step in range(1, len(partners)):
        small_step(step)

    keep.wait()
    for zi in range(n):
        for q in range(1, 4):
            to_sibling(0, zi, q).wait_recv()

        @pl.when(zi != z)
        def _(zi=zi):
            to_sibling(0, zi, 0).wait_recv()
    save_w = pltpu.make_async_copy(out_ref, w_hbm, local_sem.at[1])
    save_w.start()

    width = x_ref.shape[1]
    third = width // 2
    vec_out[...] = vec_sent[len(partners)]

    def keys_of(yi):
        return pltpu.make_async_remote_copy(
            qkv.at[:, (3 * yi + 1) * third : (3 * yi + 3) * third],
            other_hbm.at[:, 2 * yi * third : 2 * (yi + 1) * third],
            ks.at[yi], kr.at[yi], device_id=w["sibling"], device_id_type=MESH,
        )

    for yi in range(2):
        first = (3 * yi + 1) * third
        both = nn(x_ref[...], out_ref[0, :, yi * wide + third : yi * wide + 3 * third])
        qkv[:, first : first + third] = both[:, :third].astype(BF)
        bias = vec_out[1:2, yi * third : (yi + 1) * third]
        qkv[:, first + third : first + 2 * third] = (both[:, third:] + bias).astype(BF)
        keys_of(yi).start()
    for yi in range(2):
        first = 3 * yi * third
        bias = vec_out[0:1, yi * third : (yi + 1) * third]
        qkv[:, first : first + third] = (nn(x_ref[...], out_ref[0, :, yi * wide : yi * wide + third]) + bias).astype(BF)

    save_qkv = pltpu.make_async_copy(qkv, qkv_hbm, local_sem.at[2])
    save_qkv.start()
    for g in (0,):
        @pl.when(z < n - 1)
        def _(g=g):
            line_up(g, 0).wait_send()

        @pl.when(z > 0)
        def _(g=g):
            line_down(g, 0).wait_send()
        for s in range(1, n - 1):
            @pl.when((z < n - 1) & (z - s >= 0))
            def _(g=g, s=s):
                line_up(g, s).wait_send()

            @pl.when((z > 0) & (z + s < n))
            def _(g=g, s=s):
                line_down(g, s).wait_send()
        for zi in range(n):
            to_first(g, zi).wait_send()
            for far in range(2):
                to_second(g, zi, far).wait_send()
            for q in range(1, 4):
                to_sibling(g, zi, q).wait_send()
        for zi in range(n):
            @pl.when(zi != z)
            def _(g=g, zi=zi):
                to_sibling(g, zi, 0).wait_send()


    for step in range(len(partners)):
        small_send(step).wait_send()

    for yi in range(2):
        keys_of(yi).wait()
    save_w.wait()
    save_qkv.wait()


def start(own, vec, layer_in):
    dp, tp = lax.axis_size("dp"), lax.axis_size("tensor")
    n = dp // 2
    block, own_cols = own[0].shape
    parts, wide = 1, 2 * len(own) * own_cols
    piece = pltpu.VMEM((parts, block, wide), BF)
    rows, width = layer_in.shape
    steps = 3 + (n - 1).bit_length()
    dma = pltpu.SemaphoreType.DMA
    anywhere, inside = pl.BlockSpec(memory_space=pl.ANY), pl.BlockSpec(memory_space=pltpu.VMEM)
    whole = (parts, dp * block, wide * tp // 2)
    return pl.pallas_call(
        partial(start_kernel, n),
        name="start",
        in_specs=[inside] * 6,
        out_specs=[anywhere] * 3 + [inside],
        out_shape=[
            jax.ShapeDtypeStruct(whole, BF),
            jax.ShapeDtypeStruct((rows, 3 * width), BF),
            jax.ShapeDtypeStruct((rows, 2 * width), BF),
            jax.ShapeDtypeStruct(vec.shape, F32),
        ],
        scratch_shapes=[
            pltpu.VMEM(whole, BF), piece, piece, piece,
            pltpu.VMEM((rows, 3 * width), BF),
            pltpu.VMEM((steps + 1,) + vec.shape, F32), pltpu.VMEM((steps,) + vec.shape, F32),
            dma((3,)), dma((2,)), dma((1, 2, n)), dma((1, 2, n)), dma((1, n)), dma((1, n)),
            dma((1, 2, n)), dma((1, 2, n)), dma((1, 4, n)), dma((1, 4, n)), dma((2,)), dma((2,)),
            dma((steps,)), dma((steps,)),
        ],
        compiler_params=params_of(3),
    )(*own, vec, layer_in)


def in_tiles(block):
    return block % 32 == 0


def start_plainly(own, vec, layer_in):
    dp, tp = lax.axis_size("dp"), lax.axis_size("tensor")
    half = lax.rem(lax.axis_index("tensor"), 2)

    def beside(one):
        zero = jnp.zeros_like(one)
        return jnp.concatenate(
            [jnp.where(half == 0, one, zero), jnp.where(half == 0, zero, one)], axis=1
        )

    mine = jnp.concatenate([beside(one) for one in own], axis=1)[None]
    parts, block, wide = mine.shape
    width = layer_in.shape[1]
    third = width // 2
    every = lax.all_gather(mine, ("dp", "tensor"), axis=0, tiled=False)
    every = every.reshape(dp, tp // 2, 2, parts, block, wide).sum(axis=2)
    weights = every.transpose(2, 0, 3, 1, 4).reshape(parts, dp * block, tp // 2 * wide)
    vec = lax.psum(vec, ("dp", "tensor"))
    zero = jnp.zeros((1, third), F32)
    bias = jnp.concatenate(
        [v for y in range(2) for v in (vec[:1, y * third : (y + 1) * third], zero,
                                       vec[1:2, y * third : (y + 1) * third])], axis=1,
    )
    wqkv = weights[0].reshape(width, 2, 4 * third)[:, :, : 3 * third].reshape(width, 3 * width)
    qkv = (nn(layer_in, wqkv) + bias).astype(BF)
    return weights, qkv, swap_keys(qkv), vec


def q_lanes(p, pairs):
    third = pairs // 2 * PAIR
    first = p // (pairs // 2) * 3 * third + p % (pairs // 2) * PAIR
    return slice(first, first + PAIR)


def k_lanes(p, pairs):
    third = pairs // 2 * PAIR
    first = p // (pairs // 2) * 2 * third + p % (pairs // 2) * PAIR
    return slice(first, first + PAIR)


def v_lanes(p, pairs):
    third = pairs // 2 * PAIR
    lanes = k_lanes(p, pairs)
    return slice(lanes.start + third, lanes.stop + third)


def key_tile(j, qkv_ref, other_ref, kv, sems):
    rows, third = other_ref.shape[0], other_ref.shape[1] // 4
    here = pl.ds(pl.multiple_of(j * KT, KT), KT)
    from_row = pl.ds(pl.multiple_of(lax.rem(j * KT, rows), KT), KT)
    own = [
        pltpu.make_async_copy(
            qkv_ref.at[from_row, (3 * y + 1) * third : (3 * y + 3) * third],
            kv.at[here, 2 * y * third : 2 * (y + 1) * third],
            sems.at[y, j],
        )
        for y in range(2)
    ]
    far = pltpu.make_async_copy(other_ref.at[from_row, :], kv.at[here, :], sems.at[0, j])
    is_own = (j * KT) // rows == lax.rem(lax.axis_index("tensor"), 2)
    return is_own, own, far


def fetch_keys(low, high, qkv_ref, other_ref, kv, sems, use):
    @pl.loop(low, high)
    def _(j):
        is_own, own, far = key_tile(j, qkv_ref, other_ref, kv, sems)

        @pl.when(is_own)
        def _():
            for move in own:
                move.start()

        @pl.when(jnp.logical_not(is_own))
        def _():
            far.start()

    @pl.loop(low, high)
    def _(j):
        is_own, own, far = key_tile(j, qkv_ref, other_ref, kv, sems)

        @pl.when(is_own)
        def _():
            for move in own:
                move.wait()

        @pl.when(jnp.logical_not(is_own))
        def _():
            far.wait()
        use(j)


def masked_pairs(source, target, lanes_of, pairs, scale):
    rows = source.shape[0]
    low_lanes = lax.broadcasted_iota(jnp.int32, (rows, PAIR), 1) < HD
    for p in range(pairs):
        both = source[:, lanes_of(p)]
        if scale is not None:
            both = both * jnp.asarray(scale, both.dtype)
        zero = jnp.zeros_like(both)
        target[p, :rows, :] = jnp.where(low_lanes, both, zero)
        target[p, rows:, :] = jnp.where(low_lanes, zero, both)


def tile_bias(j, q_first, row_info, key_info, bias):
    seg_q, bits_q = row_info[0:1, :], row_info[1:2, :]
    queries = bias.shape[1]
    for part in range(KT // HD):
        block = j * (KT // HD) + part
        bit = jnp.bitwise_and(
            lax.shift_right_logical(bits_q, jnp.full_like(bits_q, block)), 1
        )
        wanted = jnp.where(bit == 1, seg_q, -1)
        base = pl.multiple_of(j * KT + part * HD, HD)
        seg_k = key_info[pl.ds(base, HD), :]
        key_at = base + lax.broadcasted_iota(jnp.int32, (HD, queries), 0)
        query_at = q_first + lax.broadcasted_iota(jnp.int32, (HD, queries), 1)
        allowed = (seg_k == wanted) | (key_at == query_at)
        bias[part * HD : (part + 1) * HD, :] = jnp.where(allowed, 0.0, NEGATIVE)


def attend_forward_kernel(
    bounds, q_ref, qkv_ref, other_ref, row_info, key_info, out_ref, log_ref,
    q_pairs, kv_ref, v_turned, bias, top, total, acc, scores, fades, lows, sems,
):
    step = pl.program_id(0)
    rows, width = out_ref.shape
    pairs = width // PAIR
    tiles = kv_ref.shape[0] // KT

    @pl.when(step == 0)
    def _():
        def turn(j):
            for p in range(pairs):
                span = slice(p * PAIR, (p + 1) * PAIR)
                v_turned[j, span, :] = kv_ref[pl.ds(pl.multiple_of(j * KT, KT), KT), v_lanes(p, pairs)].T

        fetch_keys(bounds[0, 0], bounds[pl.num_programs(0) - 1, 1], qkv_ref, other_ref, kv_ref, sems, turn)

    masked_pairs(q_ref, q_pairs, partial(q_lanes, pairs=pairs), pairs, HD**-0.5)
    top[...] = jnp.full_like(top, NEGATIVE)
    total[...] = jnp.zeros_like(total)
    acc[...] = jnp.zeros_like(acc)
    q_first = bounds[step, 2]

    @pl.loop(bounds[step, 0], bounds[step, 1])
    def _(j):
        tile_bias(j, q_first, row_info, key_info, bias)
        keys_at = pl.multiple_of(j * KT, KT)
        for p in range(pairs):
            keys = kv_ref[pl.ds(keys_at, KT), k_lanes(p, pairs)]
            scores[p] = nt(keys, q_pairs[p])
        for h in range(2 * pairs):
            p, e = divmod(h, 2)
            mine = scores[p, :, e * rows : (e + 1) * rows] + bias[...]
            before = top[h : h + 1, :]
            now = jnp.maximum(before, jnp.max(mine, axis=0, keepdims=True))
            fade = jnp.exp(before - now)
            expos = jnp.exp(mine - now)
            top[h : h + 1, :] = now
            fades[h : h + 1, :] = fade
            total[h : h + 1, :] = fade * total[h : h + 1, :] + jnp.sum(
                expos, axis=0, keepdims=True
            )
            lows[h] = expos.astype(BF)
        for h in range(2 * pairs):
            span = slice(h * HD, (h + 1) * HD)
            acc[span, :] = acc[span, :] * fades[h : h + 1, :] + nn(v_turned[j, span, :], lows[h])

    heads = width // HD
    for h in range(heads):
        span = slice(h * HD, (h + 1) * HD)
        acc[span, :] = acc[span, :] / total[h : h + 1, :]
    out_ref[...] = acc[...].T.astype(BF)
    log_ref[...] = top[...] + jnp.log(jnp.maximum(total[...], 1e-37))


def attend_forward(bounds, qkv, other, row_info, key_info):
    rows, width = qkv.shape[0], qkv.shape[1] // 3
    keys = 2 * rows
    stat_rows = 16
    return pl.pallas_call(
        attend_forward_kernel,
        name="attend_forward",
        grid_spec=pltpu.PrefetchScalarGridSpec(
            num_scalar_prefetch=1,
            grid=(rows // QT,),
            in_specs=[
                pl.BlockSpec((QT, 3 * width), lambda i, b: (i, 0)),
                pl.BlockSpec(memory_space=pl.ANY),
                pl.BlockSpec(memory_space=pl.ANY),
                pl.BlockSpec((8, QT), lambda i, b: (0, i)),
                pl.BlockSpec((keys, 1), lambda i, b: (0, 0), pipeline_mode=pl.Buffered(1)),
            ],
            out_specs=[
                pl.BlockSpec((QT, width), lambda i, b: (i, 0)),
                pl.BlockSpec((stat_rows, QT), lambda i, b: (0, i)),
            ],
            scratch_shapes=[
                pltpu.VMEM((width // PAIR, 2 * QT, PAIR), BF),
                pltpu.VMEM((keys, 2 * width), BF),
                pltpu.VMEM((keys // KT, width, KT), BF),
                pltpu.VMEM((KT, QT), F32),
                pltpu.VMEM((stat_rows, QT), F32),
                pltpu.VMEM((stat_rows, QT), F32),
                pltpu.VMEM((width, QT), F32),
                pltpu.VMEM((width // PAIR, KT, 2 * QT), F32),
                pltpu.VMEM((stat_rows, QT), F32),
                pltpu.VMEM((width // HD, KT, QT), BF),
                pltpu.SemaphoreType.DMA((2, keys // KT)),
            ],
        ),
        out_shape=[
            jax.ShapeDtypeStruct((rows, width), BF),
            jax.ShapeDtypeStruct((stat_rows, rows), F32),
        ],
        compiler_params=params_of(),
    )(bounds, qkv, qkv, other, row_info, key_info)


def attend_backward_kernel(
    bounds, q_ref, qkv_ref, other_ref, row_info, key_info, out_ref, log_ref, grad_ref,
    dq_ref, dkv_ref, q_pairs, g_pairs, kv_ref, k_turned, bias, inner, dq_acc, dkv_acc,
    scores, changes, probs, grads, sems,
):
    step = pl.program_id(0)
    rows, width = out_ref.shape
    pairs = width // PAIR
    tiles = kv_ref.shape[0] // KT

    @pl.when(step == 0)
    def _():
        def turn(j):
            for p in range(pairs):
                span = slice(p * PAIR, (p + 1) * PAIR)
                k_turned[j, span, :] = kv_ref[pl.ds(pl.multiple_of(j * KT, KT), KT), k_lanes(p, pairs)].T

        fetch_keys(bounds[0, 0], bounds[pl.num_programs(0) - 1, 1], qkv_ref, other_ref, kv_ref, sems, turn)
        dkv_acc[...] = jnp.zeros_like(dkv_acc)

    masked_pairs(q_ref, q_pairs, partial(q_lanes, pairs=pairs), pairs, HD**-0.5)
    masked_pairs(grad_ref, g_pairs, lambda p: slice(p * PAIR, (p + 1) * PAIR), pairs, None)
    dq_acc[...] = (out_ref[...].astype(F32) * grad_ref[...].astype(F32)).T
    for h in range(2 * pairs):
        inner[h : h + 1, :] = jnp.sum(dq_acc[h * HD : (h + 1) * HD, :], axis=0, keepdims=True)
    dq_acc[...] = jnp.zeros_like(dq_acc)
    q_first = bounds[step, 2]

    @pl.loop(bounds[step, 0], bounds[step, 1])
    def _(j):
        tile_bias(j, q_first, row_info, key_info, bias)
        here = pl.ds(pl.multiple_of(j * KT, KT), KT)
        for p in range(pairs):
            scores[p] = nt(kv_ref[here, k_lanes(p, pairs)], q_pairs[p])
            changes[p] = nt(kv_ref[here, v_lanes(p, pairs)], g_pairs[p])
        for h in range(2 * pairs):
            p, e = divmod(h, 2)
            cols = slice(e * rows, (e + 1) * rows)
            prob = jnp.exp(scores[p, :, cols] + bias[...] - log_ref[h : h + 1, :])
            probs[p, :, cols] = prob.astype(BF)
            grads[p, :, cols] = (prob * (changes[p, :, cols] - inner[h : h + 1, :])).astype(BF)
        for p in range(pairs):
            dkv_acc[here, k_lanes(p, pairs)] += nn(grads[p], q_pairs[p])
            dkv_acc[here, v_lanes(p, pairs)] += nn(probs[p], g_pairs[p])
        for h in range(2 * pairs):
            p, e = divmod(h, 2)
            span = slice(h * HD, (h + 1) * HD)
            dq_acc[span, :] += nn(k_turned[j, span, :], grads[p, :, e * rows : (e + 1) * rows])

    dq_ref[...] = (dq_acc[...] * HD**-0.5).T.astype(BF)

    @pl.when(step == pl.num_programs(0) - 1)
    def _():
        dkv_ref[...] = dkv_acc[...].astype(BF)


def attend_backward(bounds, qkv, other, row_info, key_info, attn, logs, grad_attn):
    rows, width = attn.shape
    keys = 2 * rows
    stat_rows = logs.shape[0]
    whole = dict(pipeline_mode=pl.Buffered(1))
    return pl.pallas_call(
        attend_backward_kernel,
        name="attend_backward",
        grid_spec=pltpu.PrefetchScalarGridSpec(
            num_scalar_prefetch=1,
            grid=(rows // QT,),
            in_specs=[
                pl.BlockSpec((QT, 3 * width), lambda i, b: (i, 0)),
                pl.BlockSpec(memory_space=pl.ANY),
                pl.BlockSpec(memory_space=pl.ANY),
                pl.BlockSpec((8, QT), lambda i, b: (0, i)),
                pl.BlockSpec((keys, 1), lambda i, b: (0, 0), **whole),
                pl.BlockSpec((QT, width), lambda i, b: (i, 0)),
                pl.BlockSpec((stat_rows, QT), lambda i, b: (0, i)),
                pl.BlockSpec((QT, width), lambda i, b: (i, 0)),
            ],
            out_specs=[
                pl.BlockSpec((QT, width), lambda i, b: (i, 0)),
                pl.BlockSpec((keys, 2 * width), lambda i, b: (0, 0), **whole),
            ],
            scratch_shapes=[
                pltpu.VMEM((width // PAIR, 2 * QT, PAIR), BF),
                pltpu.VMEM((width // PAIR, 2 * QT, PAIR), BF),
                pltpu.VMEM((keys, 2 * width), BF),
                pltpu.VMEM((keys // KT, width, KT), BF),
                pltpu.VMEM((KT, QT), F32),
                pltpu.VMEM((stat_rows, QT), F32),
                pltpu.VMEM((width, QT), F32),
                pltpu.VMEM((keys, 2 * width), F32),
                pltpu.VMEM((width // PAIR, KT, 2 * QT), F32),
                pltpu.VMEM((width // PAIR, KT, 2 * QT), F32),
                pltpu.VMEM((width // PAIR, KT, 2 * QT), BF),
                pltpu.VMEM((width // PAIR, KT, 2 * QT), BF),
                pltpu.SemaphoreType.DMA((2, keys // KT)),
            ],
        ),
        out_shape=[
            jax.ShapeDtypeStruct((rows, width), BF),
            jax.ShapeDtypeStruct((keys, 2 * width), BF),
        ],
        compiler_params=params_of(),
    )(bounds, qkv, qkv, other, row_info, key_info, attn, logs, grad_attn)


def attention_plan(segment_ids, pad_mask, random_blocks, global_blocks, rows):
    seq_count, nblocks = random_blocks.shape[0], random_blocks.shape[1]
    seq_len = segment_ids.shape[0] // seq_count
    rank = lax.axis_index("tensor")
    seq, half = rank // 2, lax.rem(rank, 2)
    segs = lax.dynamic_index_in_dim(segment_ids.reshape(seq_count, seq_len), seq, 0, False)
    pads = lax.dynamic_index_in_dim(pad_mask.reshape(seq_count, seq_len), seq, 0, False)
    randoms = lax.dynamic_index_in_dim(random_blocks, seq, 0, False)
    globs = lax.dynamic_index_in_dim(global_blocks, seq, 0, False)
    block_size = seq_len // nblocks
    one = jnp.int32(1)
    block = jnp.arange(nblocks, dtype=jnp.int32)

    def either(a, b):
        return jnp.bitwise_or(a, b)

    block_bits = lax.shift_left(one, block)
    window = either(
        block_bits,
        either(
            jnp.where(block > 0, lax.shift_left(one, jnp.maximum(block - 1, 0)), 0),
            jnp.where(
                block < nblocks - 1, lax.shift_left(one, jnp.minimum(block + 1, nblocks - 1)), 0
            ),
        ),
    )
    for r in range(randoms.shape[1]):
        window = either(window, lax.shift_left(one, randoms[:, r]))
    glob_bits = either(lax.shift_left(one, globs[:, 0]), lax.shift_left(one, globs[:, 1]))
    first = half * rows
    seg_q = lax.dynamic_slice_in_dim(segs, first, rows)
    own_bits = lax.dynamic_slice_in_dim(window, half * (rows // block_size), rows // block_size)
    bits = jnp.broadcast_to(own_bits[:, None], (rows // block_size, block_size)).reshape(rows)
    numbers = jnp.arange(globs.shape[0], dtype=jnp.int32)
    is_doc = seg_q[None, :] == numbers[:, None]
    bits = either(bits, jnp.sum(jnp.where(is_doc, glob_bits[:, None], 0), axis=0))
    row_info = jnp.concatenate(
        [seg_q[None], bits[None], jnp.zeros((6, rows), jnp.int32)], axis=0
    )
    key_info = jnp.where(pads == 1, segs, -2)[:, None]
    tiles = seg_q.reshape(rows // QT, QT)
    low = jnp.sum((segs[None, :] < tiles[:, :1]).astype(jnp.int32), axis=1)
    high = jnp.sum((segs[None, :] <= tiles[:, -1:]).astype(jnp.int32), axis=1)
    starts = first + QT * jnp.arange(rows // QT, dtype=jnp.int32)
    bounds = jnp.stack([low // KT, (high + KT - 1) // KT, starts, starts], axis=1)
    return bounds, row_info, key_info


TAIL_STEP = 0.47
TAIL = (0.266306628, 0.248031891, 0.336199252, -0.126105651, 0.607561554, -0.420410983, 0.0884173167)


def gelu_and_slope(pre):
    bell = jnp.exp(-0.5 * pre * pre)
    t = 1.0 / (1.0 + (TAIL_STEP * 0.5**0.5) * jnp.abs(pre))
    tail = TAIL[-1]
    for c in TAIL[-2::-1]:
        tail = tail * t + c
    tail = 0.5 * (tail * t) * bell
    cdf = jnp.where(pre < 0, tail, 1.0 - tail)
    return pre * cdf, cdf + pre * (bell * (2.0 * 3.141592653589793) ** -0.5)


def normalize(resid):
    center = resid - jnp.mean(resid, axis=1, keepdims=True)
    inverse = lax.rsqrt(jnp.mean(center * center, axis=1, keepdims=True) + EPSILON)
    return center * inverse, inverse


def norm_backward(grad_normed, normal_hat, inverse, gain):
    grad_hat = grad_normed * gain
    return inverse * (
        grad_hat
        - jnp.mean(grad_hat, axis=1, keepdims=True)
        - normal_hat * jnp.mean(grad_hat * normal_hat, axis=1, keepdims=True)
    )


def fetch_blocks(blocks_hbm, blocks_ref, sems):
    return [
        pltpu.make_async_copy(blocks_hbm.at[:, t], blocks_ref.at[:, t], sems.at[t])
        for t in range(blocks_ref.shape[1])
    ]


def begin_fetch(blocks_hbm, blocks_ref, sems):
    @pl.when(pl.program_id(0) == 0)
    def _():
        for move in fetch_blocks(blocks_hbm, blocks_ref, sems):
            move.start()


def end_fetch(blocks_hbm, blocks_ref, sems):
    @pl.when(pl.program_id(0) == 0)
    def _():
        for move in fetch_blocks(blocks_hbm, blocks_ref, sems):
            move.wait()


def unit_chunks(blocks_ref):
    dp, tp, own_rows, both = blocks_ref.shape
    units = both // 2
    for t in range(tp):
        w_in = lambda t=t: blocks_ref[:, t, :, :units].reshape(dp * own_rows, units)
        w_out = lambda t=t: blocks_ref[:, t, :, units:].reshape(dp * own_rows, units)
        yield t, slice(t * units, (t + 1) * units), w_in, w_out


def forth_kernel(
    x_ref, attn_ref, cot_ref, proj_0, proj_1, blocks_hbm, vec_ref,
    final_ref, resid_out, grad_out, norm_low, slope, ffn_grad, out_grad, sums, hidden, outer, blocks_ref, sems,
):
    begin_fetch(blocks_hbm, blocks_ref, sems)
    out_bias, last_bias, gain_1, shift_1, gain_2, shift_2 = (vec_ref[i : i + 1, :] for i in range(2, 8))

    @pl.when(pl.program_id(0) == 0)
    def _():
        sums[...] = jnp.zeros_like(sums)
        outer[...] = jnp.zeros_like(outer)

    resid = x_ref[...].astype(F32) + out_bias
    third = proj_0.shape[2]
    resid += nt(attn_ref[:, :third], proj_0[0]) + nt(attn_ref[:, third:], proj_1[0])
    resid_out[...] = resid
    hat, _ = normalize(resid)
    first_norm = hat * gain_1 + shift_1
    low = first_norm.astype(BF)
    norm_low[...] = low
    resid = first_norm + last_bias
    end_fetch(blocks_hbm, blocks_ref, sems)
    chunks = list(unit_chunks(blocks_ref))
    dp, tp, own_rows, both = blocks_ref.shape
    units, sub = both // 2, 256
    per = units // sub

    def before(c):
        first = c % per * sub
        left = blocks_ref[:, c // per, :, first : first + sub].reshape(dp * own_rows, sub)
        return nn(low, left) + vec_ref[8 + c // per : 9 + c // per, first : first + sub]

    pre = before(0)
    for c in range(tp * per):
        after = before(c + 1) if c + 1 < tp * per else None
        here = slice(c * sub, (c + 1) * sub)
        act, slope[:, here] = gelu_and_slope(pre)
        hidden[:, here] = act.astype(BF)
        pre = after
        done = c - 0
        if done >= 0 and done % per == per - 1:
            t, cols, _, w_out = chunks[done // per]
            resid += nt(hidden[:, cols], w_out())
    for c in range(tp * per - 0, tp * per):
        if c % per == per - 1:
            t, cols, _, w_out = chunks[c // per]
            resid += nt(hidden[:, cols], w_out())
    hat, inverse = normalize(resid)
    final_ref[...] = (hat * gain_2 + shift_2).astype(BF)
    cot = cot_ref[...].astype(F32)
    grad = norm_backward(cot, hat, inverse, gain_2)
    sums[6:7, :] += jnp.sum(cot * hat, axis=0, keepdims=True)
    sums[7:8, :] += jnp.sum(cot, axis=0, keepdims=True)
    sums[3:4, :] += jnp.sum(grad, axis=0, keepdims=True)
    grad_out[...] = grad
    low = grad.astype(BF)
    ffn_grad[...] = low
    turned = low.T
    for t, cols, _, _ in unit_chunks(blocks_ref):
        outer[t] += nn(turned, hidden[:, cols])

    @pl.when(pl.program_id(0) == pl.num_programs(0) - 1)
    def _():
        for t in range(out_grad.shape[1]):
            out_grad[:, t] = outer[t].reshape(out_grad.shape[0], out_grad.shape[2], out_grad.shape[3]).astype(BF)


def back_kernel(
    resid_ref, grad_ref, ffn_grad, slope, proj_0, proj_1, blocks_hbm, vec_ref, sums_ref,
    first_grad, attn_grad, unit_grad, proj_grad, sums, unit_sums, blocks_ref, sems,
):
    begin_fetch(blocks_hbm, blocks_ref, sems)
    @pl.when(pl.program_id(0) == 0)
    def _():
        sums[...] = sums_ref[...]
        unit_sums[...] = jnp.zeros_like(unit_sums)

    hat, inverse = normalize(resid_ref[...])
    low = ffn_grad[...]
    grad = grad_ref[...]
    end_fetch(blocks_hbm, blocks_ref, sems)
    for t, cols, w_in, w_out in unit_chunks(blocks_ref):
        act = (nn(low, w_out()) * slope[:, cols]).astype(BF)
        unit_grad[:, cols] = act
        unit_sums[0:1, cols] += jnp.sum(act.astype(F32), axis=0, keepdims=True)
        grad += nt(act, w_in())
    sums[4:5, :] += jnp.sum(grad * hat, axis=0, keepdims=True)
    sums[5:6, :] += jnp.sum(grad, axis=0, keepdims=True)
    grad = norm_backward(grad, hat, inverse, vec_ref[4:5, :])
    sums[2:3, :] += jnp.sum(grad, axis=0, keepdims=True)
    first_grad[...] = grad
    low = grad.astype(BF)
    proj_grad[...] = low
    third = proj_0.shape[2]
    attn_grad[:, :third] = nn(low, proj_0[0]).astype(BF)
    attn_grad[:, third:] = nn(low, proj_1[0]).astype(BF)


def middle(layer_in, attn, output_grad, weights, blocks, vectors):
    rows, width = layer_in.shape
    tp, own_units = blocks.shape[1], blocks.shape[3] // 2
    units = tp * own_units
    once = dict(pipeline_mode=pl.Buffered(1))
    whole = lambda a: pl.BlockSpec(a.shape, lambda i: (0,) * len(a.shape), **once)
    fixed = lambda w: pl.BlockSpec((8, w), lambda i: (0, 0))
    shape = lambda w, t: jax.ShapeDtypeStruct((rows, w), t)
    sums_of = lambda w: jax.ShapeDtypeStruct((8, w), F32)
    out_grad = jax.ShapeDtypeStruct(blocks.shape[:3] + (own_units,), BF)
    third = width // 2
    proj = [pl.BlockSpec((1, width, third), lambda i, y=y: (0, 0, 4 * y + 3), **once) for y in range(2)]
    held = [pltpu.VMEM(blocks.shape, BF), pltpu.SemaphoreType.DMA((tp,))]
    tile = lambda w: pl.BlockSpec((ROWS, w), lambda i: (i, 0))
    layer_out, resid, grad_second, norm_low, slope, ffn_grad, out_grad, sums = pl.pallas_call(
        forth_kernel,
        name="middle_forth",
        grid=(rows // ROWS,),
        in_specs=[tile(width)] * 3 + proj + [pl.BlockSpec(memory_space=pl.ANY), whole(vectors)],
        out_specs=[tile(width)] * 4 + [tile(units), tile(width), whole(out_grad), fixed(width)],
        out_shape=[
            shape(width, BF), shape(width, F32), shape(width, F32), shape(width, BF), shape(units, F32),
            shape(width, BF), out_grad, sums_of(width),
        ],
        scratch_shapes=[pltpu.VMEM((ROWS, units), BF), pltpu.VMEM((tp, width, own_units), F32)] + held,
        compiler_params=params_of(),
    )(layer_in, attn, output_grad, weights, weights, blocks, vectors)
    tile = lambda w: pl.BlockSpec((BACK_ROWS, w), lambda i: (i, 0))
    first_grad, attn_grad, unit_grad, proj_grad, sums, unit_sums = pl.pallas_call(
        back_kernel,
        name="middle_back",
        grid=(rows // BACK_ROWS,),
        in_specs=[tile(width)] * 3 + [tile(units)] + proj + [pl.BlockSpec(memory_space=pl.ANY), whole(vectors), whole(sums)],
        out_specs=[tile(width)] * 2 + [tile(units), tile(width), fixed(width), fixed(units)],
        out_shape=[
            shape(width, F32), shape(width, BF), shape(units, BF), shape(width, BF), sums_of(width), sums_of(units),
        ],
        scratch_shapes=held,
        compiler_params=params_of(),
    )(resid, grad_second, ffn_grad, slope, weights, weights, blocks, vectors, sums)
    return layer_out, first_grad, attn_grad, norm_low, unit_grad, proj_grad, out_grad, sums, unit_sums


def finish_kernel(
    n, x_hbm, dq_hbm, dkv_hbm, w_hbm, first_hbm, low_hbm, unit_hbm, proj_hbm, attn_hbm, sums_ref, unit_sums,
    input_hbm, q_out, k_out, v_out, o_out, in_out, vec_out,
    rows_in, turned, unit, d_qkv, attn, far, w_all, tile_in, tile_out, grads, sib, from_b, from_a, from_low, from_high,
    result, vec_sent, vec_got,
    load, swap_s, swap_r, ss, sr, bs, br, as_, ar, zs, zr, es, er, vs, vr, tile_sem,
):
    w = places()
    dp, rank, core, y, z, x = (w[k] for k in ("dp", "rank", "core", "y", "z", "x"))
    rows, width = x_hbm.shape
    third = width // 2
    wide = unit.shape[1] // 2
    slab = result.shape[1] // 2
    up, down = {"dp": lax.rem(dp + 2, 2 * n), "tensor": rank}, {"dp": lax.rem(dp + 2 * n - 2, 2 * n), "tensor": rank}
    partners = [w["sibling"], w["second"], w["first"]] + line_jumps(dp, rank, z, n)
    barrier = pltpu.get_barrier_semaphore()
    for other in partners + [up, down]:
        pl.semaphore_signal(barrier, inc=1, device_id=other, device_id_type=MESH)

    def fetch(i, src, dst):
        return pltpu.make_async_copy(src, dst, load.at[i])

    fetch_low = fetch(0, low_hbm, rows_in.at[0])
    fetch_unit = fetch(1, unit_hbm, unit)
    fetch_x = fetch(2, x_hbm, rows_in.at[1])
    fetch_proj = fetch(3, proj_hbm, rows_in.at[2])
    fetch_attn = fetch(4, attn_hbm, attn)
    fetch_w = fetch(5, w_hbm.at[0], w_all)
    fetch_dq = [fetch(6 + h, dq_hbm.at[:, h * third : (h + 1) * third], d_qkv.at[:, 3 * h * third : (3 * h + 1) * third]) for h in range(2)]
    fetch_kv = [fetch(8 + h, dkv_hbm.at[core, :, 2 * h * third : 2 * (h + 1) * third], d_qkv.at[:, (3 * h + 1) * third : (3 * h + 3) * third]) for h in range(2)]
    for move in [fetch_low, fetch_unit, fetch_x, fetch_proj, fetch_attn] + fetch_dq + fetch_kv + [fetch_w]:
        move.start()
    pl.semaphore_wait(barrier, len(partners) + 2)

    def copy(src, dst, ssem, rsem, dev):
        return pltpu.make_async_remote_copy(src, dst, ssem, rsem, device_id=dev, device_id_type=MESH)

    swap = copy(dkv_hbm.at[1 - core], far, swap_s, swap_r, w["sibling"])
    swap.start()

    def turn_rows(i):
        for c in range(0, width, 128):
            turned[i, c : c + 128, :] = rows_in[i, :, c : c + 128].T

    places_of = [xd * 2 + yd for xd, yd in (
        (x, y), (w["xa"], w["ya"]), (w["xb"], w["yb"]), (w["xa"] + w["xb"] - x, w["ya"] + w["yb"] - y))]
    mine = grads.at[core]

    def keep(k, zd, yd, lane, value):
        for xd in range(2):
            for c in range(2):
                first = (xd * 2 + c) * slab
                grads[c, k, zd, xd * 2 + yd, :, lane : lane + value.shape[1]] = value[first : first + slab, :].astype(BF)

    def rows_of_line(i, zd):
        return turned[i, pl.ds(pl.multiple_of(zd * 4 * slab, 4 * slab), 4 * slab), :]

    def compute_inner(zd):
        left = rows_of_line(0, zd)
        for yd in range(2):
            for lane in range(0, wide, 768):
                keep(1, zd, yd, lane, nn(left, unit[:, yd * wide + lane : yd * wide + lane + 768]))

    def compute_others(zd):
        left = rows_of_line(1, zd)
        for yd in range(2):
            for i in range(3):
                at = (3 * yd + i) * third
                keep(0, zd, yd, i * third, nn(left, d_qkv[:, at : at + third]))
        left = rows_of_line(2, zd)
        for yd in range(2):
            keep(0, zd, yd, 3 * third, nn(left, attn[:, yd * third : (yd + 1) * third]))

    def to_sibling(k, zd):
        return copy(grads.at[1 - core, k, zd], sib.at[k, zd], ss.at[k, zd], sr.at[k, zd], w["sibling"])

    def over_b(k, far_side, zd):
        place = places_of[2 + far_side]
        return copy(mine.at[k, zd, place], from_b.at[k, far_side, zd], bs.at[k, far_side, zd], br.at[k, far_side, zd], w["second"])

    def over_a(k, zd):
        return copy(mine.at[k, zd, places_of[1]], from_a.at[k, zd], as_.at[k, zd], ar.at[k, zd], w["first"])

    def over_up(k, zd):
        return copy(mine.at[k, zd, places_of[0]], from_low.at[k, zd], zs.at[k, zd], zr.at[0, k, zd], up)

    def over_down(k, zd):
        return copy(mine.at[k, zd, places_of[0]], from_high.at[k, zd], zs.at[k, zd], zr.at[1, k, zd], down)

    def put(q, k, zd, more):
        place = places_of[q]
        total = grads[core, k, zd, place].astype(F32) + sib[k, zd, place].astype(F32)
        for term in more:
            total = total + term[...].astype(F32)
        grads[core, k, zd, place] = total.astype(BF)

    def stage_b(k, zd):
        to_sibling(k, zd).wait_recv()
        for far_side in (1, 0):
            put(2 + far_side, k, zd, ())
            over_b(k, far_side, zd).start()

    def stage_a(k, zd):
        over_b(k, 1, zd).wait_recv()
        put(1, k, zd, (from_b.at[k, 1, zd],))
        over_a(k, zd).start()

    def stage_line(k, zd):
        over_b(k, 0, zd).wait_recv()
        over_a(k, zd).wait_recv()
        put(0, k, zd, (from_b.at[k, 0, zd], from_a.at[k, zd]))

        @pl.when((zd > z) & (z == 0))
        def _():
            over_up(k, zd).start()

        @pl.when((zd < z) & (z == n - 1))
        def _():
            over_down(k, zd).start()

    def grow(k, zd, term):
        place = places_of[0]
        grads[core, k, zd, place] = (grads[core, k, zd, place].astype(F32) + term[...].astype(F32)).astype(BF)

    def stage_hop(k, zd):
        @pl.when((zd > z) & (z > 0))
        def _():
            over_up(k, zd).wait_recv()
            grow(k, zd, from_low.at[k, zd])
            over_up(k, zd).start()

        @pl.when((zd < z) & (z < n - 1))
        def _():
            over_down(k, zd).wait_recv()
            grow(k, zd, from_high.at[k, zd])
            over_down(k, zd).start()

    def turn(i):
        below, above = z, n - 1 - z
        near = jnp.minimum(below, above)
        only = jnp.maximum(below, above) - near
        side = jnp.where(above >= below, 1, -1)
        distance = jnp.where(i < only, only + near - i, near - (i - only) // 2)
        sign = jnp.where(i < only, side, jnp.where(lax.rem(i - only, 2) == 0, side, -side))
        return jnp.where(i == n - 1, z, z + sign * distance)

    def item(j):
        return 1 - j // n, turn(lax.rem(j, n))

    def small_send(step):
        return copy(vec_sent.at[step], vec_got.at[step], vs.at[step], vr.at[step], partners[step])

    def input_tile(t):
        at = pl.ds(pl.multiple_of(t * ROWS, ROWS), ROWS)
        return (pltpu.make_async_copy(first_hbm.at[at, :], tile_in.at[lax.rem(t, 2)], tile_sem.at[0, lax.rem(t, 2)]),
                pltpu.make_async_copy(tile_out.at[lax.rem(t, 2)], input_hbm.at[at, :], tile_sem.at[1, lax.rem(t, 2)]), at)

    def input_grad(t):
        into, out, at = input_tile(t)
        into.start()
        total = nt(d_qkv[at, : 3 * third], w_all[:, : 3 * third])
        total += nt(d_qkv[at, 3 * third :], w_all[:, wide : wide + 3 * third])
        into.wait()
        tile_out[lax.rem(t, 2)] = tile_in[lax.rem(t, 2)] + total
        out.start()

    tiles = rows // ROWS
    last_item = 2 * n

    fetch_low.wait()
    turn_rows(0)
    fetch_unit.wait()

    @pl.loop(0, last_item + 4)
    def _(j):
        @pl.when((j >= 1) & (j < last_item + 1))
        def _():
            stage_b(*item(j - 1))

        @pl.when(j < n)
        def _():
            k, zd = item(j)
            compute_inner(zd)
            to_sibling(1, zd).start()

        @pl.when(j == n - 1)
        def _():
            fetch_x.wait()
            fetch_proj.wait()
            fetch_attn.wait()
            turn_rows(1)
            turn_rows(2)
            for move in fetch_dq + fetch_kv:
                move.wait()
            swap.wait_recv()
            for h in range(2):
                at = slice((3 * h + 1) * third, (3 * h + 3) * third)
                d_qkv[:, at] = (d_qkv[:, at].astype(F32) + far[:, 2 * h * third : 2 * (h + 1) * third].astype(F32)).astype(BF)
            vec_sent[0] = jnp.zeros_like(vec_sent[0])
            vec_sent[0, 2:8, :] = sums_ref[2:8, :]
            for h in range(2):
                for row, i in ((0, 0), (1, 2)):
                    cols = d_qkv[:, (3 * h + i) * third : (3 * h + i + 1) * third].astype(F32)
                    vec_sent[0, row : row + 1, h * third : (h + 1) * third] = jnp.sum(cols, axis=0, keepdims=True)
            for u in range(unit_sums.shape[1] // width):
                vec_sent[0, 8 + u : 9 + u, :] = unit_sums[0:1, u * width : (u + 1) * width]
            small_send(0).start()
            fetch_w.wait()

        @pl.when((j >= n) & (j < last_item))
        def _():
            k, zd = item(j)
            compute_others(zd)
            to_sibling(0, zd).start()

        @pl.when((j >= 2) & (j < last_item + 2))
        def _():
            stage_a(*item(j - 2))

        @pl.when((j >= 3) & (j < last_item + 3))
        def _():
            stage_line(*item(j - 3))

        @pl.when(j >= 4)
        def _():
            stage_hop(*item(j - 4))

        for step in range(len(partners)):
            @pl.when(j == n + step)
            def _(step=step):
                small_send(step).wait_recv()
                vec_sent[step + 1] = vec_sent[step] + vec_got[step]
                if step + 1 < len(partners):
                    small_send(step + 1).start()

        @pl.when((j >= last_item - tiles) & (j < last_item))
        def _():
            t = j - (last_item - tiles)

            @pl.when(t >= 2)
            def _():
                input_tile(t - 2)[1].wait()
            input_grad(t)

    vec_out[...] = vec_sent[len(partners)]
    own = pl.ds(pl.multiple_of(core * slab, slab), slab)
    theirs = pl.ds(pl.multiple_of((1 - core) * slab, slab), slab)
    for k in (1, 0):
        result[k, own, :] = grads[core, k, z, places_of[0]].astype(F32)

        @pl.when(z > 0)
        def _():
            over_up(k, z).wait_recv()
            result[k, own, :] += from_low[k, z].astype(F32)

        @pl.when(z < n - 1)
        def _():
            over_down(k, z).wait_recv()
            result[k, own, :] += from_high[k, z].astype(F32)

        copy(result.at[k, own, :], result.at[k, own, :], es.at[k], er.at[k], w["sibling"]).start()
    for t in range(max(tiles - 2, 0), tiles):
        input_tile(t)[1].wait()
    swap.wait_send()
    for step in range(len(partners)):
        small_send(step).wait_send()

    @pl.loop(0, n)
    def _(zd):
        for k in range(2):
            to_sibling(k, zd).wait_send()
            over_b(k, 0, zd).wait_send()
            over_b(k, 1, zd).wait_send()
            over_a(k, zd).wait_send()

            @pl.when(zd > z)
            def _():
                over_up(k, zd).wait_send()

            @pl.when(zd < z)
            def _():
                over_down(k, zd).wait_send()
    for k in (1, 0):
        copy(result.at[k, theirs, :], result.at[k, theirs, :], es.at[k], er.at[k], w["sibling"]).wait()

    def chosen(k, lane, w_own):
        both = result[k, :, lane : lane + 2 * w_own]
        return jnp.where(core == 0, both[:, :w_own], both[:, w_own:])

    for i, out in enumerate((q_out, k_out, v_out, o_out)):
        out[...] = chosen(0, i * third, third // 2)
    in_out[...] = chosen(1, 0, wide // 2)


def finish(layer_in, dq, dkv, weights, grad_first, norm_low, unit_grad, proj_grad, attn, sums, unit_sums):
    rows, width = layer_in.shape
    units = unit_grad.shape[1]
    dp, tp = lax.axis_size("dp"), lax.axis_size("tensor")
    n = dp // 2
    block = width // dp
    slab, wide, third = block // 2, units // 2, width // 2
    steps = 3 + (n - 1).bit_length()
    dma = pltpu.SemaphoreType.DMA
    slabs = lambda *lead: pltpu.VMEM(lead + (slab, wide), BF)
    anywhere, inside = pl.BlockSpec(memory_space=pl.ANY), pl.BlockSpec(memory_space=pltpu.VMEM)
    result = lambda *shape: jax.ShapeDtypeStruct(shape, F32)
    return pl.pallas_call(
        partial(finish_kernel, n),
        name="finish",
        in_specs=[anywhere] * 9 + [inside] * 2,
        out_specs=[anywhere] + [inside] * 6,
        out_shape=[result(rows, width)] + [result(block, third // 2)] * 4 + [result(block, wide // 2), result(16, width)],
        scratch_shapes=[
            pltpu.VMEM((3, rows, width), BF),
            pltpu.VMEM((3, width, rows), BF),
            pltpu.VMEM((rows, units), BF),
            pltpu.VMEM((rows, 3 * width), BF),
            pltpu.VMEM((rows, width), BF),
            pltpu.VMEM((rows, 2 * width), BF),
            pltpu.VMEM((width, units), BF),
            pltpu.VMEM((2, ROWS, width), F32),
            pltpu.VMEM((2, ROWS, width), F32),
            slabs(2, 2, n, 4),
            slabs(2, n, 4),
            slabs(2, 2, n),
            slabs(2, n),
            slabs(2, n),
            slabs(2, n),
            pltpu.VMEM((2, block, wide), F32),
            pltpu.VMEM((steps + 1, 16, width), F32),
            pltpu.VMEM((steps, 16, width), F32),
            dma((10,)), dma(()), dma(()),
            dma((2, n)), dma((2, n)), dma((2, 2, n)), dma((2, 2, n)), dma((2, n)), dma((2, n)),
            dma((2, n)), dma((2, 2, n)), dma((2,)), dma((2,)), dma((steps,)), dma((steps,)), dma((2, 2)),
        ],
        compiler_params=pltpu.CompilerParams(
            collective_id=4, has_side_effects=True, vmem_limit_bytes=60 * 2**20
        ),
    )(layer_in, dq, dkv.reshape(2, rows, 2 * width), weights, grad_first, norm_low, unit_grad, proj_grad, attn, sums, unit_sums)


def finish_plainly(layer_in, dq, dkv, weights, grad_first, norm_low, unit_grad, proj_grad, attn, sums, unit_sums):
    rows, width = layer_in.shape
    units = unit_grad.shape[1]
    dp, tp = lax.axis_size("dp"), lax.axis_size("tensor")
    third, block, pairs = width // 2, width // dp, tp // 2
    half = lax.rem(lax.axis_index("tensor"), 2)
    both = dkv.reshape(2, rows, 2 * width)
    far = swap_pair(both)
    near = lax.dynamic_index_in_dim(both, half, 0, False)
    own = (near.astype(F32) + far.astype(F32)).astype(BF)
    d_qkv = jnp.concatenate([dq[:, :third], own[:, :width], dq[:, third:], own[:, width:]], axis=1)
    wqkv = weights[0].reshape(width, 2, 4 * third)[:, :, : 3 * third].reshape(width, 3 * width)
    input_grad = grad_first + nt(d_qkv, wqkv)
    grads = [g.astype(BF) for g in (tn(layer_in, d_qkv), tn(proj_grad, attn), tn(norm_low, unit_grad))]
    joined = jnp.concatenate([g.reshape(width, pairs, -1) for g in grads[:2]], axis=2)
    every = jnp.stack([joined.reshape(width, units), grads[2]])
    every = every.reshape(2, dp, block, pairs, 1, units // pairs).transpose(1, 3, 4, 0, 2, 5)
    every = jnp.broadcast_to(every, (dp, pairs, 2, 2, block, units // pairs))
    total = lax.psum_scatter(
        every.reshape(dp * tp, 2, block, units // pairs), ("dp", "tensor"), scatter_dimension=0, tiled=False
    ).astype(F32)
    d_bias = jnp.sum(d_qkv.astype(F32), axis=0).reshape(2, 3, third)
    vec = jnp.concatenate(
        [d_bias[:, 0].reshape(1, width), d_bias[:, 2].reshape(1, width), sums[2:],
         unit_sums[0].reshape(-1, width), jnp.zeros((8 - units // width, width), F32)], axis=0,
    )
    vec = lax.psum(vec, ("dp", "tensor"))

    def chosen(k, lane, w_own):
        return lax.dynamic_slice_in_dim(total[k], lane + half * w_own, w_own, axis=1)

    return (input_grad,) + tuple(chosen(0, i * third, third // 2) for i in range(4)) + (
        chosen(1, 0, units // tp), vec)


def on_device(
    layer_in, query_weight, key_weight, value_weight, output_weight, inner_weight, outer_weight,
    query_bias, value_bias, output_bias, inner_bias, outer_bias, first_gain, first_shift,
    second_gain, second_shift, segment_ids, pad_mask, random_blocks, global_blocks, output_grad,
):
    rows, width = layer_in.shape
    dp, tp = lax.axis_size("dp"), lax.axis_size("tensor")
    own_rows, own_cols = query_weight.shape
    own_units = inner_weight.shape[1]
    third = width // 2
    half = lax.rem(lax.axis_index("tensor"), 2)

    units_own = jnp.concatenate([inner_weight, outer_weight.T], axis=1)
    blocks = lax.all_gather(units_own, ("dp", "tensor"), axis=0, tiled=False)
    blocks = blocks.reshape(dp, tp, own_rows, 2 * own_units)
    mine = (query_weight, key_weight, value_weight, output_weight.T)
    place = lax.axis_index("dp") * tp + lax.axis_index("tensor")
    one, own_bias = query_bias.shape[0], inner_bias.shape[0]
    small = jnp.stack([query_bias, value_bias, output_bias, outer_bias, first_gain, first_shift,
                       second_gain, second_shift])
    eight = lax.dynamic_update_slice(jnp.zeros((8, width), F32), small, (0, place * one))
    unit = lax.dynamic_update_slice(jnp.zeros((8 * width,), F32), inner_bias, (place * own_bias,))
    vec = jnp.concatenate([eight, unit.reshape(8, width)], axis=0)
    begin = start if in_tiles(own_rows) else start_plainly
    weights, qkv, other, vectors = begin(mine, vec, layer_in)

    bounds, row_info, key_info = attention_plan(
        segment_ids, pad_mask, random_blocks, global_blocks, rows
    )
    attn, logs = attend_forward(bounds, qkv, other, row_info, key_info)
    (layer_out, grad_first, grad_attn, norm_low, unit_grad, proj_grad, out_grad, sums, unit_sums) = middle(
        layer_in, attn, output_grad, weights, blocks, vectors
    )
    d_outer = lax.psum_scatter(
        out_grad.reshape((dp * tp,) + out_grad.shape[2:]), ("dp", "tensor"), scatter_dimension=0, tiled=False
    )
    dq, dkv = attend_backward(bounds, qkv, other, row_info, key_info, attn, logs, grad_attn)
    end = finish if in_tiles(own_rows) else finish_plainly
    input_grad, d_q, d_k, d_v, d_o, d_inner, vec = end(
        layer_in, dq, dkv, weights, grad_first, norm_low, unit_grad, proj_grad, attn, sums, unit_sums
    )
    pieces = lax.dynamic_slice_in_dim(vec[:8], place * one, one, axis=1)
    (r_bq, r_bv, r_bo, r_bout, r_g1, r_s1, r_g2, r_s2) = (pieces[i] for i in range(8))
    d_bin = lax.dynamic_slice_in_dim(vec[8:].reshape(-1), place * own_bias, own_bias)
    return (
        layer_out, input_grad, d_q, d_k, d_v, d_o.T, d_inner, d_outer.astype(F32).T,
        r_bq, r_bv, r_bo, d_bin, r_bout, r_g1, r_s1, r_g2, r_s2,
    )


def solution(mesh):
    tokens = P(("dp", "tensor"), None)
    vector = P(("dp", "tensor"))
    cols, turned = P("dp", "tensor"), P("tensor", "dp")
    return jax.shard_map(
        on_device,
        mesh=mesh,
        in_specs=(tokens, cols, cols, cols, turned, cols, turned)
        + (vector,) * 9
        + (P("dp"), P("dp"), P("dp", None, None), P("dp", None, None), tokens),
        out_specs=(tokens, tokens, cols, cols, cols, turned, cols, turned) + (vector,) * 9,
        check_vma=False,
    )
```
